128 devices in a mesh: cube: 4 (over y), grid: 32 (over z, x, core).
Axes of the slice: x: 4, y: 4, z: 4, core: 2. Of those that a mesh axis runs over, the one named last changes fastest.
Arguments:
- parent_front: float32 [8192, 4, 4096], P('grid', 'cube'), as said below
- child_block: bfloat16 [4, 6144, 6144], P('cube', 'grid'), as said below
- child_panel: bfloat16 [4, 6144, 512], P('cube', 'grid'), may hold values from -0.15625 to 0.15625
- row_map: int32 [4, 6144], replicated, may hold values from 0 to 8191, as said below
Outputs:
- schur_block: float32 [8192, 4, 4096], P('grid', 'cube')
- panel_factor: float32 [8192, 4, 256], P('grid', 'cube')
The draws below stay inside these ranges and needn't reach their ends.
Inputs may be any that keep to these rules, and one draw needn't show every extreme that they name: Each row of row_map lists 6144 distinct parent rows. Cut the 6144 entries of a row into 192 entries for each grid index, and the parent rows into blocks of 256: from one grid index at most 12 entries fall into one block, a number reached in every draw. `parent_front`: symmetric with a dominant positive diagonal. `child_block`: symmetric with a dominant positive diagonal.
All inputs are finite; a program needn't handle non-finite values.
Results may differ from the reference program's by a relative error of at most 0.0015.
Values may be sent and summed in bfloat16 or wider, within the bound.
No kernel may reach another device: no remote copies, remote signals or barrier semaphores. Data moves between devices by JAX's collectives and lax.ppermute only.
A program may use at most 128 MiB of HBM per device.

```python
import jax
import jax.numpy as jnp
from jax import lax

PF = 8192
CB = 6144
PW = 512
N_GRID = 32


def symmetric_matrix(key, order, spread, diag_low, diag_high):
    first_key, second_key = jax.random.split(key)
    entries = jax.random.normal(first_key, (order, order), jnp.float32)
    entries = (entries + entries.T) * (spread * 0.7071)
    diagonal = jax.random.uniform(second_key, (order,), jnp.float32, diag_low, diag_high)
    return entries + jnp.diag(diagonal)


def draw_parent_front(key, part):
    fronts = [symmetric_matrix(jax.random.fold_in(key, 11 + parent_index), PF, 0.02, 3.0, 6.0) for parent_index in range(2)]
    stacked = jnp.stack(fronts)
    return stacked.reshape(2, PF, PF // 2, 2).transpose(1, 0, 3, 2).reshape(PF, 4, PF // 2)


def draw_child_block(key, part):
    blocks = [symmetric_matrix(jax.random.fold_in(key, 21 + child_index), CB, 0.01, 1.0, 2.0) for child_index in range(4)]
    return jnp.stack(blocks).astype(jnp.bfloat16)


def child_map(key):
    owners = N_GRID
    source_rows = CB // owners
    owned_rows = PF // owners
    mean_count = source_rows // owners
    first_key, second_key, third_key = jax.random.split(key, 3)
    order_draw = jax.random.permutation(first_key, owners).astype(jnp.int32)
    levels = jnp.where(order_draw < owners // 4, 2 * mean_count, jnp.where(order_draw < 3 * owners // 4, mean_count, 0)).astype(jnp.int32)
    source_ids = jnp.arange(owners, dtype=jnp.int32)[:, None]
    owner_ids = jnp.arange(owners, dtype=jnp.int32)[None, :]
    counts = levels[(owner_ids - source_ids) % owners]
    segment_end = jnp.cumsum(counts, axis=1)
    segment_start = segment_end - counts
    base_offset = jnp.cumsum(counts, axis=0) - counts
    positions = jnp.arange(source_rows, dtype=jnp.int32)
    owner_of = jnp.sum((positions[None, :, None] >= segment_end[:, None, :]).astype(jnp.int32), axis=2)
    start_sel = jnp.take_along_axis(segment_start, owner_of, axis=1)
    base_sel = jnp.take_along_axis(base_offset, owner_of, axis=1)
    offsets = base_sel + positions[None, :] - start_sel
    slot_tables = jax.vmap(lambda sub_key: jax.random.permutation(sub_key, owned_rows))(jax.random.split(second_key, owners)).astype(jnp.int32)
    slots = slot_tables[owner_of, offsets]
    parent_rows = owner_of * owned_rows + slots
    row_orders = jax.vmap(lambda sub_key: jax.random.permutation(sub_key, source_rows))(jax.random.split(third_key, owners)).astype(jnp.int32)
    child_rows = source_ids * source_rows + row_orders
    return jnp.zeros((CB,), jnp.int32).at[child_rows.reshape(-1)].set(parent_rows.reshape(-1).astype(jnp.int32))


def draw_row_map(key, part):
    return jnp.stack([child_map(jax.random.fold_in(key, 31 + child_index)) for child_index in range(4)])


def steps_of(stream_key, dims, pieces, least, top_value):
    gain, own = 1.0, jax.random.fold_in(stream_key, 6)
    for position, shards_of in pieces:
        draws = jnp.exp(jax.random.uniform(jax.random.fold_in(own, position), (shards_of,), jnp.float32, least / len(pieces), top_value / len(pieces)))
        gain = gain * jnp.repeat(draws, dims[position] // shards_of).reshape([-1 if axis == position else 1 for axis in range(len(dims))])
    return gain


def bell_draw(rng, dims, scale, reach, cuts=(), kind=jnp.bfloat16):
    values = scale * jax.random.normal(rng, dims, jnp.float32)
    if cuts:
        values = values * steps_of(rng, dims, cuts, -0.22, 0.18)
    return jnp.clip(values, -reach, reach).astype(kind)


def setup_inputs(seed: int = 0) -> dict:
    streams_of = jax.random.split(jax.random.key(seed), 5)
    return {
        "parent_front": draw_parent_front(jax.random.fold_in(streams_of[4], 71), 0),
        "child_block": draw_child_block(jax.random.fold_in(streams_of[4], 71), 0),
        "child_panel": bell_draw(streams_of[2], (4, CB, PW), (PW * 25 // 9) ** -0.5, 0.15625, ((0, 4), (1, 32))),
        "row_map": draw_row_map(jax.random.fold_in(streams_of[4], 71), 0),
    }


def contribution(block_data, panel_data):
    product = jnp.dot(panel_data.astype(jnp.float32), panel_data.T.astype(jnp.float32), preferred_element_type=jnp.float32)
    return (block_data.astype(jnp.float32) - product).astype(jnp.bfloat16)

def reference(parent_front, child_block, child_panel, row_map):
    schur_parts = []
    panel_parts = []
    for parent_index in range(2):
        front_matrix = jnp.stack([parent_front[:, 2 * parent_index, :], parent_front[:, 2 * parent_index + 1, :]], axis=2).reshape(PF, PF)
        for child_index in (2 * parent_index, 2 * parent_index + 1):
            update = contribution(child_block[child_index], child_panel[child_index]).astype(jnp.float32)
            indices = row_map[child_index]
            front_matrix = front_matrix.at[indices[:, None], indices[None, :]].add(update)
        lower_factor = jnp.linalg.cholesky(front_matrix[:PW, :PW])
        factor = lax.linalg.triangular_solve(lower_factor, front_matrix[:, :PW], left_side=False, lower=True, transpose_a=True)
        outer_term = jnp.dot(factor.astype(jnp.float32), factor.T.astype(jnp.float32), precision=lax.Precision.HIGHEST, preferred_element_type=jnp.float32)
        schur_matrix = front_matrix - outer_term
        schur_parts.append(schur_matrix.reshape(PF, PF // 2, 2).transpose(0, 2, 1))
        panel_parts.append(factor.reshape(PF, PW // 2, 2).transpose(0, 2, 1))
    return (jnp.concatenate(schur_parts, axis=1), jnp.concatenate(panel_parts, axis=1))
```

```python
import functools

import jax
import jax.numpy as jnp
from jax import lax
from jax.experimental import pallas as pl
from jax.experimental.pallas import tpu as pltpu
from jax.sharding import PartitionSpec as P

PW = 512
BF = jnp.bfloat16
F32 = jnp.float32
NN = (((1,), (0,)), ((), ()))
NT = (((1,), (1,)), ((), ()))
VMEM_LIMIT = 60 << 20


def dot(a, b, dims=NN, precision=None):
    return lax.dot_general(a, b, dims, precision=precision, preferred_element_type=F32)


def hot(rows, row_vector):
    n = row_vector.shape[-1]
    rows_iota = lax.broadcasted_iota(jnp.int32, (rows, n), 0)
    return jnp.where(rows_iota == row_vector, 1.0, 0.0).astype(BF)


def eye(n, dtype=F32):
    r = lax.broadcasted_iota(jnp.int32, (n, n), 0)
    c = lax.broadcasted_iota(jnp.int32, (n, n), 1)
    return jnp.where(r == c, 1.0, 0.0).astype(dtype)


def call(kernel, out_shape, scratch=(), **kw):
    return pl.pallas_call(
        kernel,
        out_shape=out_shape,
        scratch_shapes=list(scratch),
        compiler_params=pltpu.CompilerParams(vmem_limit_bytes=VMEM_LIMIT),
        **kw,
    )


def source_kernel(owners, slots, owned, block_ref, slot_ref, target_ref, out_ref, y_ref):
    width = block_ref.shape[0]
    total = owners * slots

    def first(pair, carry):
        pick = hot(2 * total, slot_ref[pl.ds(pair, 1), :])
        cols = block_ref[:, pl.ds(pl.multiple_of(pair * 2 * width, 128), 2 * width)]
        y = dot(pick, cols, NT).astype(BF).reshape(2, owners, slots, width)
        base = pl.multiple_of(pair * 2 * slots, 16)
        y_ref[:, pl.ds(base, slots), :] = y[0]
        y_ref[:, pl.ds(base + slots, slots), :] = y[1]
        return carry

    lax.fori_loop(0, owners // 2, first, 0, unroll=2)
    unit = eye(width, BF)

    def second(owner, carry):
        pick = hot(owned, target_ref[pl.ds(owner, 1), :])
        turned = dot(pick, y_ref[owner]).astype(BF)
        out_ref[owner] = dot(unit, turned, NT).astype(BF)
        return carry

    lax.fori_loop(0, owners, second, 0, unroll=2)


def owner_kernel(owners, slots, owned, recv_ref, panel_ref, local_ref, slot_ref, target_ref, own_ref, other_ref, q_ref, y_ref):
    total = owners * slots
    q_ref[...] = jnp.zeros_like(q_ref)

    def gather(s, carry):
        q_ref[...] += dot(hot(owned, local_ref[pl.ds(s, 1), :]), panel_ref[s])
        return carry

    lax.fori_loop(0, owners, gather, 0, unroll=2)
    q = q_ref[...].astype(BF)

    def first(s, carry):
        product = dot(panel_ref[s], q, NT)
        contrib = (recv_ref[s].astype(F32) - product).astype(BF)
        y = dot(hot(total, slot_ref[pl.ds(s, 1), :]), contrib).astype(BF)
        y_ref[:, pl.ds(pl.multiple_of(s * slots, 16), slots), :] = y.reshape(owners, slots, owned)
        return carry

    lax.fori_loop(0, owners, first, 0, unroll=2)
    half = owned // 2

    def second(owner, carry):
        z = dot(hot(owned, target_ref[pl.ds(owner, 1), :]), y_ref[owner]).astype(BF)
        own_ref[owner] = z[:half]
        other_ref[owner] = z[half:]
        return carry

    lax.fori_loop(0, owners, second, 0, unroll=2)


def split(x):
    hi = x.astype(BF)
    return hi, (x - hi.astype(F32)).astype(BF)


def dot3(a, b, dims=NN):
    return dot(a[0], b[0], dims) + (dot(a[0], b[1], dims) + dot(a[1], b[0], dims))


def natural(position, parity, half):
    return jnp.where(position < half, 2 * position + parity, 2 * (position - half) + 1 - parity)


def inverse_kernel(parity_ref, a_ref, w_ref, s_ref, t_ref):
    n = a_ref.shape[0]
    half = n // 2
    parity = parity_ref[0]
    row_at = lax.broadcasted_iota(jnp.int32, (n, n), 0)
    col_at = lax.broadcasted_iota(jnp.int32, (n, n), 1)
    row_nat = natural(row_at, parity, half)
    col_nat = natural(col_at, parity, half)
    on = row_at == col_at
    phi = jnp.where(on, 0.5, jnp.where(row_nat > col_nat, 1.0, 0.0))
    unit = jnp.where(on, 1.0, 0.0)
    a = a_ref[...]
    diagonal = jnp.where(on, a, 0.0)
    scale_row = lax.rsqrt(jnp.sum(diagonal, axis=0, keepdims=True))
    scale_col = lax.rsqrt(jnp.sum(diagonal, axis=1, keepdims=True))
    scaled = a * scale_row * scale_col
    s_ref[...] = scaled
    w_ref[...] = unit - phi * (scaled - unit)
    s_parts = split(scaled)

    def step(state):
        count, _ = state
        w = w_ref[...]
        w_parts = split(w)
        m_parts = split(dot3(w_parts, s_parts))
        e = dot3(m_parts, w_parts, NT) - unit
        w_ref[...] = w - dot3(split(phi * e), w_parts)
        return count + 1, jnp.sum(e * e)

    def more(state):
        count, size = state
        return jnp.logical_and(count < 16, jnp.logical_not(size < 1e-6))

    _, size = lax.while_loop(more, step, (jnp.int32(0), jnp.float32(1.0)))

    @pl.when(jnp.logical_not(size < 1e-6))
    def _():
        lane = lax.broadcasted_iota(jnp.int32, (1, n), 1)
        lane_nat = natural(lane, parity, half)

        def place(j):
            return jnp.where((j & 1) == parity, j >> 1, half + (j >> 1))

        def column(j, carry):
            p = place(j)
            row = jnp.where(lane_nat >= j, s_ref[pl.ds(p, 1), :], 0.0)
            pivot = jnp.sum(jnp.where(lane == p, row, 0.0))
            row = row * lax.rsqrt(jnp.full((1, n), pivot))
            t_ref[pl.ds(p, 1), :] = row
            col = jnp.sum(jnp.where(on, row, 0.0), axis=1, keepdims=True)
            s_ref[...] = s_ref[...] - col * row
            return carry

        lax.fori_loop(0, n, column, 0)
        w_ref[...] = jnp.zeros_like(w_ref)

        def solve(j, carry):
            p = place(j)
            col = jnp.sum(jnp.where(col_at == p, t_ref[...], 0.0), axis=1, keepdims=True)
            known = jnp.sum(col * w_ref[...], axis=0, keepdims=True)
            pivot = jnp.sum(jnp.where(lane == p, t_ref[pl.ds(p, 1), :], 0.0))
            w_ref[pl.ds(p, 1), :] = (jnp.where(lane == p, 1.0, 0.0) - known) / pivot
            return carry

        lax.fori_loop(0, n, solve, 0)

    w_ref[...] = w_ref[...] * scale_row


def final_kernel(parent_ref, cols_ref, own_ref, recv_ref, w_ref, rows_ref, pivot_ref, schur_ref, panel_ref):
    owned = rows_ref.shape[0]
    strips = parent_ref.shape[0] // owned
    high = lax.Precision.HIGHEST
    factor = dot(rows_ref[...], w_ref[...], NT, high)
    panel_ref[...] = factor[:, : panel_ref.shape[1]]
    g = dot(factor, w_ref[...], NN, high)
    g_hi, g_lo = split(g)
    unit = eye(owned, BF)
    for chunk in range(strips // 2):
        at = pl.ds(chunk * 256, 256)
        if chunk == 0:
            update = dot(g, pivot_ref[...], NT, high)
        else:
            update = dot(g_hi, cols_ref[at, :], NT) + dot(g_lo, cols_ref[at, :], NT)
        placed = dot(unit, own_ref[at, :], NT) + dot(unit, recv_ref[at, :], NT)
        change = placed - update
        for side in range(2):
            lanes = pl.ds(2 * chunk + side, owned, stride=strips)
            schur_ref[lanes, :] = parent_ref[lanes, :] + change[:, side * 128 : side * 128 + 128]


def swap_halves(x, axis):
    a, b = jnp.split(x, 2, axis=axis)
    return jnp.concatenate([b, a], axis=axis)


def swapped(block):
    count = lax.axis_size("cube")
    return lax.ppermute(block, "cube", [(i, i ^ 1) for i in range(count)])


def shards(parent_front, child_block, child_panel, row_map):
    owners = lax.axis_size("grid")
    cube_pos = lax.axis_index("cube")
    grid_pos = lax.axis_index("grid")
    parity = cube_pos % 2
    width = child_block.shape[1]
    owned = parent_front.shape[0]
    half_cols = parent_front.shape[2]
    capacity = 2 * width // owners
    slots = -(-capacity // 16) * 16
    total = owners * slots
    half = owned // 2
    block = child_block[0]
    own_panel = child_panel[0]
    panel_all = lax.all_gather(own_panel, "grid")

    parent_pan = parent_front[:, 0, : PW // 2]
    hi = parent_pan.astype(BF)
    lo = (parent_pan - hi.astype(F32)).astype(BF)
    per = owned // owners
    scatter = jnp.concatenate([hi, lo], axis=1).reshape(owners, per, PW)
    pieces = lax.all_to_all(scatter, "grid", 0, 0, tiled=True)[:2].reshape(per, 2 * PW)

    row_of = lax.dynamic_index_in_dim(row_map, cube_pos, 0, keepdims=False).reshape(owners, width)
    owner_of = row_of // owned
    local_of = row_of % owned
    earlier = lax.iota(jnp.int32, width)[:, None] < lax.iota(jnp.int32, width)[None, :]
    same = (owner_of[:, :, None] == owner_of[:, None, :]) & earlier[None]
    rank_of = jnp.sum(same.astype(jnp.int32), axis=1)
    slot_of = owner_of * slots + rank_of
    hits = slot_of[:, :, None] == lax.iota(jnp.int32, total)[None, None, :]
    target = jnp.sum(jnp.where(hits, local_of[:, :, None] + 1, 0), axis=1) - 1
    target = target.reshape(owners, owners, slots).transpose(1, 0, 2)
    target_nat = target.reshape(owners, total)
    target_own = jnp.where(
        target_nat >= 0, ((target_nat & 1) ^ parity) * half + (target_nat >> 1), -1
    )
    pair_slot = (slot_of.reshape(owners // 2, 2, width) + jnp.array([0, total])[None, :, None]).reshape(
        owners // 2, 2 * width
    )
    my_slot = lax.dynamic_index_in_dim(slot_of, grid_pos, 0, keepdims=False)
    my_owner = lax.dynamic_index_in_dim(owner_of, grid_pos, 0, keepdims=False)
    my_rank = lax.dynamic_index_in_dim(rank_of, grid_pos, 0, keepdims=False)

    spread = call(
        functools.partial(source_kernel, owners, slots, owned),
        jax.ShapeDtypeStruct((owners, width, owned), BF),
        [pltpu.VMEM((owners, total, width), BF)],
    )(block, pair_slot, target_nat)

    pan_nat = lax.iota(jnp.int32, PW)
    pan_pos = ((pan_nat & 1) ^ parity) * (PW // 2) + (pan_nat >> 1)
    turn = (pan_pos[:, None] == lax.iota(jnp.int32, PW)[None, :]).astype(BF)
    block_pan = jnp.concatenate([spread[0], spread[1]], axis=1)
    block_pan = dot(block_pan, turn).astype(BF)
    pivot_slot = jnp.where(my_owner < 2, my_owner * capacity + my_rank, -1)
    pivot_pick = (lax.iota(jnp.int32, 2 * capacity)[:, None] == pivot_slot[None, :]).astype(BF)
    pivot_rows = dot(pivot_pick, jnp.concatenate([block_pan, own_panel], axis=1)).astype(BF)
    message = jnp.concatenate([pivot_rows, pieces], axis=0)
    message = lax.all_to_all(
        jnp.broadcast_to(message[None], (owners,) + message.shape), "grid", 0, 0, tiled=True
    )
    bulk = lax.all_to_all(spread, "grid", 0, 0, tiled=True)

    pivot_target = target[:2, :, :capacity]
    pivot_pos = jnp.where(
        pivot_target >= 0,
        ((pivot_target & 1) ^ parity) * (PW // 2)
        + lax.iota(jnp.int32, 2)[:, None, None] * half
        + (pivot_target >> 1),
        -1,
    )
    pivot_pos = pivot_pos.transpose(1, 0, 2).reshape(-1)
    pivot_hot = (lax.iota(jnp.int32, PW)[:, None] == pivot_pos[None, :]).astype(BF)
    child_part = dot(pivot_hot, message[:, : 2 * capacity].reshape(-1, 2 * PW)).astype(BF)
    panel_pan = child_part[:, PW:]
    pivot_child = (child_part[:, :PW].astype(F32) - dot(panel_pan, panel_pan, NT)).astype(BF)
    parts = message[:, 2 * capacity :].reshape(owners, 2, per, PW).transpose(1, 0, 2, 3).reshape(PW, PW)
    parts = dot(turn, parts, (((0,), (0,)), ((), ())))
    pivot_parent = parts[:, : PW // 2] + parts[:, PW // 2 :]
    pivot_mine = pivot_child.astype(F32) + jnp.pad(pivot_parent, ((0, 0), (0, PW // 2)))
    pivot_theirs = swapped(pivot_mine.astype(BF))

    contrib_pan = (block_pan.astype(F32) - dot(own_panel, panel_pan, NT)).astype(BF)
    pack = (lax.iota(jnp.int32, total)[:, None] == my_slot[None, :]).astype(BF)
    packed = dot(pack, contrib_pan).astype(BF).reshape(owners, slots, PW)
    packed = lax.all_to_all(packed, "grid", 0, 0, tiled=True).reshape(total, PW)
    my_target = lax.dynamic_index_in_dim(target_nat, grid_pos, 0, keepdims=False)
    unpack = (lax.iota(jnp.int32, owned)[:, None] == my_target[None, :]).astype(BF)
    rows_mine = dot(unpack, packed) + jnp.pad(parent_pan, ((0, 0), (0, PW // 2)))
    rows_theirs = swapped(rows_mine.astype(BF))
    rows = rows_mine + swap_halves(rows_theirs, 1).astype(F32)
    choose = (2 * lax.iota(jnp.int32, half)[:, None] + parity == lax.iota(jnp.int32, owned)[None, :]).astype(BF)
    parity_rows = dot(choose, rows.astype(BF)).astype(BF)
    front_cols = lax.all_gather(parity_rows, "grid", tiled=True)

    pivot = pivot_mine + swap_halves(swap_halves(pivot_theirs, 0), 1).astype(F32)
    pos_nat = natural(lax.iota(jnp.int32, PW), parity, PW // 2)
    pivot = jnp.where(pos_nat[:, None] >= pos_nat[None, :], pivot, pivot.T)
    vmem = pl.BlockSpec(memory_space=pltpu.VMEM)
    inverse = call(
        inverse_kernel,
        jax.ShapeDtypeStruct((PW, PW), F32),
        [pltpu.VMEM((PW, PW), F32), pltpu.VMEM((PW, PW), F32)],
        in_specs=[pl.BlockSpec(memory_space=pltpu.SMEM), vmem],
    )(parity.reshape(1).astype(jnp.int32), pivot)

    local_here = jnp.where(owner_of == grid_pos, local_of, -1)
    own_t, other_t = call(
        functools.partial(owner_kernel, owners, slots, owned),
        [jax.ShapeDtypeStruct((owners, half, owned), BF)] * 2,
        [pltpu.VMEM((owned, PW), F32), pltpu.VMEM((owners, total, owned), BF)],
    )(bulk, panel_all, local_here, slot_of, target_own)
    recv_t = swapped(other_t)

    strips = half_cols // 128
    schur, panel = call(
        final_kernel,
        [
            jax.ShapeDtypeStruct((owned * strips, 128), F32),
            jax.ShapeDtypeStruct((owned, PW // 2), F32),
        ],
    )(
        parent_front.reshape(owned * strips, 128),
        front_cols,
        own_t.reshape(half_cols, owned),
        recv_t.reshape(half_cols, owned),
        inverse,
        rows,
        pivot[: PW // 2],
    )
    return (schur.reshape(owned, 1, half_cols), panel[:, None, :])


def solution(mesh):
    in_specs = (P("grid", "cube", None), P("cube", "grid", None), P("cube", "grid", None), P())
    out_specs = (P("grid", "cube", None), P("grid", "cube", None))
    return jax.shard_map(shards, mesh=mesh, in_specs=in_specs, out_specs=out_specs, check_vma=False)
```

```python
import functools

import jax
import jax.numpy as jnp
from jax import lax
from jax.experimental import pallas as pl
from jax.experimental.pallas import tpu as pltpu
from jax.sharding import PartitionSpec as P

PW = 512
CHUNKS = 2
LOW_ROWS = 16
BF = jnp.bfloat16
F32 = jnp.float32
NN = (((1,), (0,)), ((), ()))
NT = (((1,), (1,)), ((), ()))
VMEM_LIMIT = 60 << 20


def dot(a, b, dims=NN, precision=None):
    return lax.dot_general(a, b, dims, precision=precision, preferred_element_type=F32)


def row_numbers(rows, n):
    return lax.broadcasted_iota(jnp.int32, (rows, n), 0).astype(F32).astype(BF)


def hot(numbers, row_vector):
    one, zero = jnp.ones((), BF), jnp.zeros((), BF)
    return jnp.where(numbers == row_vector.astype(BF), one, zero)


def eye(n, dtype=F32):
    r = lax.broadcasted_iota(jnp.int32, (n, n), 0)
    c = lax.broadcasted_iota(jnp.int32, (n, n), 1)
    return jnp.where(r == c, 1.0, 0.0).astype(dtype)


def call(kernel, out_shape, scratch=(), **kw):
    return pl.pallas_call(
        kernel,
        out_shape=out_shape,
        scratch_shapes=list(scratch),
        compiler_params=pltpu.CompilerParams(vmem_limit_bytes=VMEM_LIMIT),
        **kw,
    )


def source_kernel(owners, slots, owned, block_ref, slot_ref, target_ref, pan_target_ref, *refs):
    outs, pan_ref, y_ref = refs[:CHUNKS], refs[CHUNKS], refs[CHUNKS + 1]
    width = block_ref.shape[0]
    part = owners * slots // 2
    numbers = row_numbers(part, width)

    def first(pair, carry):
        cols = block_ref[:, pl.ds(pl.multiple_of(pair * 2 * width, 128), 2 * width)]
        for side in range(2):
            s = pair * 2 + side
            mine = cols[:, side * width : (side + 1) * width]
            for b in range(2):
                pick = hot(numbers, slot_ref[b, pl.ds(s, 1), :])
                y = dot(pick, mine, NT).astype(BF).reshape(owners // 2, slots, width)
                y_ref[pl.ds(b * (owners // 2), owners // 2), pl.ds(pl.multiple_of(s * slots, 16), slots), :] = y
        return carry

    lax.fori_loop(0, owners // 2, first, 0, unroll=2)
    unit = eye(width, BF)
    spots = row_numbers(owned, owners * slots)
    lanes = owned // CHUNKS

    def place(targets, owner):
        turned = dot(hot(spots, targets), y_ref[owner]).astype(BF)
        return dot(unit, turned, NT).astype(BF)

    half = owned // 2
    for b in range(2):
        z = place(pan_target_ref[pl.ds(b, 1), :], b)
        pan_ref[:, b * half : (b + 1) * half] = z[:, :half]
        pan_ref[:, owned + b * half : owned + (b + 1) * half] = z[:, half:]

    def second(owner, carry):
        z = place(target_ref[pl.ds(owner, 1), :], owner)
        for c in range(CHUNKS):
            outs[c][owner] = z[:, c * lanes : (c + 1) * lanes]
        return carry

    lax.fori_loop(0, owners, second, 0, unroll=2)


def owner_kernel(owners, slots, owned, recv_ref, panel_ref, local_ref, slot_ref, target_ref, own_ref, other_ref, q_ref, y_ref):
    width, lanes = panel_ref.shape[1], recv_ref.shape[2]
    part = owners * slots // 2
    q_ref[...] = jnp.zeros_like(q_ref)
    here = row_numbers(lanes, width)

    def gather(s, carry):
        q_ref[...] += dot(hot(here, local_ref[pl.ds(s, 1), :]), panel_ref[s])
        return carry

    lax.fori_loop(0, owners, gather, 0, unroll=4)
    q = q_ref[...].astype(BF)
    numbers = row_numbers(part, width)

    def first(s, carry):
        product = dot(panel_ref[s], q, NT)
        contrib = (recv_ref[s, :width].astype(F32) - product).astype(BF)
        for b in range(2):
            y = dot(hot(numbers, slot_ref[b, pl.ds(s, 1), :]), contrib).astype(BF)
            y_ref[pl.ds(b * (owners // 2), owners // 2), pl.ds(pl.multiple_of(s * slots, 16), slots), :] = y.reshape(
                owners // 2, slots, lanes
            )
        return carry

    lax.fori_loop(0, owners, first, 0, unroll=4)
    half = owned // 2
    spots = row_numbers(owned, owners * slots)

    def second(owner, carry):
        z = dot(hot(spots, target_ref[pl.ds(owner, 1), :]), y_ref[owner]).astype(BF)
        own_ref[owner] = z[:half]
        other_ref[owner] = z[half:]
        return carry

    lax.fori_loop(0, owners, second, 0, unroll=4)


def split(x):
    hi = x.astype(BF)
    return hi, (x - hi.astype(F32)).astype(BF)


def dot3(a, b, dims=NN):
    return dot(a[0], b[0], dims) + (dot(a[0], b[1], dims) + dot(a[1], b[0], dims))


def natural(position, parity, half):
    return jnp.where(position < half, 2 * position + parity, 2 * (position - half) + 1 - parity)


def inverse_factor(parity, a, w_ref, s_ref, t_ref):
    n = a.shape[0]
    half = n // 2
    row_at = lax.broadcasted_iota(jnp.int32, (n, n), 0)
    col_at = lax.broadcasted_iota(jnp.int32, (n, n), 1)
    row_nat = natural(row_at, parity, half)
    col_nat = natural(col_at, parity, half)
    on = row_at == col_at
    a = jnp.where(row_nat >= col_nat, a, a.T)
    phi = jnp.where(on, 0.5, jnp.where(row_nat > col_nat, 1.0, 0.0))
    unit = jnp.where(on, 1.0, 0.0)
    diagonal = jnp.where(on, a, 0.0)
    scale_row = lax.rsqrt(jnp.sum(diagonal, axis=0, keepdims=True))
    scale_col = lax.rsqrt(jnp.sum(diagonal, axis=1, keepdims=True))
    scaled = a * scale_row * scale_col
    s_ref[...] = scaled
    w_ref[...] = unit - phi * (scaled - unit)
    s_parts = split(scaled)

    def step(state):
        count, _ = state
        w = w_ref[...]
        w_parts = split(w)
        m_parts = split(dot3(w_parts, s_parts))
        e = dot3(m_parts, w_parts, NT) - unit
        w_ref[...] = w - dot3(split(phi * e), w_parts)
        return count + 1, jnp.sum(e * e)

    def more(state):
        count, size = state
        return jnp.logical_and(count < 16, jnp.logical_not(size < 1e-6))

    _, size = lax.while_loop(more, step, (jnp.int32(0), jnp.float32(1.0)))

    @pl.when(jnp.logical_not(size < 1e-6))
    def _():
        lane = lax.broadcasted_iota(jnp.int32, (1, n), 1)
        lane_nat = natural(lane, parity, half)

        def place(j):
            return jnp.where((j & 1) == parity, j >> 1, half + (j >> 1))

        def column(j, carry):
            p = place(j)
            row = jnp.where(lane_nat >= j, s_ref[pl.ds(p, 1), :], 0.0)
            pivot = jnp.sum(jnp.where(lane == p, row, 0.0))
            row = row * lax.rsqrt(jnp.full((1, n), pivot))
            t_ref[pl.ds(p, 1), :] = row
            col = jnp.sum(jnp.where(on, row, 0.0), axis=1, keepdims=True)
            s_ref[...] = s_ref[...] - col * row
            return carry

        lax.fori_loop(0, n, column, 0)
        w_ref[...] = jnp.zeros_like(w_ref)

        def solve(j, carry):
            p = place(j)
            col = jnp.sum(jnp.where(col_at == p, t_ref[...], 0.0), axis=1, keepdims=True)
            known = jnp.sum(col * w_ref[...], axis=0, keepdims=True)
            pivot = jnp.sum(jnp.where(lane == p, t_ref[pl.ds(p, 1), :], 0.0))
            w_ref[pl.ds(p, 1), :] = (jnp.where(lane == p, 1.0, 0.0) - known) / pivot
            return carry

        lax.fori_loop(0, n, solve, 0)

    return w_ref[...] * scale_row


def final_kernel(parity_ref, rows_ref, front_hbm, parent_hbm, *refs):
    own_hbm, recv_hbm = refs[:CHUNKS], refs[CHUNKS : 2 * CHUNKS]
    schur_ref, panel_ref, w_ref, s_ref, t_ref, lead_ref, cols_ref, parent_ref = refs[2 * CHUNKS : 2 * CHUNKS + 8]
    own_ref, recv_ref, sems = refs[2 * CHUNKS + 8 :]
    owned = rows_ref.shape[0]
    half = owned // 2
    strips = parent_ref.shape[0] // owned
    high = lax.Precision.HIGHEST
    copies = [
        pltpu.make_async_copy(front_hbm.at[pl.ds(0, 2)], lead_ref, sems.at[0]),
        pltpu.make_async_copy(front_hbm.at[:, pl.ds(0, half), :], cols_ref, sems.at[1]),
        pltpu.make_async_copy(parent_hbm, parent_ref, sems.at[2]),
    ]
    for c in range(CHUNKS):
        copies.append(pltpu.make_async_copy(own_hbm[c], own_ref.at[c], sems.at[3 + 2 * c]))
        copies.append(pltpu.make_async_copy(recv_hbm[c], recv_ref.at[c], sems.at[4 + 2 * c]))
    for copy in copies:
        copy.start()
    copies[0].wait()
    pieces = [(0, 0), (1, 0), (0, half), (1, half)]
    pivot = jnp.concatenate([lead_ref[b, i : i + half] for b, i in pieces], axis=0).astype(F32)
    low = jnp.concatenate([lead_ref[b, owned : owned + 1, i : i + half] for b, i in pieces], axis=1).astype(F32)
    pivot = pivot + eye(PW) * low
    lead_cols = split(pivot[: PW // 2])
    w = inverse_factor(parity_ref[0], pivot, w_ref, s_ref, t_ref)
    w_ref[...] = w
    factor = dot(rows_ref[...], w, NT, high)
    panel_ref[...] = factor[:, : panel_ref.shape[1]]
    g_hi, g_lo = split(dot(factor, w_ref[...], NN, high))
    for copy in copies[1:]:
        copy.wait()
    lanes = owned // CHUNKS
    unit = eye(lanes, BF)
    for pair in range(strips // 2):
        cols = cols_ref[pl.ds(2 * pair, 2)].reshape(2 * half, PW)
        if pair == 0:
            update = dot3((g_hi, g_lo), lead_cols, NT)
        else:
            update = dot(g_hi, cols, NT) + dot(g_lo, cols, NT)
        placed = []
        for c in range(CHUNKS):
            own = own_ref[c, pl.ds(2 * pair, 2)].reshape(2 * half, lanes)
            recv = recv_ref[c, pl.ds(2 * pair, 2)].reshape(2 * half, lanes)
            placed.append(dot(unit, own, NT) + dot(unit, recv, NT))
        change = jnp.concatenate(placed, axis=0) - update
        for side in range(2):
            at = pl.ds(2 * pair + side, owned, stride=strips)
            schur_ref[at, :] = parent_ref[at, :] + change[:, side * half : (side + 1) * half]


def swap_halves(x, axis):
    a, b = jnp.split(x, 2, axis=axis)
    return jnp.concatenate([b, a], axis=axis)


def swapped(block):
    count = lax.axis_size("cube")
    return lax.ppermute(block, "cube", [(i, i ^ 1) for i in range(count)])


def natural_position(row, parity):
    return ((row & 1) ^ parity) * (PW // 2) + (row >> 1) + jnp.where(row < PW, 0, PW)


def low_message(low):
    return jnp.pad(low.astype(BF)[None, :], ((0, LOW_ROWS - 1), (0, PW - low.shape[0])))


def exchanged(block):
    return lax.all_to_all(block, "grid", 0, 0, tiled=True)


def shards(parent_front, child_block, child_panel, row_map):
    owners = lax.axis_size("grid")
    cube_pos = lax.axis_index("cube")
    grid_pos = lax.axis_index("grid")
    parity = cube_pos % 2
    width = child_block.shape[1]
    owned = parent_front.shape[0]
    half_cols = parent_front.shape[2]
    capacity = 2 * width // owners
    slots = -(-capacity // 16) * 16
    total = owners * slots
    half = owned // 2
    lanes = owned // CHUNKS
    own_panel = child_panel[0]
    panel_all = lax.all_gather(own_panel, "grid")

    row_of = lax.dynamic_index_in_dim(row_map, cube_pos, 0, keepdims=False).reshape(owners, width)
    owner_of = row_of // owned
    local_of = row_of % owned
    earlier = lax.iota(jnp.int32, width)[:, None] < lax.iota(jnp.int32, width)[None, :]
    same = (owner_of[:, :, None] == owner_of[:, None, :]) & earlier[None]
    rank_of = jnp.sum(same.astype(jnp.int32), axis=1)
    slot_of = owner_of * slots + rank_of
    hits = slot_of[:, :, None] == lax.iota(jnp.int32, total)[None, None, :]
    target = jnp.sum(jnp.where(hits, local_of[:, :, None] + 1, 0), axis=1) - 1
    target = target.reshape(owners, owners, slots).transpose(1, 0, 2)
    target_nat = target.reshape(owners, total)
    target_own = jnp.where(
        target_nat >= 0, ((target_nat & 1) ^ parity) * half + (target_nat >> 1), -1
    ).astype(F32)
    slot_parts = slot_of[None] - jnp.array([0, total // 2])[:, None, None]
    slot_parts = jnp.where((slot_parts >= 0) & (slot_parts < total // 2), slot_parts, -1).astype(F32)
    my_slot = lax.dynamic_index_in_dim(slot_of, grid_pos, 0, keepdims=False)
    my_owner = lax.dynamic_index_in_dim(owner_of, grid_pos, 0, keepdims=False)
    my_rank = lax.dynamic_index_in_dim(rank_of, grid_pos, 0, keepdims=False)

    pivot_slot = jnp.where(my_owner < 2, my_owner * capacity + my_rank, -1)
    pivot_pick = (lax.iota(jnp.int32, 2 * capacity)[:, None] == pivot_slot[None, :]).astype(BF)
    pivot_rows = dot(pivot_pick, own_panel).astype(BF)
    pivot_rows = exchanged(jnp.broadcast_to(pivot_rows[None], (owners,) + pivot_rows.shape))

    outs = call(
        functools.partial(source_kernel, owners, slots, owned),
        [jax.ShapeDtypeStruct((owners, width, lanes), BF)] * CHUNKS + [jax.ShapeDtypeStruct((width, PW), BF)],
        [pltpu.VMEM((owners, total, width), BF)],
    )(child_block[0], slot_parts, target_nat.astype(F32), target_own)
    spread, block_pan = outs[:CHUNKS], outs[CHUNKS]
    pivot_target = target[:2, :, :capacity]
    pivot_pos = jnp.where(
        pivot_target >= 0,
        ((pivot_target & 1) ^ parity) * (PW // 2)
        + lax.iota(jnp.int32, 2)[:, None, None] * half
        + (pivot_target >> 1),
        -1,
    )
    pivot_pos = pivot_pos.transpose(1, 0, 2).reshape(-1)
    pivot_hot = (lax.iota(jnp.int32, PW)[:, None] == pivot_pos[None, :]).astype(BF)
    panel_pan = dot(pivot_hot, pivot_rows.reshape(-1, PW)).astype(BF)

    contrib_pan = (block_pan.astype(F32) - dot(own_panel, panel_pan, NT)).astype(BF)
    pack = (lax.iota(jnp.int32, total)[:, None] == my_slot[None, :]).astype(BF)
    packed = dot(pack, contrib_pan).astype(BF).reshape(owners, slots, PW)
    packed = [packed[:, :, i : i + lanes] for i in range(0, PW, lanes)]
    bulk_first = exchanged(jnp.concatenate([spread[0]] + packed, axis=1))
    bulk = [bulk_first] + [exchanged(part) for part in spread[1:]]
    packed = [bulk_first[:, width + i * slots : width + (i + 1) * slots] for i in range(PW // lanes)]
    packed = jnp.concatenate(packed, axis=2).reshape(total, PW)
    my_target = lax.dynamic_index_in_dim(target_nat, grid_pos, 0, keepdims=False)
    unpack = (lax.iota(jnp.int32, owned)[:, None] == my_target[None, :]).astype(BF)
    rows_mine = dot(unpack, packed) + jnp.pad(parent_front[:, 0, : PW // 2], ((0, 0), (0, PW // 2)))
    row_pos = natural_position(grid_pos * owned + lax.iota(jnp.int32, owned), parity)
    diagonal = row_pos[:, None] == lax.iota(jnp.int32, PW)[None, :]

    def rounded(x):
        return lax.reduce_precision(x, 8, 7)

    low_mine = jnp.sum(jnp.where(diagonal, rows_mine - rounded(rows_mine), 0.0), axis=1)
    rows_theirs = swapped(jnp.concatenate([rows_mine.astype(BF), low_message(low_mine)], axis=0))
    low_theirs = rows_theirs[owned, :owned].astype(F32)[:, None]
    rows = rows_mine + swap_halves(rows_theirs[:owned], 1).astype(F32)
    rows = rows + jnp.where(diagonal & (row_pos >= PW // 2)[:, None], low_theirs, 0.0)
    low_rows = jnp.sum(jnp.where(diagonal, rows - rounded(rows), 0.0), axis=1)
    local_order = natural(lax.iota(jnp.int32, owned), parity, half)
    choose = local_order[:, None] == lax.iota(jnp.int32, owned)[None, :]
    low_rows = jnp.sum(jnp.where(choose, low_rows[None, :], 0.0), axis=1)
    front_cols = dot(choose.astype(BF), rows.astype(BF)).astype(BF)
    front_cols = lax.all_gather(jnp.concatenate([front_cols, low_message(low_rows)], axis=0), "grid")

    local_here = jnp.where(owner_of == grid_pos, local_of, -1)
    own_t, other_t = [], []
    for c in range(CHUNKS):
        local_part = local_here - c * lanes
        local_part = jnp.where((local_here >= 0) & (local_part >= 0) & (local_part < lanes), local_part, -1)
        a, b = call(
            functools.partial(owner_kernel, owners, slots, owned),
            [jax.ShapeDtypeStruct((owners, half, lanes), BF)] * 2,
            [pltpu.VMEM((lanes, PW), F32), pltpu.VMEM((owners, total, lanes), BF)],
        )(bulk[c], panel_all, local_part.astype(F32), slot_parts, target_own)
        own_t.append(a)
        other_t.append(b)
    recv_t = [swapped(x) for x in other_t]

    strips = half_cols // 128
    anywhere = pl.BlockSpec(memory_space=pl.ANY)
    vmem = pl.BlockSpec(memory_space=pltpu.VMEM)
    schur, panel = call(
        final_kernel,
        [
            jax.ShapeDtypeStruct((owned * strips, 128), F32),
            jax.ShapeDtypeStruct((owned, PW // 2), F32),
        ],
        [
            pltpu.VMEM((PW, PW), F32),
            pltpu.VMEM((PW, PW), F32),
            pltpu.VMEM((PW, PW), F32),
            pltpu.VMEM((2, owned + LOW_ROWS, PW), BF),
            pltpu.VMEM((owners, half, PW), BF),
            pltpu.VMEM((owned * strips, 128), F32),
            pltpu.VMEM((CHUNKS, owners, half, lanes), BF),
            pltpu.VMEM((CHUNKS, owners, half, lanes), BF),
            pltpu.SemaphoreType.DMA((3 + 2 * CHUNKS,)),
        ],
        in_specs=[pl.BlockSpec(memory_space=pltpu.SMEM), vmem] + [anywhere] * (2 + 2 * CHUNKS),
        out_specs=[vmem, vmem],
    )(
        parity.reshape(1).astype(jnp.int32),
        rows,
        front_cols,
        parent_front.reshape(owned * strips, 128),
        *own_t,
        *recv_t,
    )
    return (schur.reshape(owned, 1, half_cols), panel[:, None, :])


def solution(mesh):
    in_specs = (P("grid", "cube", None), P("cube", "grid", None), P("cube", "grid", None), P())
    out_specs = (P("grid", "cube", None), P("grid", "cube", None))
    return jax.shard_map(shards, mesh=mesh, in_specs=in_specs, out_specs=out_specs, check_vma=False)
```

```python
import functools

import jax
import jax.numpy as jnp
from jax import lax
from jax.experimental import pallas as pl
from jax.experimental.pallas import tpu as pltpu
from jax.sharding import PartitionSpec as P

PW = 512
CHUNKS = 2
LOW_ROWS = 16
SOURCE_UNROLL = 4
OWNER_UNROLL = 8
BF = jnp.bfloat16
F32 = jnp.float32
NN = (((1,), (0,)), ((), ()))
NT = (((1,), (1,)), ((), ()))
VMEM_LIMIT = 60 << 20


def dot(a, b, dims=NN, precision=None):
    return lax.dot_general(a, b, dims, precision=precision, preferred_element_type=F32)


def row_numbers(rows, n):
    return lax.broadcasted_iota(jnp.int32, (rows, n), 0).astype(F32).astype(BF)


def hot(numbers, row_vector):
    one, zero = jnp.ones((), BF), jnp.zeros((), BF)
    return jnp.where(numbers == row_vector.astype(BF), one, zero)


def eye(n, dtype=F32):
    r = lax.broadcasted_iota(jnp.int32, (n, n), 0)
    c = lax.broadcasted_iota(jnp.int32, (n, n), 1)
    return jnp.where(r == c, 1.0, 0.0).astype(dtype)


def call(kernel, out_shape, scratch=(), flops=0, **kw):
    moved = sum(x.size * x.dtype.itemsize for x in jax.tree.leaves(out_shape))
    return pl.pallas_call(
        kernel,
        out_shape=out_shape,
        scratch_shapes=list(scratch),
        cost_estimate=pl.CostEstimate(flops=flops, transcendentals=0, bytes_accessed=2 * moved),
        compiler_params=pltpu.CompilerParams(vmem_limit_bytes=VMEM_LIMIT),
        **kw,
    )


def source_kernel(owners, slots, owned, block_ref, slot_ref, target_ref, *refs):
    outs, y_ref = refs[:CHUNKS], refs[CHUNKS]
    width = block_ref.shape[0]
    part = owners * slots // 2
    numbers = row_numbers(part, width)

    def first(pair, carry):
        cols = block_ref[:, pl.ds(pl.multiple_of(pair * 2 * width, 128), 2 * width)]
        for side in range(2):
            s = pair * 2 + side
            mine = cols[:, side * width : (side + 1) * width]
            for b in range(2):
                pick = hot(numbers, slot_ref[b, pl.ds(s, 1), :])
                y = dot(pick, mine, NT).astype(BF).reshape(owners // 2, slots, width)
                y_ref[pl.ds(b * (owners // 2), owners // 2), pl.ds(pl.multiple_of(s * slots, 16), slots), :] = y
        return carry

    lax.fori_loop(0, owners // 2, first, 0, unroll=SOURCE_UNROLL)
    unit = eye(width, BF)
    spots = row_numbers(owned, owners * slots)
    lanes = owned // CHUNKS

    def second(owner, carry):
        turned = dot(hot(spots, target_ref[pl.ds(owner, 1), :]), y_ref[owner]).astype(BF)
        z = dot(unit, turned, NT).astype(BF)
        for c in range(CHUNKS):
            outs[c][owner] = z[:, c * lanes : (c + 1) * lanes]
        return carry

    lax.fori_loop(0, owners, second, 0, unroll=2 * SOURCE_UNROLL)


def product_kernel(panel_ref, local_ref, *refs):
    outs, q_ref = refs[:CHUNKS], refs[CHUNKS]
    owners, width = panel_ref.shape[:2]
    owned = q_ref.shape[0]
    lanes = owned // CHUNKS
    here = row_numbers(owned, width)
    q_ref[...] = jnp.zeros_like(q_ref)

    def gather(s, carry):
        q_ref[...] += dot(hot(here, local_ref[pl.ds(s, 1), :]), panel_ref[s])
        return carry

    lax.fori_loop(0, owners, gather, 0, unroll=4)
    q = q_ref[...].astype(BF)

    def first(s, carry):
        product = dot(panel_ref[s], q, NT)
        for c in range(CHUNKS):
            outs[c][s] = product[:, c * lanes : (c + 1) * lanes]
        return carry

    lax.fori_loop(0, owners, first, 0, unroll=4)


def owner_kernel(owners, slots, owned, recv_ref, product_ref, slot_ref, target_ref, own_ref, other_ref, y_ref):
    width, lanes = recv_ref.shape[1:]
    part = owners * slots // 2
    numbers = row_numbers(part, width)

    def first(s, carry):
        contrib = (recv_ref[s].astype(F32) - product_ref[s]).astype(BF)
        for b in range(2):
            y = dot(hot(numbers, slot_ref[b, pl.ds(s, 1), :]), contrib).astype(BF)
            y_ref[pl.ds(b * (owners // 2), owners // 2), pl.ds(pl.multiple_of(s * slots, 16), slots), :] = y.reshape(
                owners // 2, slots, lanes
            )
        return carry

    lax.fori_loop(0, owners, first, 0, unroll=OWNER_UNROLL)
    half = owned // 2
    spots = row_numbers(owned, owners * slots)

    def second(owner, carry):
        z = dot(hot(spots, target_ref[pl.ds(owner, 1), :]), y_ref[owner]).astype(BF)
        own_ref[owner] = z[:half]
        other_ref[owner] = z[half:]
        return carry

    lax.fori_loop(0, owners, second, 0, unroll=OWNER_UNROLL)


def split(x):
    hi = x.astype(BF)
    return hi, (x - hi.astype(F32)).astype(BF)


def dot3(a, b, dims=NN):
    return dot(a[0], b[0], dims) + (dot(a[0], b[1], dims) + dot(a[1], b[0], dims))


def natural(position, parity, half):
    return jnp.where(position < half, 2 * position + parity, 2 * (position - half) + 1 - parity)


def inverse_factor(parity, a, w_ref, s_ref, t_ref):
    n = a.shape[0]
    half = n // 2
    row_at = lax.broadcasted_iota(jnp.int32, (n, n), 0)
    col_at = lax.broadcasted_iota(jnp.int32, (n, n), 1)
    row_nat = natural(row_at, parity, half)
    col_nat = natural(col_at, parity, half)
    on = row_at == col_at
    a = jnp.where(row_nat >= col_nat, a, a.T)
    phi = jnp.where(on, 0.5, jnp.where(row_nat > col_nat, 1.0, 0.0))
    unit = jnp.where(on, 1.0, 0.0)
    diagonal = jnp.where(on, a, 0.0)
    scale_row = lax.rsqrt(jnp.sum(diagonal, axis=0, keepdims=True))
    scale_col = lax.rsqrt(jnp.sum(diagonal, axis=1, keepdims=True))
    scaled = a * scale_row * scale_col
    s_ref[...] = scaled
    w_ref[...] = unit - phi * (scaled - unit)
    s_parts = split(scaled)

    def step(state):
        count, _ = state
        w = w_ref[...]
        w_parts = split(w)
        m_parts = split(dot3(w_parts, s_parts))
        e = dot3(m_parts, w_parts, NT) - unit
        w_ref[...] = w - dot3(split(phi * e), w_parts)
        return count + 1, jnp.sum(e * e)

    def more(state):
        count, size = state
        return jnp.logical_and(count < 16, jnp.logical_not(size < 1e-6))

    _, size = lax.while_loop(more, step, (jnp.int32(0), jnp.float32(1.0)))

    @pl.when(jnp.logical_not(size < 1e-6))
    def _():
        lane = lax.broadcasted_iota(jnp.int32, (1, n), 1)
        lane_nat = natural(lane, parity, half)

        def place(j):
            return jnp.where((j & 1) == parity, j >> 1, half + (j >> 1))

        def column(j, carry):
            p = place(j)
            row = jnp.where(lane_nat >= j, s_ref[pl.ds(p, 1), :], 0.0)
            pivot = jnp.sum(jnp.where(lane == p, row, 0.0))
            row = row * lax.rsqrt(jnp.full((1, n), pivot))
            t_ref[pl.ds(p, 1), :] = row
            col = jnp.sum(jnp.where(on, row, 0.0), axis=1, keepdims=True)
            s_ref[...] = s_ref[...] - col * row
            return carry

        lax.fori_loop(0, n, column, 0)
        w_ref[...] = jnp.zeros_like(w_ref)

        def solve(j, carry):
            p = place(j)
            col = jnp.sum(jnp.where(col_at == p, t_ref[...], 0.0), axis=1, keepdims=True)
            known = jnp.sum(col * w_ref[...], axis=0, keepdims=True)
            pivot = jnp.sum(jnp.where(lane == p, t_ref[pl.ds(p, 1), :], 0.0))
            w_ref[pl.ds(p, 1), :] = (jnp.where(lane == p, 1.0, 0.0) - known) / pivot
            return carry

        lax.fori_loop(0, n, solve, 0)

    return w_ref[...] * scale_row


def factor_kernel(parity_ref, rows_ref, front_hbm, parent_hbm, *refs):
    own_hbm, recv_hbm = refs[:CHUNKS], refs[CHUNKS : 2 * CHUNKS - 1]
    schur_ref, panel_ref, w_ref, s_ref, t_ref, lead_ref, cols_ref, parent_ref = refs[2 * CHUNKS - 1 : 2 * CHUNKS + 7]
    own_ref, recv_ref, sems = refs[2 * CHUNKS + 7 :]
    owned = rows_ref.shape[0]
    half = owned // 2
    strips = parent_ref.shape[0] // owned
    high = lax.Precision.HIGHEST
    copies = [
        pltpu.make_async_copy(front_hbm.at[pl.ds(0, 2)], lead_ref, sems.at[0]),
        pltpu.make_async_copy(front_hbm.at[:, pl.ds(0, half), :], cols_ref, sems.at[1]),
        pltpu.make_async_copy(parent_hbm, parent_ref, sems.at[2]),
    ]
    for c in range(CHUNKS):
        copies.append(pltpu.make_async_copy(own_hbm[c], own_ref.at[c], sems.at[3 + c]))
    for c in range(CHUNKS - 1):
        copies.append(pltpu.make_async_copy(recv_hbm[c], recv_ref.at[c], sems.at[3 + CHUNKS + c]))
    for copy in copies:
        copy.start()
    copies[0].wait()
    pieces = [(0, 0), (1, 0), (0, half), (1, half)]
    pivot = jnp.concatenate([lead_ref[b, i : i + half] for b, i in pieces], axis=0).astype(F32)
    low = jnp.concatenate([lead_ref[b, owned : owned + 1, i : i + half] for b, i in pieces], axis=1).astype(F32)
    pivot = pivot + eye(PW) * low
    lead_cols = split(pivot[: PW // 2])
    w = inverse_factor(parity_ref[0], pivot, w_ref, s_ref, t_ref)
    w_ref[...] = w
    factor = dot(rows_ref[...], w, NT, high)
    panel_ref[...] = factor[:, : panel_ref.shape[1]]
    g_hi, g_lo = split(dot(factor, w_ref[...], NN, high))
    for copy in copies[1:]:
        copy.wait()
    lanes = owned // CHUNKS
    unit = eye(lanes, BF)
    for pair in range(strips // 2):
        cols = cols_ref[pl.ds(2 * pair, 2)].reshape(2 * half, PW)
        if pair == 0:
            update = dot3((g_hi, g_lo), lead_cols, NT)
        else:
            update = dot(g_hi, cols, NT) + dot(g_lo, cols, NT)
        placed = []
        for c in range(CHUNKS):
            z = dot(unit, own_ref[c, pl.ds(2 * pair, 2)].reshape(2 * half, lanes), NT)
            if c < CHUNKS - 1:
                z = z + dot(unit, recv_ref[c, pl.ds(2 * pair, 2)].reshape(2 * half, lanes), NT)
            placed.append(z)
        change = jnp.concatenate(placed, axis=0) - update
        for side in range(2):
            at = pl.ds(2 * pair + side, owned, stride=strips)
            schur_ref[at, :] = parent_ref[at, :] + change[:, side * half : (side + 1) * half]


def last_kernel(schur_ref, recv_ref, out_ref):
    rows = pl.program_id(0)
    lanes = recv_ref.shape[2]
    strips = recv_ref.shape[0]
    part = schur_ref.shape[0] // strips
    r = lax.broadcasted_iota(jnp.int32, (part, lanes), 0) + rows * part
    c = lax.broadcasted_iota(jnp.int32, (part, lanes), 1)
    unit = jnp.where(r == c, 1.0, 0.0).astype(BF)
    for pair in range(strips // 2):
        z = dot(unit, recv_ref[pl.ds(2 * pair, 2)].reshape(-1, lanes), NT)
        for side in range(2):
            at = pl.ds(2 * pair + side, part, stride=strips)
            out_ref[at, :] = schur_ref[at, :] + z[:, side * 128 : (side + 1) * 128]


def swap_halves(x, axis):
    a, b = jnp.split(x, 2, axis=axis)
    return jnp.concatenate([b, a], axis=axis)


def swapped(block):
    count = lax.axis_size("cube")
    return lax.ppermute(block, "cube", [(i, i ^ 1) for i in range(count)])


def natural_position(row, parity):
    return ((row & 1) ^ parity) * (PW // 2) + (row >> 1) + jnp.where(row < PW, 0, PW)


def low_message(low):
    return jnp.pad(low.astype(BF)[None, :], ((0, LOW_ROWS - 1), (0, PW - low.shape[0])))


def exchanged(block):
    return lax.all_to_all(block, "grid", 0, 0, tiled=True)


def shards(parent_front, child_block, child_panel, row_map):
    owners = lax.axis_size("grid")
    cube_pos = lax.axis_index("cube")
    grid_pos = lax.axis_index("grid")
    parity = cube_pos % 2
    width = child_block.shape[1]
    owned = parent_front.shape[0]
    half_cols = parent_front.shape[2]
    capacity = 2 * width // owners
    slots = -(-capacity // 16) * 16
    total = owners * slots
    half = owned // 2
    lanes = owned // CHUNKS
    own_panel = child_panel[0]
    panel_all = lax.all_gather(own_panel, "grid")

    row_of = lax.dynamic_index_in_dim(row_map, cube_pos, 0, keepdims=False).reshape(owners, width)
    owner_of = row_of // owned
    local_of = row_of % owned
    earlier = lax.iota(jnp.int32, width)[:, None] < lax.iota(jnp.int32, width)[None, :]
    same = (owner_of[:, :, None] == owner_of[:, None, :]) & earlier[None]
    rank_of = jnp.sum(same.astype(jnp.int32), axis=1)
    slot_of = owner_of * slots + rank_of
    hits = slot_of[:, :, None] == lax.iota(jnp.int32, total)[None, None, :]
    target = jnp.sum(jnp.where(hits, local_of[:, :, None] + 1, 0), axis=1) - 1
    target = target.reshape(owners, owners, slots).transpose(1, 0, 2)
    target_nat = target.reshape(owners, total)
    target_own = jnp.where(
        target_nat >= 0, ((target_nat & 1) ^ parity) * half + (target_nat >> 1), -1
    ).astype(F32)
    slot_parts = slot_of[None] - jnp.array([0, total // 2])[:, None, None]
    slot_parts = jnp.where((slot_parts >= 0) & (slot_parts < total // 2), slot_parts, -1).astype(F32)
    my_slot = lax.dynamic_index_in_dim(slot_of, grid_pos, 0, keepdims=False)
    my_owner = lax.dynamic_index_in_dim(owner_of, grid_pos, 0, keepdims=False)
    my_rank = lax.dynamic_index_in_dim(rank_of, grid_pos, 0, keepdims=False)

    pivot_slot = jnp.where(my_owner < 2, my_owner * capacity + my_rank, -1)
    pivot_pick = (lax.iota(jnp.int32, 2 * capacity)[:, None] == pivot_slot[None, :]).astype(BF)
    pivot_rows = dot(pivot_pick, own_panel).astype(BF)
    pivot_rows = exchanged(jnp.broadcast_to(pivot_rows[None], (owners,) + pivot_rows.shape))

    row_flat = row_of.reshape(-1)
    pan_of = jnp.where(row_flat < PW, ((row_flat & 1) ^ parity) * (PW // 2) + (row_flat >> 1), -1)
    block_pan = dot(child_block[0], (pan_of[:, None] == lax.iota(jnp.int32, PW)[None, :]).astype(BF)).astype(BF)

    pivot_target = target[:2, :, :capacity]
    pivot_pos = jnp.where(
        pivot_target >= 0,
        ((pivot_target & 1) ^ parity) * (PW // 2)
        + lax.iota(jnp.int32, 2)[:, None, None] * half
        + (pivot_target >> 1),
        -1,
    )
    pivot_pos = pivot_pos.transpose(1, 0, 2).reshape(-1)
    pivot_hot = (lax.iota(jnp.int32, PW)[:, None] == pivot_pos[None, :]).astype(BF)
    panel_pan = dot(pivot_hot, pivot_rows.reshape(-1, PW)).astype(BF)

    contrib_pan = (block_pan.astype(F32) - dot(own_panel, panel_pan, NT)).astype(BF)
    pack = (lax.iota(jnp.int32, total)[:, None] == my_slot[None, :]).astype(BF)
    packed = dot(pack, contrib_pan).astype(BF).reshape(owners, slots, PW)
    packed, slot_parts = lax.optimization_barrier((packed, slot_parts))
    packed = exchanged(packed)
    spread = call(
        functools.partial(source_kernel, owners, slots, owned),
        [jax.ShapeDtypeStruct((owners, width, lanes), BF)] * CHUNKS,
        [pltpu.VMEM((owners, total, width), BF)],
        flops=6 * owners * total * width * width,
    )(child_block[0], slot_parts, target_nat.astype(F32))
    packed, spread = lax.optimization_barrier((packed, spread))
    packed = packed.reshape(total, PW)
    my_target = lax.dynamic_index_in_dim(target_nat, grid_pos, 0, keepdims=False)
    unpack = (lax.iota(jnp.int32, owned)[:, None] == my_target[None, :]).astype(BF)
    rows_mine = dot(unpack, packed) + jnp.pad(parent_front[:, 0, : PW // 2], ((0, 0), (0, PW // 2)))
    row_pos = natural_position(grid_pos * owned + lax.iota(jnp.int32, owned), parity)
    diagonal = row_pos[:, None] == lax.iota(jnp.int32, PW)[None, :]

    def rounded(x):
        return lax.reduce_precision(x, 8, 7)

    low_mine = jnp.sum(jnp.where(diagonal, rows_mine - rounded(rows_mine), 0.0), axis=1)
    rows_theirs = swapped(jnp.concatenate([rows_mine.astype(BF), low_message(low_mine)], axis=0))
    low_theirs = rows_theirs[owned, :owned].astype(F32)[:, None]
    rows = rows_mine + swap_halves(rows_theirs[:owned], 1).astype(F32)
    rows = rows + jnp.where(diagonal & (row_pos >= PW // 2)[:, None], low_theirs, 0.0)
    low_rows = jnp.sum(jnp.where(diagonal, rows - rounded(rows), 0.0), axis=1)
    local_order = natural(lax.iota(jnp.int32, owned), parity, half)
    choose = local_order[:, None] == lax.iota(jnp.int32, owned)[None, :]
    low_rows = jnp.sum(jnp.where(choose, low_rows[None, :], 0.0), axis=1)
    front_cols = dot(choose.astype(BF), rows.astype(BF)).astype(BF)
    front_cols = lax.all_gather(jnp.concatenate([front_cols, low_message(low_rows)], axis=0), "grid")

    bulk = [exchanged(spread[0])]
    local_here = jnp.where(owner_of == grid_pos, local_of, -1).astype(F32)
    product = call(
        product_kernel,
        [jax.ShapeDtypeStruct((owners, width, lanes), F32)] * CHUNKS,
        [pltpu.VMEM((owned, PW), F32)],
        flops=4 * owners * width * owned * PW,
    )(panel_all, local_here)
    rest, product = lax.optimization_barrier((spread[1:], product))
    bulk = bulk + [exchanged(part) for part in rest]
    own_t, other_t = [], []
    for c in range(CHUNKS):
        a, b = call(
            functools.partial(owner_kernel, owners, slots, owned),
            [jax.ShapeDtypeStruct((owners, half, lanes), BF)] * 2,
            [pltpu.VMEM((owners, total, lanes), BF)],
            flops=8 * owners * total * width * lanes,
        )(bulk[c], product[c], slot_parts, target_own)
        own_t.append(a)
        other_t.append(b)
    recv_t = [swapped(x) for x in other_t]

    strips = half_cols // 128
    anywhere = pl.BlockSpec(memory_space=pl.ANY)
    vmem = pl.BlockSpec(memory_space=pltpu.VMEM)
    schur, panel = call(
        factor_kernel,
        [
            jax.ShapeDtypeStruct((owned * strips, 128), F32),
            jax.ShapeDtypeStruct((owned, PW // 2), F32),
        ],
        [
            pltpu.VMEM((PW, PW), F32),
            pltpu.VMEM((PW, PW), F32),
            pltpu.VMEM((PW, PW), F32),
            pltpu.VMEM((2, owned + LOW_ROWS, PW), BF),
            pltpu.VMEM((owners, half, PW), BF),
            pltpu.VMEM((owned * strips, 128), F32),
            pltpu.VMEM((CHUNKS, owners, half, lanes), BF),
            pltpu.VMEM((CHUNKS - 1, owners, half, lanes), BF),
            pltpu.SemaphoreType.DMA((2 + 2 * CHUNKS,)),
        ],
        flops=60 * PW**3,
        in_specs=[pl.BlockSpec(memory_space=pltpu.SMEM), vmem] + [anywhere] * (1 + 2 * CHUNKS),
        out_specs=[vmem, vmem],
    )(
        parity.reshape(1).astype(jnp.int32),
        rows,
        front_cols,
        parent_front.reshape(owned * strips, 128),
        *own_t,
        *recv_t[:-1],
    )
    steps = 4
    last_rows = pl.BlockSpec((lanes * strips // steps, 128), lambda i: ((CHUNKS - 1) * steps + i, 0))
    schur = call(
        last_kernel,
        jax.ShapeDtypeStruct((owned * strips, 128), F32),
        grid=(steps,),
        in_specs=[last_rows, pl.BlockSpec((owners, half, lanes), lambda i: (0, 0, 0))],
        out_specs=last_rows,
        input_output_aliases={0: 0},
    )(schur, recv_t[-1])
    return (schur.reshape(owned, 1, half_cols), panel[:, None, :])


def solution(mesh):
    in_specs = (P("grid", "cube", None), P("cube", "grid", None), P("cube", "grid", None), P())
    out_specs = (P("grid", "cube", None), P("grid", "cube", None))
    return jax.shard_map(shards, mesh=mesh, in_specs=in_specs, out_specs=out_specs, check_vma=False)
```

```python
import functools

import jax
import jax.numpy as jnp
from jax import lax
from jax.experimental import pallas as pl
from jax.experimental.pallas import tpu as pltpu
from jax.sharding import PartitionSpec as P

PW = 512
CHUNKS = 2
LOW_ROWS = 16
SOURCE_UNROLL = 4
OWNER_UNROLL = 8
BF = jnp.bfloat16
F32 = jnp.float32
NN = (((1,), (0,)), ((), ()))
NT = (((1,), (1,)), ((), ()))
VMEM_LIMIT = 60 << 20


def dot(a, b, dims=NN, precision=None):
    return lax.dot_general(a, b, dims, precision=precision, preferred_element_type=F32)


def row_numbers(rows, n):
    return lax.broadcasted_iota(jnp.int32, (rows, n), 0).astype(F32).astype(BF)


def hot(numbers, row_vector):
    one, zero = jnp.ones((), BF), jnp.zeros((), BF)
    return jnp.where(numbers == row_vector.astype(BF), one, zero)


def eye(n, dtype=F32):
    r = lax.broadcasted_iota(jnp.int32, (n, n), 0)
    c = lax.broadcasted_iota(jnp.int32, (n, n), 1)
    return jnp.where(r == c, 1.0, 0.0).astype(dtype)


def call(kernel, out_shape, scratch=(), flops=0, **kw):
    moved = sum(x.size * x.dtype.itemsize for x in jax.tree.leaves(out_shape))
    return pl.pallas_call(
        kernel,
        out_shape=out_shape,
        scratch_shapes=list(scratch),
        cost_estimate=pl.CostEstimate(flops=flops, transcendentals=0, bytes_accessed=2 * moved),
        compiler_params=pltpu.CompilerParams(vmem_limit_bytes=VMEM_LIMIT),
        **kw,
    )


def source_kernel(owners, slots, owned, block_ref, slot_ref, target_ref, *refs):
    outs, y_ref = refs[:CHUNKS], refs[CHUNKS]
    width = block_ref.shape[0]
    part = owners * slots // 2
    numbers = row_numbers(part, width)

    def first(pair, carry):
        cols = block_ref[:, pl.ds(pl.multiple_of(pair * 2 * width, 128), 2 * width)]
        for side in range(2):
            s = pair * 2 + side
            mine = cols[:, side * width : (side + 1) * width]
            for b in range(2):
                pick = hot(numbers, slot_ref[b, pl.ds(s, 1), :])
                y = dot(pick, mine, NT).astype(BF).reshape(owners // 2, slots, width)
                y_ref[pl.ds(b * (owners // 2), owners // 2), pl.ds(pl.multiple_of(s * slots, 16), slots), :] = y
        return carry

    lax.fori_loop(0, owners // 2, first, 0, unroll=SOURCE_UNROLL)
    unit = eye(width, BF)
    spots = row_numbers(owned, owners * slots)
    lanes = owned // CHUNKS

    def second(owner, carry):
        turned = dot(hot(spots, target_ref[pl.ds(owner, 1), :]), y_ref[owner]).astype(BF)
        z = dot(unit, turned, NT).astype(BF)
        for c in range(CHUNKS):
            outs[c][owner] = z[:, c * lanes : (c + 1) * lanes]
        return carry

    lax.fori_loop(0, owners, second, 0, unroll=2 * SOURCE_UNROLL)


def panel_kernel(
    owners, slots, place_ref, panel_ref, here_ref, slot_ref, targets_ref, mine_ref, packed_ref, parent_ref,
    rows_ref, message_ref, q_ref, pick_ref,
):
    parity, grid_pos = place_ref[0], place_ref[1]
    width = panel_ref.shape[1]
    owned = q_ref.shape[0]
    half = owned // 2
    few, more = row_numbers(slots, width), row_numbers(2 * slots, width)

    def select(s, carry):
        pick = jnp.concatenate([hot(few, here_ref[pl.ds(s, 1), :]), hot(more, slot_ref[0, pl.ds(s, 1), :])], axis=0)
        found = dot(pick, panel_ref[s]).astype(BF).reshape(3, slots, PW)
        pick_ref[:, pl.ds(pl.multiple_of(s * slots, 16), slots), :] = found
        return carry

    lax.fori_loop(0, owners, select, 0, unroll=8)
    spots = row_numbers(owned, owners * slots)
    mine = hot(spots, mine_ref[...])
    q = dot(mine, pick_ref[0]).astype(BF)
    q_ref[...] = q
    placed = dot(mine, packed_ref[...])
    own, other = [], []
    for b in range(2):
        pan = dot(hot(spots, targets_ref[b : b + 1, :]), pick_ref[1 + b]).astype(BF)
        product = dot(q, pan, NT)
        own.append(product[:, :half])
        other.append(product[:, half:])
    contrib = (placed - jnp.concatenate(own + other, axis=1)).astype(BF).astype(F32)
    rows = jnp.concatenate([contrib[:, :owned] + parent_ref[...], contrib[:, owned:]], axis=1)
    rows_ref[...] = rows
    rounded = rows.astype(BF)
    low = jnp.where(diagonal_at(grid_pos, parity, owned), rows - rounded.astype(F32), 0.0)
    message_ref[:owned] = rounded
    message_ref[owned:] = jnp.broadcast_to(jnp.sum(low, axis=0, keepdims=True), (LOW_ROWS, PW)).astype(BF)


def diagonal_at(grid_pos, parity, owned):
    row = lax.broadcasted_iota(jnp.int32, (owned, PW), 0) + grid_pos * owned
    return natural(lax.broadcasted_iota(jnp.int32, (owned, PW), 1), parity, PW // 2) == row


def rows_kernel(place_ref, mine_ref, theirs_ref, rows_ref, message_ref):
    parity, grid_pos = place_ref[0], place_ref[1]
    owned = mine_ref.shape[0]
    half = owned // 2
    theirs = theirs_ref[...].astype(F32)
    theirs = jnp.concatenate([theirs[:, PW // 2 :], theirs[:, : PW // 2]], axis=1)
    on = diagonal_at(grid_pos, parity, owned)
    rows = mine_ref[...] + theirs[:owned] + jnp.where(on, theirs[owned : owned + 1], 0.0)
    rows_ref[...] = rows
    rounded = rows.astype(BF)
    low = jnp.sum(jnp.where(on, rows - rounded.astype(F32), 0.0), axis=0, keepdims=True)
    at = lax.broadcasted_iota(jnp.int32, (owned, owned), 0)
    pick = natural(at, parity, half) == lax.broadcasted_iota(jnp.int32, (owned, owned), 1)
    ordered = dot(jnp.where(pick, 1.0, 0.0).astype(BF), rounded).astype(BF)
    message_ref[:half] = ordered[:half]
    message_ref[half : half + half // 2] = jnp.concatenate(
        [ordered[half : half + half // 2, PW // 2 :], ordered[half + half // 2 :, PW // 2 :]], axis=1
    )
    message_ref[half + half // 2 :] = jnp.broadcast_to(low, (LOW_ROWS, PW)).astype(BF)


def product_kernel(panel_ref, q_ref, *outs):
    owners = panel_ref.shape[0]
    lanes = q_ref.shape[0] // CHUNKS
    q = q_ref[...]

    def first(s, carry):
        product = dot(panel_ref[s], q, NT)
        for c in range(CHUNKS):
            outs[c][s] = product[:, c * lanes : (c + 1) * lanes]
        return carry

    lax.fori_loop(0, owners, first, 0, unroll=8)


def owner_kernel(owners, slots, owned, recv_ref, product_ref, slot_ref, target_ref, own_ref, other_ref, y_ref):
    width, lanes = recv_ref.shape[1:]
    part = owners * slots // 2
    numbers = row_numbers(part, width)

    def first(s, carry):
        contrib = (recv_ref[s].astype(F32) - product_ref[s]).astype(BF)
        for b in range(2):
            y = dot(hot(numbers, slot_ref[b, pl.ds(s, 1), :]), contrib).astype(BF)
            y_ref[pl.ds(b * (owners // 2), owners // 2), pl.ds(pl.multiple_of(s * slots, 16), slots), :] = y.reshape(
                owners // 2, slots, lanes
            )
        return carry

    lax.fori_loop(0, owners, first, 0, unroll=OWNER_UNROLL)
    half = owned // 2
    spots = row_numbers(owned, owners * slots)

    def second(owner, carry):
        z = dot(hot(spots, target_ref[pl.ds(owner, 1), :]), y_ref[owner]).astype(BF)
        own_ref[owner] = z[:half]
        other_ref[owner] = z[half:]
        return carry

    lax.fori_loop(0, owners, second, 0, unroll=OWNER_UNROLL)


def split(x):
    hi = x.astype(BF)
    return hi, (x - hi.astype(F32)).astype(BF)


def dot3(a, b, dims=NN):
    return dot(a[0], b[0], dims) + (dot(a[0], b[1], dims) + dot(a[1], b[0], dims))


def natural(position, parity, half):
    return jnp.where(position < half, 2 * position + parity, 2 * (position - half) + 1 - parity)


def inverse_factor(parity, a, w_ref, s_ref, t_ref):
    n = a.shape[0]
    half = n // 2
    row_at = lax.broadcasted_iota(jnp.int32, (n, n), 0)
    col_at = lax.broadcasted_iota(jnp.int32, (n, n), 1)
    row_nat = natural(row_at, parity, half)
    col_nat = natural(col_at, parity, half)
    on = row_at == col_at
    a = jnp.where(row_nat >= col_nat, a, a.T)
    phi = jnp.where(on, 0.5, jnp.where(row_nat > col_nat, 1.0, 0.0))
    unit = jnp.where(on, 1.0, 0.0)
    diagonal = jnp.where(on, a, 0.0)
    scale_row = lax.rsqrt(jnp.sum(diagonal, axis=0, keepdims=True))
    scale_col = lax.rsqrt(jnp.sum(diagonal, axis=1, keepdims=True))
    scaled = a * scale_row * scale_col
    s_ref[...] = scaled
    w_ref[...] = unit - phi * (scaled - unit)
    s_parts = split(scaled)

    def step(state):
        count, _ = state
        w = w_ref[...]
        w_parts = split(w)
        m_parts = split(dot3(w_parts, s_parts))
        e = dot3(m_parts, w_parts, NT) - unit
        w_ref[...] = w - dot3(split(phi * e), w_parts)
        return count + 1, jnp.sum(e * e)

    def more(state):
        count, size = state
        return jnp.logical_and(count < 16, jnp.logical_not(size < 1e-6))

    _, size = lax.while_loop(more, step, (jnp.int32(0), jnp.float32(1.0)))

    @pl.when(jnp.logical_not(size < 1e-6))
    def _():
        lane = lax.broadcasted_iota(jnp.int32, (1, n), 1)
        lane_nat = natural(lane, parity, half)

        def place(j):
            return jnp.where((j & 1) == parity, j >> 1, half + (j >> 1))

        def column(j, carry):
            p = place(j)
            row = jnp.where(lane_nat >= j, s_ref[pl.ds(p, 1), :], 0.0)
            pivot = jnp.sum(jnp.where(lane == p, row, 0.0))
            row = row * lax.rsqrt(jnp.full((1, n), pivot))
            t_ref[pl.ds(p, 1), :] = row
            col = jnp.sum(jnp.where(on, row, 0.0), axis=1, keepdims=True)
            s_ref[...] = s_ref[...] - col * row
            return carry

        lax.fori_loop(0, n, column, 0)
        w_ref[...] = jnp.zeros_like(w_ref)

        def solve(j, carry):
            p = place(j)
            col = jnp.sum(jnp.where(col_at == p, t_ref[...], 0.0), axis=1, keepdims=True)
            known = jnp.sum(col * w_ref[...], axis=0, keepdims=True)
            pivot = jnp.sum(jnp.where(lane == p, t_ref[pl.ds(p, 1), :], 0.0))
            w_ref[pl.ds(p, 1), :] = (jnp.where(lane == p, 1.0, 0.0) - known) / pivot
            return carry

        lax.fori_loop(0, n, solve, 0)

    return w_ref[...] * scale_row


def factor_kernel(parity_ref, rows_ref, front_hbm, parent_hbm, *refs):
    own_hbm, recv_hbm = refs[:CHUNKS], refs[CHUNKS : 2 * CHUNKS]
    schur_ref, panel_ref, w_ref, s_ref, t_ref, lead_ref, cols_ref, parent_ref = refs[2 * CHUNKS : 2 * CHUNKS + 8]
    own_ref, recv_ref, sems = refs[2 * CHUNKS + 8 :]
    owned = rows_ref.shape[0]
    half = owned // 2
    strips = parent_ref.shape[0] // owned
    high = lax.Precision.HIGHEST
    copies = [
        pltpu.make_async_copy(front_hbm.at[pl.ds(0, 2)], lead_ref, sems.at[0]),
        pltpu.make_async_copy(front_hbm.at[:, pl.ds(0, half), :], cols_ref, sems.at[1]),
        pltpu.make_async_copy(parent_hbm, parent_ref, sems.at[2]),
    ]
    for c in range(CHUNKS):
        copies.append(pltpu.make_async_copy(own_hbm[c], own_ref.at[c], sems.at[3 + c]))
    for c in range(CHUNKS):
        copies.append(pltpu.make_async_copy(recv_hbm[c], recv_ref.at[c], sems.at[3 + CHUNKS + c]))
    for copy in copies:
        copy.start()
    copies[0].wait()
    top = jnp.concatenate([lead_ref[0, :half], lead_ref[1, :half]], axis=0).astype(F32)
    fold = lead_ref[:, half : half + half // 2].astype(F32)
    corner = jnp.concatenate([fold[b, :, i : i + owned] for b in range(2) for i in (0, owned)], axis=0)
    low = lead_ref[:, half + half // 2 : half + half // 2 + 1].astype(F32)
    bottom = jnp.concatenate([top[:, owned:].T, corner], axis=1)
    pivot = jnp.concatenate([top, bottom], axis=0) + eye(PW) * (low[0] + low[1])
    lead_cols = split(pivot[: PW // 2])
    w = inverse_factor(parity_ref[0], pivot, w_ref, s_ref, t_ref)
    w_ref[...] = w
    factor = dot(rows_ref[...], w, NT, high)
    panel_ref[...] = factor[:, : panel_ref.shape[1]]
    g_hi, g_lo = split(dot(factor, w_ref[...], NN, high))
    for copy in copies[1:]:
        copy.wait()
    lanes = owned // CHUNKS
    unit = eye(lanes, BF)
    for pair in range(strips // 2):
        cols = cols_ref[pl.ds(2 * pair, 2)].reshape(2 * half, PW)
        if pair == 0:
            update = dot3((g_hi, g_lo), lead_cols, NT)
        else:
            update = dot(g_hi, cols, NT) + dot(g_lo, cols, NT)
        placed = []
        for c in range(CHUNKS):
            z = dot(unit, own_ref[c, pl.ds(2 * pair, 2)].reshape(2 * half, lanes), NT)
            placed.append(z + dot(unit, recv_ref[c, pl.ds(2 * pair, 2)].reshape(2 * half, lanes), NT))
        change = jnp.concatenate(placed, axis=0) - update
        for side in range(2):
            at = pl.ds(2 * pair + side, owned, stride=strips)
            schur_ref[at, :] = parent_ref[at, :] + change[:, side * half : (side + 1) * half]


def swapped(block):
    count = lax.axis_size("cube")
    return lax.ppermute(block, "cube", [(i, i ^ 1) for i in range(count)])


def exchanged(block):
    return lax.all_to_all(block, "grid", 0, 0, tiled=True)


def shards(parent_front, child_block, child_panel, row_map):
    owners = lax.axis_size("grid")
    cube_pos = lax.axis_index("cube")
    grid_pos = lax.axis_index("grid")
    parity = cube_pos % 2
    width = child_block.shape[1]
    owned = parent_front.shape[0]
    half_cols = parent_front.shape[2]
    capacity = 2 * width // owners
    slots = -(-capacity // 16) * 16
    total = owners * slots
    half = owned // 2
    lanes = owned // CHUNKS
    own_panel = child_panel[0]
    panel_all = lax.all_gather(own_panel, "grid")

    row_of = lax.dynamic_index_in_dim(row_map, cube_pos, 0, keepdims=False).reshape(owners, width)
    owner_of = row_of // owned
    local_of = row_of % owned
    earlier = lax.iota(jnp.int32, width)[:, None] < lax.iota(jnp.int32, width)[None, :]
    same = (owner_of[:, :, None] == owner_of[:, None, :]) & earlier[None]
    rank_of = jnp.sum(same.astype(jnp.int32), axis=1)
    slot_of = owner_of * slots + rank_of
    hits = slot_of[:, :, None] == lax.iota(jnp.int32, total)[None, None, :]
    target = jnp.sum(jnp.where(hits, local_of[:, :, None] + 1, 0), axis=1) - 1
    target = target.reshape(owners, owners, slots).transpose(1, 0, 2)
    target_nat = target.reshape(owners, total)
    target_own = jnp.where(
        target_nat >= 0, ((target_nat & 1) ^ parity) * half + (target_nat >> 1), -1
    ).astype(F32)
    slot_parts = slot_of[None] - jnp.array([0, total // 2])[:, None, None]
    slot_parts = jnp.where((slot_parts >= 0) & (slot_parts < total // 2), slot_parts, -1).astype(F32)
    my_slot = lax.dynamic_index_in_dim(slot_of, grid_pos, 0, keepdims=False)

    row_flat = row_of.reshape(-1)
    pan_of = jnp.where(row_flat < PW, ((row_flat & 1) ^ parity) * (PW // 2) + (row_flat >> 1), -1)
    block_pan = dot(child_block[0], (pan_of[:, None] == lax.iota(jnp.int32, PW)[None, :]).astype(BF)).astype(BF)

    pack = (lax.iota(jnp.int32, total)[:, None] == my_slot[None, :]).astype(BF)
    packed = dot(pack, block_pan).astype(BF).reshape(owners, slots, PW)
    packed, slot_parts = lax.optimization_barrier((packed, slot_parts))
    packed = exchanged(packed)
    spread = call(
        functools.partial(source_kernel, owners, slots, owned),
        [jax.ShapeDtypeStruct((owners, width, lanes), BF)] * CHUNKS,
        [pltpu.VMEM((owners, total, width), BF)],
        flops=6 * owners * total * width * width,
    )(child_block[0], slot_parts, target_nat.astype(F32))
    packed, spread = lax.optimization_barrier((packed, spread))
    bulk = [exchanged(spread[0])]

    smem, vmem = pl.BlockSpec(memory_space=pltpu.SMEM), pl.BlockSpec(memory_space=pltpu.VMEM)
    place = jnp.stack([parity, grid_pos]).astype(jnp.int32)
    here = slot_of - grid_pos * slots
    here = jnp.where((here >= 0) & (here < slots), here, -1).astype(F32)
    my_target = lax.dynamic_slice_in_dim(target_nat, grid_pos, 1).astype(F32)
    rows_mine, message, q = call(
        functools.partial(panel_kernel, owners, slots),
        [
            jax.ShapeDtypeStruct((owned, PW), F32),
            jax.ShapeDtypeStruct((owned + LOW_ROWS, PW), BF),
            jax.ShapeDtypeStruct((owned, PW), BF),
        ],
        [pltpu.VMEM((3, total, PW), BF)],
        flops=4 * owners * width * owned * PW,
        in_specs=[smem] + [vmem] * 7,
    )(place, panel_all, here, slot_parts, target_own, my_target, packed.reshape(total, PW), parent_front[:, 0, : PW // 2])
    product = call(
        product_kernel,
        [jax.ShapeDtypeStruct((owners, width, lanes), F32)] * CHUNKS,
        flops=4 * owners * width * owned * PW,
    )(panel_all, q)
    theirs, bulk[0], product = lax.optimization_barrier((swapped(message), bulk[0], product))
    rest, product = lax.optimization_barrier((spread[1:], product))
    bulk = bulk + [exchanged(part) for part in rest]
    rows, message = call(
        rows_kernel,
        [
            jax.ShapeDtypeStruct((owned, PW), F32),
            jax.ShapeDtypeStruct((half + half // 2 + LOW_ROWS, PW), BF),
        ],
        in_specs=[smem, vmem, vmem],
    )(place, rows_mine, theirs)
    front_cols = lax.all_gather(message, "grid")

    own_t, other_t = [], []
    for c in range(CHUNKS):
        a, b = call(
            functools.partial(owner_kernel, owners, slots, owned),
            [jax.ShapeDtypeStruct((owners, half, lanes), BF)] * 2,
            [pltpu.VMEM((owners, total, lanes), BF)],
            flops=8 * owners * total * width * lanes,
        )(bulk[c], product[c], slot_parts, target_own)
        own_t.append(a)
        other_t.append(b)
    recv_t = [swapped(x) for x in other_t]

    strips = half_cols // 128
    anywhere = pl.BlockSpec(memory_space=pl.ANY)
    schur, panel = call(
        factor_kernel,
        [
            jax.ShapeDtypeStruct((owned * strips, 128), F32),
            jax.ShapeDtypeStruct((owned, PW // 2), F32),
        ],
        [
            pltpu.VMEM((PW, PW), F32),
            pltpu.VMEM((PW, PW), F32),
            pltpu.VMEM((PW, PW), F32),
            pltpu.VMEM((2, half + half // 2 + LOW_ROWS, PW), BF),
            pltpu.VMEM((owners, half, PW), BF),
            pltpu.VMEM((owned * strips, 128), F32),
            pltpu.VMEM((CHUNKS, owners, half, lanes), BF),
            pltpu.VMEM((CHUNKS, owners, half, lanes), BF),
            pltpu.SemaphoreType.DMA((3 + 2 * CHUNKS,)),
        ],
        flops=60 * PW**3,
        in_specs=[smem, vmem] + [anywhere] * (2 + 2 * CHUNKS),
        out_specs=[vmem, vmem],
    )(
        place,
        rows,
        front_cols,
        parent_front.reshape(owned * strips, 128),
        *own_t,
        *recv_t,
    )
    return (schur.reshape(owned, 1, half_cols), panel[:, None, :])


def solution(mesh):
    in_specs = (P("grid", "cube", None), P("cube", "grid", None), P("cube", "grid", None), P())
    out_specs = (P("grid", "cube", None), P("grid", "cube", None))
    return jax.shard_map(shards, mesh=mesh, in_specs=in_specs, out_specs=out_specs, check_vma=False)
```

```python
import functools

import jax
import jax.numpy as jnp
from jax import lax
from jax.experimental import pallas as pl
from jax.experimental.pallas import tpu as pltpu
from jax.sharding import PartitionSpec as P

PW = 512
CHUNKS = 2
LOW_ROWS = 16
SOURCE_UNROLL = 4
OWNER_UNROLL = 8
BF = jnp.bfloat16
F32 = jnp.float32
NN = (((1,), (0,)), ((), ()))
NT = (((1,), (1,)), ((), ()))
VMEM_LIMIT = 60 << 20


def dot(a, b, dims=NN, precision=None):
    return lax.dot_general(a, b, dims, precision=precision, preferred_element_type=F32)


def row_numbers(rows, n):
    return lax.broadcasted_iota(jnp.int32, (rows, n), 0).astype(F32).astype(BF)


def hot(numbers, row_vector):
    one, zero = jnp.ones((), BF), jnp.zeros((), BF)
    return jnp.where(numbers == row_vector.astype(BF), one, zero)


def eye(n, dtype=F32):
    r = lax.broadcasted_iota(jnp.int32, (n, n), 0)
    c = lax.broadcasted_iota(jnp.int32, (n, n), 1)
    return jnp.where(r == c, 1.0, 0.0).astype(dtype)


def call(kernel, out_shape, scratch=(), flops=0, **kw):
    moved = sum(x.size * x.dtype.itemsize for x in jax.tree.leaves(out_shape))
    return pl.pallas_call(
        kernel,
        out_shape=out_shape,
        scratch_shapes=list(scratch),
        cost_estimate=pl.CostEstimate(flops=flops, transcendentals=0, bytes_accessed=2 * moved),
        compiler_params=pltpu.CompilerParams(vmem_limit_bytes=VMEM_LIMIT),
        **kw,
    )


def source_kernel(owners, slots, owned, block_ref, slot_ref, target_ref, *refs):
    outs, y_ref = refs[:CHUNKS], refs[CHUNKS]
    width = block_ref.shape[0]
    part = owners * slots // 2
    numbers = row_numbers(part, width)

    def first(pair, carry):
        cols = block_ref[:, pl.ds(pl.multiple_of(pair * 2 * width, 128), 2 * width)]
        for side in range(2):
            s = pair * 2 + side
            mine = cols[:, side * width : (side + 1) * width]
            for b in range(2):
                pick = hot(numbers, slot_ref[b, pl.ds(s, 1), :])
                y = dot(pick, mine, NT).astype(BF).reshape(owners // 2, slots, width)
                y_ref[pl.ds(b * (owners // 2), owners // 2), pl.ds(pl.multiple_of(s * slots, 16), slots), :] = y
        return carry

    lax.fori_loop(0, owners // 2, first, 0, unroll=SOURCE_UNROLL)
    unit = eye(width, BF)
    spots = row_numbers(owned, owners * slots)
    lanes = owned // CHUNKS

    def second(owner, carry):
        turned = dot(hot(spots, target_ref[pl.ds(owner, 1), :]), y_ref[owner]).astype(BF)
        z = dot(unit, turned, NT).astype(BF)
        for c in range(CHUNKS):
            outs[c][owner] = z[:, c * lanes : (c + 1) * lanes]
        return carry

    lax.fori_loop(0, owners, second, 0, unroll=2 * SOURCE_UNROLL)


def panel_kernel(place_ref, received_ref, target_ref, parent_ref, rows_ref, message_ref, q_ref):
    parity, grid_pos = place_ref[0], place_ref[1]
    owned = q_ref.shape[0]

    def chosen(rows, kind):
        at = lax.broadcasted_iota(jnp.int32, (rows, target_ref.shape[1]), 0).astype(F32)
        pick = jnp.where(at == target_ref[kind : kind + 1, :], 1.0, 0.0).astype(BF)
        return dot(pick, received_ref[...])

    placed = chosen(owned, 0)
    q = chosen(owned, 1).astype(BF)
    pan = chosen(PW, 2).astype(BF)
    q_ref[...] = q
    contrib = (placed - dot(q, pan, NT)).astype(BF).astype(F32)
    rows = jnp.concatenate([contrib[:, :owned] + parent_ref[...], contrib[:, owned:]], axis=1)
    rows_ref[...] = rows
    rounded = rows.astype(BF)
    low = jnp.where(diagonal_at(grid_pos, parity, owned), rows - rounded.astype(F32), 0.0)
    message_ref[:owned] = rounded
    message_ref[owned:] = jnp.broadcast_to(jnp.sum(low, axis=0, keepdims=True), (LOW_ROWS, PW)).astype(BF)


def diagonal_at(grid_pos, parity, owned):
    row = lax.broadcasted_iota(jnp.int32, (owned, PW), 0) + grid_pos * owned
    return natural(lax.broadcasted_iota(jnp.int32, (owned, PW), 1), parity, PW // 2) == row


def rows_kernel(place_ref, mine_ref, theirs_ref, rows_ref, message_ref):
    parity, grid_pos = place_ref[0], place_ref[1]
    owned = mine_ref.shape[0]
    half = owned // 2
    theirs = theirs_ref[...].astype(F32)
    theirs = jnp.concatenate([theirs[:, PW // 2 :], theirs[:, : PW // 2]], axis=1)
    on = diagonal_at(grid_pos, parity, owned)
    rows = mine_ref[...] + theirs[:owned] + jnp.where(on, theirs[owned : owned + 1], 0.0)
    rows_ref[...] = rows
    rounded = rows.astype(BF)
    low = jnp.sum(jnp.where(on, rows - rounded.astype(F32), 0.0), axis=0, keepdims=True)
    at = lax.broadcasted_iota(jnp.int32, (owned, owned), 0)
    pick = natural(at, parity, half) == lax.broadcasted_iota(jnp.int32, (owned, owned), 1)
    ordered = dot(jnp.where(pick, 1.0, 0.0).astype(BF), rounded).astype(BF)
    message_ref[:half] = ordered[:half]
    message_ref[half : half + half // 2] = jnp.concatenate(
        [ordered[half : half + half // 2, PW // 2 :], ordered[half + half // 2 :, PW // 2 :]], axis=1
    )
    message_ref[half + half // 2 :] = jnp.broadcast_to(low, (LOW_ROWS, PW)).astype(BF)


def product_kernel(panel_ref, q_ref, *outs):
    owners = panel_ref.shape[0]
    lanes = q_ref.shape[0] // CHUNKS
    q = q_ref[...]

    def first(s, carry):
        product = dot(panel_ref[s], q, NT)
        for c in range(CHUNKS):
            outs[c][s] = product[:, c * lanes : (c + 1) * lanes]
        return carry

    lax.fori_loop(0, owners, first, 0, unroll=8)


def owner_kernel(owners, slots, owned, recv_ref, product_ref, slot_ref, target_ref, own_ref, other_ref, y_ref):
    width, lanes = recv_ref.shape[1:]
    part = owners * slots // 2
    numbers = row_numbers(part, width)

    def first(s, carry):
        contrib = (recv_ref[s].astype(F32) - product_ref[s]).astype(BF)
        for b in range(2):
            y = dot(hot(numbers, slot_ref[b, pl.ds(s, 1), :]), contrib).astype(BF)
            y_ref[pl.ds(b * (owners // 2), owners // 2), pl.ds(pl.multiple_of(s * slots, 16), slots), :] = y.reshape(
                owners // 2, slots, lanes
            )
        return carry

    lax.fori_loop(0, owners, first, 0, unroll=OWNER_UNROLL)
    half = owned // 2
    spots = row_numbers(owned, owners * slots)

    def second(owner, carry):
        z = dot(hot(spots, target_ref[pl.ds(owner, 1), :]), y_ref[owner]).astype(BF)
        own_ref[owner] = z[:half]
        other_ref[owner] = z[half:]
        return carry

    lax.fori_loop(0, owners, second, 0, unroll=OWNER_UNROLL)


def split(x):
    hi = x.astype(BF)
    return hi, (x - hi.astype(F32)).astype(BF)


def dot3(a, b, dims=NN):
    return dot(a[0], b[0], dims) + (dot(a[0], b[1], dims) + dot(a[1], b[0], dims))


def natural(position, parity, half):
    return jnp.where(position < half, 2 * position + parity, 2 * (position - half) + 1 - parity)


def inverse_factor(parity, a, w_ref, s_ref, t_ref):
    n = a.shape[0]
    half = n // 2
    row_at = lax.broadcasted_iota(jnp.int32, (n, n), 0)
    col_at = lax.broadcasted_iota(jnp.int32, (n, n), 1)
    row_nat = natural(row_at, parity, half)
    col_nat = natural(col_at, parity, half)
    on = row_at == col_at
    a = jnp.where(row_nat >= col_nat, a, a.T)
    phi = jnp.where(on, 0.5, jnp.where(row_nat > col_nat, 1.0, 0.0))
    unit = jnp.where(on, 1.0, 0.0)
    diagonal = jnp.where(on, a, 0.0)
    scale_row = lax.rsqrt(jnp.sum(diagonal, axis=0, keepdims=True))
    scale_col = lax.rsqrt(jnp.sum(diagonal, axis=1, keepdims=True))
    scaled = a * scale_row * scale_col
    s_ref[...] = scaled
    w_ref[...] = unit - phi * (scaled - unit)
    s_parts = split(scaled)

    def step(state):
        count, _ = state
        w = w_ref[...]
        w_parts = split(w)
        m_parts = split(dot3(w_parts, s_parts))
        e = dot3(m_parts, w_parts, NT) - unit
        w_ref[...] = w - dot3(split(phi * e), w_parts)
        return count + 1, jnp.sum(e * e)

    def more(state):
        count, size = state
        return jnp.logical_and(count < 16, jnp.logical_not(size < 1e-6))

    _, size = lax.while_loop(more, step, (jnp.int32(0), jnp.float32(1.0)))

    @pl.when(jnp.logical_not(size < 1e-6))
    def _():
        lane = lax.broadcasted_iota(jnp.int32, (1, n), 1)
        lane_nat = natural(lane, parity, half)

        def place(j):
            return jnp.where((j & 1) == parity, j >> 1, half + (j >> 1))

        def column(j, carry):
            p = place(j)
            row = jnp.where(lane_nat >= j, s_ref[pl.ds(p, 1), :], 0.0)
            pivot = jnp.sum(jnp.where(lane == p, row, 0.0))
            row = row * lax.rsqrt(jnp.full((1, n), pivot))
            t_ref[pl.ds(p, 1), :] = row
            col = jnp.sum(jnp.where(on, row, 0.0), axis=1, keepdims=True)
            s_ref[...] = s_ref[...] - col * row
            return carry

        lax.fori_loop(0, n, column, 0)
        w_ref[...] = jnp.zeros_like(w_ref)

        def solve(j, carry):
            p = place(j)
            col = jnp.sum(jnp.where(col_at == p, t_ref[...], 0.0), axis=1, keepdims=True)
            known = jnp.sum(col * w_ref[...], axis=0, keepdims=True)
            pivot = jnp.sum(jnp.where(lane == p, t_ref[pl.ds(p, 1), :], 0.0))
            w_ref[pl.ds(p, 1), :] = (jnp.where(lane == p, 1.0, 0.0) - known) / pivot
            return carry

        lax.fori_loop(0, n, solve, 0)

    return w_ref[...] * scale_row


def factor_kernel(parity_ref, rows_ref, front_hbm, parent_hbm, *refs):
    own_hbm, recv_hbm = refs[:CHUNKS], refs[CHUNKS : 2 * CHUNKS - 1]
    schur_ref, panel_ref, w_ref, s_ref, t_ref, lead_ref, cols_ref, parent_ref = refs[2 * CHUNKS - 1 : 2 * CHUNKS + 7]
    own_ref, recv_ref, sems = refs[2 * CHUNKS + 7 :]
    owned = rows_ref.shape[0]
    half = owned // 2
    strips = parent_ref.shape[0] // owned
    high = lax.Precision.HIGHEST
    copies = [
        pltpu.make_async_copy(front_hbm.at[pl.ds(0, 2)], lead_ref, sems.at[0]),
        pltpu.make_async_copy(front_hbm.at[:, pl.ds(0, half), :], cols_ref, sems.at[1]),
        pltpu.make_async_copy(parent_hbm, parent_ref, sems.at[2]),
    ]
    for c in range(CHUNKS):
        copies.append(pltpu.make_async_copy(own_hbm[c], own_ref.at[c], sems.at[3 + c]))
    for c in range(CHUNKS - 1):
        copies.append(pltpu.make_async_copy(recv_hbm[c], recv_ref.at[c], sems.at[3 + CHUNKS + c]))
    for copy in copies:
        copy.start()
    copies[0].wait()
    top = jnp.concatenate([lead_ref[0, :half], lead_ref[1, :half]], axis=0).astype(F32)
    fold = lead_ref[:, half : half + half // 2].astype(F32)
    corner = jnp.concatenate([fold[b, :, i : i + owned] for b in range(2) for i in (0, owned)], axis=0)
    low = lead_ref[:, half + half // 2 : half + half // 2 + 1].astype(F32)
    bottom = jnp.concatenate([top[:, owned:].T, corner], axis=1)
    pivot = jnp.concatenate([top, bottom], axis=0) + eye(PW) * (low[0] + low[1])
    lead_cols = split(pivot[: PW // 2])
    w = inverse_factor(parity_ref[0], pivot, w_ref, s_ref, t_ref)
    w_ref[...] = w
    factor = dot(rows_ref[...], w, NT, high)
    panel_ref[...] = factor[:, : panel_ref.shape[1]]
    g_hi, g_lo = split(dot(factor, w_ref[...], NN, high))
    for copy in copies[1:]:
        copy.wait()
    lanes = owned // CHUNKS
    unit = eye(lanes, BF)
    for pair in range(strips // 2):
        cols = cols_ref[pl.ds(2 * pair, 2)].reshape(2 * half, PW)
        if pair == 0:
            update = dot3((g_hi, g_lo), lead_cols, NT)
        else:
            update = dot(g_hi, cols, NT) + dot(g_lo, cols, NT)
        placed = []
        for c in range(CHUNKS):
            z = dot(unit, own_ref[c, pl.ds(2 * pair, 2)].reshape(2 * half, lanes), NT)
            if c < CHUNKS - 1:
                z = z + dot(unit, recv_ref[c, pl.ds(2 * pair, 2)].reshape(2 * half, lanes), NT)
            placed.append(z)
        change = jnp.concatenate(placed, axis=0) - update
        for side in range(2):
            at = pl.ds(2 * pair + side, owned, stride=strips)
            schur_ref[at, :] = parent_ref[at, :] + change[:, side * half : (side + 1) * half]


def last_kernel(schur_ref, recv_ref, out_ref):
    rows = pl.program_id(0)
    lanes = recv_ref.shape[2]
    strips = recv_ref.shape[0]
    part = schur_ref.shape[0] // strips
    r = lax.broadcasted_iota(jnp.int32, (part, lanes), 0) + rows * part
    c = lax.broadcasted_iota(jnp.int32, (part, lanes), 1)
    unit = jnp.where(r == c, 1.0, 0.0).astype(BF)
    for pair in range(strips // 2):
        z = dot(unit, recv_ref[pl.ds(2 * pair, 2)].reshape(-1, lanes), NT)
        for side in range(2):
            at = pl.ds(2 * pair + side, part, stride=strips)
            out_ref[at, :] = schur_ref[at, :] + z[:, side * 128 : (side + 1) * 128]


def swapped(block):
    count = lax.axis_size("cube")
    return lax.ppermute(block, "cube", [(i, i ^ 1) for i in range(count)])


def exchanged(block):
    return lax.all_to_all(block, "grid", 0, 0, tiled=True)


def shards(parent_front, child_block, child_panel, row_map):
    owners = lax.axis_size("grid")
    cube_pos = lax.axis_index("cube")
    grid_pos = lax.axis_index("grid")
    parity = cube_pos % 2
    width = child_block.shape[1]
    owned = parent_front.shape[0]
    half_cols = parent_front.shape[2]
    capacity = 2 * width // owners
    slots = -(-capacity // 16) * 16
    total = owners * slots
    half = owned // 2
    lanes = owned // CHUNKS
    own_panel = child_panel[0]
    panel_all = lax.all_gather(own_panel, "grid")

    row_of = lax.dynamic_index_in_dim(row_map, cube_pos, 0, keepdims=False).reshape(owners, width)
    owner_of = row_of // owned
    local_of = row_of % owned
    earlier = lax.iota(jnp.int32, width)[:, None] < lax.iota(jnp.int32, width)[None, :]
    same = (owner_of[:, :, None] == owner_of[:, None, :]) & earlier[None]
    rank_of = jnp.sum(same.astype(jnp.int32), axis=1)
    slot_of = owner_of * slots + rank_of
    hits = slot_of[:, :, None] == lax.iota(jnp.int32, total)[None, None, :]
    target = jnp.sum(jnp.where(hits, local_of[:, :, None] + 1, 0), axis=1) - 1
    target = target.reshape(owners, owners, slots).transpose(1, 0, 2)
    target_nat = target.reshape(owners, total)
    target_own = jnp.where(
        target_nat >= 0, ((target_nat & 1) ^ parity) * half + (target_nat >> 1), -1
    ).astype(F32)
    slot_parts = slot_of[None] - jnp.array([0, total // 2])[:, None, None]
    slot_parts = jnp.where((slot_parts >= 0) & (slot_parts < total // 2), slot_parts, -1).astype(F32)

    row_flat = row_of.reshape(-1)
    pan_of = jnp.where(row_flat < PW, ((row_flat & 1) ^ parity) * (PW // 2) + (row_flat >> 1), -1)
    block_pan = dot(child_block[0], (pan_of[:, None] == lax.iota(jnp.int32, PW)[None, :]).astype(BF)).astype(BF)

    my_owner = lax.dynamic_index_in_dim(owner_of, grid_pos, 0, keepdims=False)
    my_rank = lax.dynamic_index_in_dim(rank_of, grid_pos, 0, keepdims=False)
    kinds = 4 * capacity
    code = my_owner * kinds + my_rank
    pivot_code = jnp.where(my_owner < 2, (2 + my_owner) * capacity + my_rank, -1)
    never = jnp.full((width,), -1, jnp.int32)
    code = jnp.concatenate([code, code + capacity])
    pivot_code = jnp.concatenate([never, pivot_code])
    at = lax.iota(jnp.int32, owners * kinds)[:, None]
    pack = ((at == code[None, :]) | (at % kinds == pivot_code[None, :])).astype(BF)
    packed = dot(pack, jnp.concatenate([block_pan, own_panel], axis=0)).astype(BF).reshape(owners, kinds, PW)
    packed, slot_parts = lax.optimization_barrier((packed, slot_parts))
    packed = exchanged(packed)
    spread = call(
        functools.partial(source_kernel, owners, slots, owned),
        [jax.ShapeDtypeStruct((owners, width, lanes), BF)] * CHUNKS,
        [pltpu.VMEM((owners, total, width), BF)],
        flops=6 * owners * total * width * width,
    )(child_block[0], slot_parts, target_nat.astype(F32))
    packed, spread = lax.optimization_barrier((packed, spread))

    smem, vmem = pl.BlockSpec(memory_space=pltpu.SMEM), pl.BlockSpec(memory_space=pltpu.VMEM)
    place = jnp.stack([parity, grid_pos]).astype(jnp.int32)
    my_target = lax.dynamic_index_in_dim(target, grid_pos, 0, keepdims=False)[:, :capacity]
    pivot_target = target[:2, :, :capacity]
    pivot_pos = jnp.where(
        pivot_target >= 0,
        ((pivot_target & 1) ^ parity) * (PW // 2)
        + lax.iota(jnp.int32, 2)[:, None, None] * half
        + (pivot_target >> 1),
        -1,
    )
    pivot_pos = pivot_pos.transpose(1, 0, 2).reshape(owners, 2 * capacity)
    none = jnp.full((owners, capacity), -1, jnp.int32)
    kind_targets = jnp.stack(
        [
            jnp.concatenate([my_target, none, none, none], axis=1),
            jnp.concatenate([none, my_target, none, none], axis=1),
            jnp.concatenate([none, none, pivot_pos], axis=1),
        ]
    )
    kind_targets = kind_targets.reshape(3, owners * kinds).astype(F32)
    rows_mine, message, q = call(
        panel_kernel,
        [
            jax.ShapeDtypeStruct((owned, PW), F32),
            jax.ShapeDtypeStruct((owned + LOW_ROWS, PW), BF),
            jax.ShapeDtypeStruct((owned, PW), BF),
        ],
        flops=8 * owned * owners * kinds * PW,
        in_specs=[smem] + [vmem] * 3,
    )(place, packed.reshape(owners * kinds, PW), kind_targets, parent_front[:, 0, : PW // 2])
    theirs = swapped(message)
    bulk = [exchanged(spread[0])]
    rows, message = call(
        rows_kernel,
        [
            jax.ShapeDtypeStruct((owned, PW), F32),
            jax.ShapeDtypeStruct((half + half // 2 + LOW_ROWS, PW), BF),
        ],
        in_specs=[smem, vmem, vmem],
    )(place, rows_mine, theirs)
    front_cols = lax.all_gather(message, "grid")

    product = call(
        product_kernel,
        [jax.ShapeDtypeStruct((owners, width, lanes), F32)] * CHUNKS,
        flops=4 * owners * width * owned * PW,
    )(panel_all, q)
    rest, product = lax.optimization_barrier((spread[1:], product))
    bulk = bulk + [exchanged(part) for part in rest]

    own_t, other_t = [], []
    for c in range(CHUNKS):
        a, b = call(
            functools.partial(owner_kernel, owners, slots, owned),
            [jax.ShapeDtypeStruct((owners, half, lanes), BF)] * 2,
            [pltpu.VMEM((owners, total, lanes), BF)],
            flops=8 * owners * total * width * lanes,
        )(bulk[c], product[c], slot_parts, target_own)
        own_t.append(a)
        other_t.append(b)
    recv_t = [swapped(x) for x in other_t]

    strips = half_cols // 128
    anywhere = pl.BlockSpec(memory_space=pl.ANY)
    schur, panel = call(
        factor_kernel,
        [
            jax.ShapeDtypeStruct((owned * strips, 128), F32),
            jax.ShapeDtypeStruct((owned, PW // 2), F32),
        ],
        [
            pltpu.VMEM((PW, PW), F32),
            pltpu.VMEM((PW, PW), F32),
            pltpu.VMEM((PW, PW), F32),
            pltpu.VMEM((2, half + half // 2 + LOW_ROWS, PW), BF),
            pltpu.VMEM((owners, half, PW), BF),
            pltpu.VMEM((owned * strips, 128), F32),
            pltpu.VMEM((CHUNKS, owners, half, lanes), BF),
            pltpu.VMEM((CHUNKS - 1, owners, half, lanes), BF),
            pltpu.SemaphoreType.DMA((2 + 2 * CHUNKS,)),
        ],
        flops=60 * PW**3,
        in_specs=[smem, vmem] + [anywhere] * (1 + 2 * CHUNKS),
        out_specs=[vmem, vmem],
    )(
        place,
        rows,
        front_cols,
        parent_front.reshape(owned * strips, 128),
        *own_t,
        *recv_t[:-1],
    )
    steps = 4
    last_rows = pl.BlockSpec((lanes * strips // steps, 128), lambda i: ((CHUNKS - 1) * steps + i, 0))
    schur = call(
        last_kernel,
        jax.ShapeDtypeStruct((owned * strips, 128), F32),
        grid=(steps,),
        in_specs=[last_rows, pl.BlockSpec((owners, half, lanes), lambda i: (0, 0, 0))],
        out_specs=last_rows,
        input_output_aliases={0: 0},
    )(schur, recv_t[-1])
    return (schur.reshape(owned, 1, half_cols), panel[:, None, :])


def solution(mesh):
    in_specs = (P("grid", "cube", None), P("cube", "grid", None), P("cube", "grid", None), P())
    out_specs = (P("grid", "cube", None), P("grid", "cube", None))
    return jax.shard_map(shards, mesh=mesh, in_specs=in_specs, out_specs=out_specs, check_vma=False)
```

```python
import functools

import jax
import jax.numpy as jnp
from jax import lax
from jax.experimental import pallas as pl
from jax.experimental.pallas import tpu as pltpu
from jax.sharding import PartitionSpec as P

PW = 512
CHUNKS = 2
LOW_ROWS = 16
SOURCE_UNROLL = 4
OWNER_UNROLL = 8
OWNER_COST = 2500
BF = jnp.bfloat16
F32 = jnp.float32
NN = (((1,), (0,)), ((), ()))
NT = (((1,), (1,)), ((), ()))
VMEM_LIMIT = 60 << 20


def dot(a, b, dims=NN, precision=None):
    return lax.dot_general(a, b, dims, precision=precision, preferred_element_type=F32)


def row_numbers(rows, n):
    return lax.broadcasted_iota(jnp.int32, (rows, n), 0).astype(F32).astype(BF)


def hot(numbers, row_vector):
    one, zero = jnp.ones((), BF), jnp.zeros((), BF)
    return jnp.where(numbers == row_vector.astype(BF), one, zero)


def eye(n, dtype=F32):
    r = lax.broadcasted_iota(jnp.int32, (n, n), 0)
    c = lax.broadcasted_iota(jnp.int32, (n, n), 1)
    return jnp.where(r == c, 1.0, 0.0).astype(dtype)


def call(kernel, out_shape, scratch=(), flops=0, **kw):
    moved = sum(x.size * x.dtype.itemsize for x in jax.tree.leaves(out_shape))
    return pl.pallas_call(
        kernel,
        out_shape=out_shape,
        scratch_shapes=list(scratch),
        cost_estimate=pl.CostEstimate(flops=flops, transcendentals=0, bytes_accessed=2 * moved),
        compiler_params=pltpu.CompilerParams(vmem_limit_bytes=VMEM_LIMIT),
        **kw,
    )


def source_kernel(owners, slots, owned, block_ref, slot_ref, target_ref, *refs):
    outs, y_ref = refs[:CHUNKS], refs[CHUNKS]
    width = block_ref.shape[0]
    part = owners * slots // 2
    numbers = row_numbers(part, width)

    def first(pair, carry):
        cols = block_ref[:, pl.ds(pl.multiple_of(pair * 2 * width, 128), 2 * width)]
        for side in range(2):
            s = pair * 2 + side
            mine = cols[:, side * width : (side + 1) * width]
            for b in range(2):
                pick = hot(numbers, slot_ref[b, pl.ds(s, 1), :])
                y = dot(pick, mine, NT).astype(BF).reshape(owners // 2, slots, width)
                y_ref[pl.ds(b * (owners // 2), owners // 2), pl.ds(pl.multiple_of(s * slots, 16), slots), :] = y
        return carry

    lax.fori_loop(0, owners // 2, first, 0, unroll=SOURCE_UNROLL)
    unit = eye(width, BF)
    spots = row_numbers(owned, owners * slots)
    lanes = owned // CHUNKS

    def second(owner, carry):
        turned = dot(hot(spots, target_ref[pl.ds(owner, 1), :]), y_ref[owner]).astype(BF)
        z = dot(unit, turned, NT).astype(BF)
        for c in range(CHUNKS):
            outs[c][owner] = z[:, c * lanes : (c + 1) * lanes]
        return carry

    lax.fori_loop(0, owners, second, 0, unroll=2 * SOURCE_UNROLL)


def panel_kernel(place_ref, received_ref, target_ref, parent_ref, rows_ref, message_ref, q_ref):
    parity, grid_pos = place_ref[0], place_ref[1]
    owned = q_ref.shape[0]

    def chosen(rows, kind):
        at = lax.broadcasted_iota(jnp.int32, (rows, target_ref.shape[1]), 0).astype(F32)
        pick = jnp.where(at == target_ref[kind : kind + 1, :], 1.0, 0.0).astype(BF)
        return dot(pick, received_ref[...])

    placed = chosen(owned, 0)
    q = chosen(owned, 1).astype(BF)
    pan = chosen(PW, 2).astype(BF)
    q_ref[...] = q
    contrib = (placed - dot(q, pan, NT)).astype(BF).astype(F32)
    rows = jnp.concatenate([contrib[:, :owned] + parent_ref[...], contrib[:, owned:]], axis=1)
    rows_ref[...] = rows
    rounded = rows.astype(BF)
    low = jnp.where(diagonal_at(grid_pos, parity, owned), rows - rounded.astype(F32), 0.0)
    message_ref[:owned] = rounded
    message_ref[owned:] = jnp.broadcast_to(jnp.sum(low, axis=0, keepdims=True), (LOW_ROWS, PW)).astype(BF)


def diagonal_at(grid_pos, parity, owned):
    row = lax.broadcasted_iota(jnp.int32, (owned, PW), 0) + grid_pos * owned
    return natural(lax.broadcasted_iota(jnp.int32, (owned, PW), 1), parity, PW // 2) == row


def rows_kernel(place_ref, mine_ref, theirs_ref, rows_ref, message_ref):
    parity, grid_pos = place_ref[0], place_ref[1]
    owned = mine_ref.shape[0]
    half = owned // 2
    theirs = theirs_ref[...].astype(F32)
    theirs = jnp.concatenate([theirs[:, PW // 2 :], theirs[:, : PW // 2]], axis=1)
    on = diagonal_at(grid_pos, parity, owned)
    rows = mine_ref[...] + theirs[:owned] + jnp.where(on, theirs[owned : owned + 1], 0.0)
    rows_ref[...] = rows
    rounded = rows.astype(BF)
    low = jnp.sum(jnp.where(on, rows - rounded.astype(F32), 0.0), axis=0, keepdims=True)
    at = lax.broadcasted_iota(jnp.int32, (owned, owned), 0)
    pick = natural(at, parity, half) == lax.broadcasted_iota(jnp.int32, (owned, owned), 1)
    ordered = dot(jnp.where(pick, 1.0, 0.0).astype(BF), rounded).astype(BF)
    message_ref[:half] = ordered[:half]
    message_ref[half : half + half // 2] = jnp.concatenate(
        [ordered[half : half + half // 2, PW // 2 :], ordered[half + half // 2 :, PW // 2 :]], axis=1
    )
    message_ref[half + half // 2 :] = jnp.broadcast_to(low, (LOW_ROWS, PW)).astype(BF)


def product_kernel(panel_ref, q_ref, *outs):
    owners = panel_ref.shape[0]
    lanes = q_ref.shape[0] // CHUNKS
    q = q_ref[...]

    def first(s, carry):
        product = dot(panel_ref[s], q, NT)
        for c in range(CHUNKS):
            outs[c][s] = product[:, c * lanes : (c + 1) * lanes]
        return carry

    lax.fori_loop(0, owners, first, 0, unroll=8)


def owner_kernel(owners, slots, owned, recv_ref, product_ref, slot_ref, target_ref, own_ref, other_ref, y_ref):
    width, lanes = recv_ref.shape[1:]
    part = owners * slots // 2
    numbers = row_numbers(part, width)

    def first(s, carry):
        contrib = (recv_ref[s].astype(F32) - product_ref[s]).astype(BF)
        for b in range(2):
            y = dot(hot(numbers, slot_ref[b, pl.ds(s, 1), :]), contrib).astype(BF)
            y_ref[pl.ds(b * (owners // 2), owners // 2), pl.ds(pl.multiple_of(s * slots, 16), slots), :] = y.reshape(
                owners // 2, slots, lanes
            )
        return carry

    lax.fori_loop(0, owners, first, 0, unroll=OWNER_UNROLL)
    half = owned // 2
    spots = row_numbers(owned, owners * slots)

    def second(owner, carry):
        z = dot(hot(spots, target_ref[pl.ds(owner, 1), :]), y_ref[owner]).astype(BF)
        own_ref[owner] = z[:half]
        other_ref[owner] = z[half:]
        return carry

    lax.fori_loop(0, owners, second, 0, unroll=OWNER_UNROLL)


def split(x):
    hi = x.astype(BF)
    return hi, (x - hi.astype(F32)).astype(BF)


def dot3(a, b, dims=NN):
    return dot(a[0], b[0], dims) + (dot(a[0], b[1], dims) + dot(a[1], b[0], dims))


def natural(position, parity, half):
    return jnp.where(position < half, 2 * position + parity, 2 * (position - half) + 1 - parity)


def inverse_factor(parity, a, w_ref, s_ref, t_ref):
    n = a.shape[0]
    half = n // 2
    row_at = lax.broadcasted_iota(jnp.int32, (n, n), 0)
    col_at = lax.broadcasted_iota(jnp.int32, (n, n), 1)
    row_nat = natural(row_at, parity, half)
    col_nat = natural(col_at, parity, half)
    on = row_at == col_at
    a = jnp.where(row_nat >= col_nat, a, a.T)
    phi = jnp.where(on, 0.5, jnp.where(row_nat > col_nat, 1.0, 0.0))
    unit = jnp.where(on, 1.0, 0.0)
    diagonal = jnp.where(on, a, 0.0)
    scale_row = lax.rsqrt(jnp.sum(diagonal, axis=0, keepdims=True))
    scale_col = lax.rsqrt(jnp.sum(diagonal, axis=1, keepdims=True))
    scaled = a * scale_row * scale_col
    s_ref[...] = scaled
    w_ref[...] = unit - phi * (scaled - unit)
    s_parts = split(scaled)

    w = w_ref[...]
    w_hi = w.astype(BF)
    e = dot(dot(w_hi, s_parts[0]).astype(BF), w_hi, NT) - unit
    w_ref[...] = w - dot((phi * e).astype(BF), w_hi)

    def step(state):
        count, _ = state
        w = w_ref[...]
        w_parts = split(w)
        m_parts = split(dot3(w_parts, s_parts))
        e = dot3(m_parts, w_parts, NT) - unit
        w_ref[...] = w - dot3(split(phi * e), w_parts)
        return count + 1, jnp.sum(e * e)

    def more(state):
        count, size = state
        return jnp.logical_and(count < 16, jnp.logical_not(size < 1e-6))

    _, size = lax.while_loop(more, step, (jnp.int32(0), jnp.float32(1.0)))

    @pl.when(jnp.logical_not(size < 1e-6))
    def _():
        lane = lax.broadcasted_iota(jnp.int32, (1, n), 1)
        lane_nat = natural(lane, parity, half)

        def place(j):
            return jnp.where((j & 1) == parity, j >> 1, half + (j >> 1))

        def column(j, carry):
            p = place(j)
            row = jnp.where(lane_nat >= j, s_ref[pl.ds(p, 1), :], 0.0)
            pivot = jnp.sum(jnp.where(lane == p, row, 0.0))
            row = row * lax.rsqrt(jnp.full((1, n), pivot))
            t_ref[pl.ds(p, 1), :] = row
            col = jnp.sum(jnp.where(on, row, 0.0), axis=1, keepdims=True)
            s_ref[...] = s_ref[...] - col * row
            return carry

        lax.fori_loop(0, n, column, 0)
        w_ref[...] = jnp.zeros_like(w_ref)

        def solve(j, carry):
            p = place(j)
            col = jnp.sum(jnp.where(col_at == p, t_ref[...], 0.0), axis=1, keepdims=True)
            known = jnp.sum(col * w_ref[...], axis=0, keepdims=True)
            pivot = jnp.sum(jnp.where(lane == p, t_ref[pl.ds(p, 1), :], 0.0))
            w_ref[pl.ds(p, 1), :] = (jnp.where(lane == p, 1.0, 0.0) - known) / pivot
            return carry

        lax.fori_loop(0, n, solve, 0)

    return w_ref[...] * scale_row


def factor_kernel(place_ref, rows_ref, lead_ref, panel_ref, g_ref, pivot_ref, w_ref, s_ref, t_ref):
    owned = rows_ref.shape[0]
    half = owned // 2
    high = lax.Precision.HIGHEST
    top = jnp.concatenate([lead_ref[0, :half], lead_ref[1, :half]], axis=0).astype(F32)
    fold = lead_ref[:, half : half + half // 2].astype(F32)
    corner = jnp.concatenate([fold[b, :, i : i + owned] for b in range(2) for i in (0, owned)], axis=0)
    low = lead_ref[:, half + half // 2 : half + half // 2 + 1].astype(F32)
    bottom = jnp.concatenate([top[:, owned:].T, corner], axis=1)
    pivot = jnp.concatenate([top, bottom], axis=0) + eye(PW) * (low[0] + low[1])
    pivot_ref[0], pivot_ref[1] = split(pivot[: PW // 2])
    w = inverse_factor(place_ref[0], pivot, w_ref, s_ref, t_ref)
    w_ref[...] = w
    factor = dot(rows_ref[...], w, NT, high)
    panel_ref[...] = factor[:, : panel_ref.shape[1]]
    g_ref[0], g_ref[1] = split(dot(factor, w_ref[...], NN, high))


def update_kernel(g_ref, pivot_ref, cols_ref, parent_ref, own_ref, recv_ref, *refs):
    schur_ref = refs[-1]
    rows = g_ref.shape[1]
    strips, half, lanes = own_ref.shape
    both = jnp.concatenate([g_ref[0], g_ref[1]], axis=0)
    r = lax.broadcasted_iota(jnp.int32, (rows, lanes), 0) + pl.program_id(0) * rows
    c = lax.broadcasted_iota(jnp.int32, (rows, lanes), 1)
    unit = jnp.where(r == c, 1.0, 0.0).astype(BF)
    for pair in range(strips // 2):
        if pair == 0:
            update = dot(both, pivot_ref[0], NT)
            update = update[:rows] + update[rows:] + dot(g_ref[0], pivot_ref[1], NT)
        else:
            update = dot(both, cols_ref[pl.ds(2 * pair, 2)].reshape(2 * half, PW), NT)
            update = update[:rows] + update[rows:]
        own = own_ref[pl.ds(2 * pair, 2)].reshape(2 * half, lanes)
        recv = recv_ref[pl.ds(2 * pair, 2)].reshape(2 * half, lanes)
        change = dot(unit, own, NT) + dot(unit, recv, NT) - update
        for side in range(2):
            at = pl.ds(2 * pair + side, rows, stride=strips)
            schur_ref[at, :] = parent_ref[at, :] + change[:, side * half : (side + 1) * half]


def swapped(block):
    count = lax.axis_size("cube")
    return lax.ppermute(block, "cube", [(i, i ^ 1) for i in range(count)])


def exchanged(block):
    return lax.all_to_all(block, "grid", 0, 0, tiled=True)


def shards(parent_front, child_block, child_panel, row_map):
    owners = lax.axis_size("grid")
    cube_pos = lax.axis_index("cube")
    grid_pos = lax.axis_index("grid")
    parity = cube_pos % 2
    width = child_block.shape[1]
    owned = parent_front.shape[0]
    half_cols = parent_front.shape[2]
    capacity = 2 * width // owners
    slots = -(-capacity // 16) * 16
    total = owners * slots
    half = owned // 2
    lanes = owned // CHUNKS
    own_panel = child_panel[0]
    panel_all = lax.all_gather(own_panel, "grid")

    row_of = lax.dynamic_index_in_dim(row_map, cube_pos, 0, keepdims=False).reshape(owners, width)
    owner_of = row_of // owned
    local_of = row_of % owned
    earlier = lax.iota(jnp.int32, width)[:, None] < lax.iota(jnp.int32, width)[None, :]
    same = (owner_of[:, :, None] == owner_of[:, None, :]) & earlier[None]
    rank_of = jnp.sum(same.astype(jnp.int32), axis=1)
    slot_of = owner_of * slots + rank_of
    hits = slot_of[:, :, None] == lax.iota(jnp.int32, total)[None, None, :]
    target = jnp.sum(jnp.where(hits, local_of[:, :, None] + 1, 0), axis=1) - 1
    target = target.reshape(owners, owners, slots).transpose(1, 0, 2)
    target_nat = target.reshape(owners, total)
    target_own = jnp.where(
        target_nat >= 0, ((target_nat & 1) ^ parity) * half + (target_nat >> 1), -1
    ).astype(F32)
    slot_parts = slot_of[None] - jnp.array([0, total // 2])[:, None, None]
    slot_parts = jnp.where((slot_parts >= 0) & (slot_parts < total // 2), slot_parts, -1).astype(F32)

    row_flat = row_of.reshape(-1)
    pan_of = jnp.where(row_flat < PW, ((row_flat & 1) ^ parity) * (PW // 2) + (row_flat >> 1), -1)
    block_pan = dot(child_block[0], (pan_of[:, None] == lax.iota(jnp.int32, PW)[None, :]).astype(BF)).astype(BF)

    my_owner = lax.dynamic_index_in_dim(owner_of, grid_pos, 0, keepdims=False)
    my_rank = lax.dynamic_index_in_dim(rank_of, grid_pos, 0, keepdims=False)
    kinds = 4 * capacity
    code = my_owner * kinds + my_rank
    pivot_code = jnp.where(my_owner < 2, (2 + my_owner) * capacity + my_rank, -1)
    never = jnp.full((width,), -1, jnp.int32)
    code = jnp.concatenate([code, code + capacity])
    pivot_code = jnp.concatenate([never, pivot_code])
    at = lax.iota(jnp.int32, owners * kinds)[:, None]
    pack = ((at == code[None, :]) | (at % kinds == pivot_code[None, :])).astype(BF)
    packed = dot(pack, jnp.concatenate([block_pan, own_panel], axis=0)).astype(BF).reshape(owners, kinds, PW)
    packed, slot_parts = lax.optimization_barrier((packed, slot_parts))
    packed = exchanged(packed)
    spread = call(
        functools.partial(source_kernel, owners, slots, owned),
        [jax.ShapeDtypeStruct((owners, width, lanes), BF)] * CHUNKS,
        [pltpu.VMEM((owners, total, width), BF)],
        flops=6 * owners * total * width * width,
    )(child_block[0], slot_parts, target_nat.astype(F32))
    packed, spread = lax.optimization_barrier((packed, spread))

    smem, vmem = pl.BlockSpec(memory_space=pltpu.SMEM), pl.BlockSpec(memory_space=pltpu.VMEM)
    place = jnp.stack([parity, grid_pos]).astype(jnp.int32)
    my_target = lax.dynamic_index_in_dim(target, grid_pos, 0, keepdims=False)[:, :capacity]
    pivot_target = target[:2, :, :capacity]
    pivot_pos = jnp.where(
        pivot_target >= 0,
        ((pivot_target & 1) ^ parity) * (PW // 2)
        + lax.iota(jnp.int32, 2)[:, None, None] * half
        + (pivot_target >> 1),
        -1,
    )
    pivot_pos = pivot_pos.transpose(1, 0, 2).reshape(owners, 2 * capacity)
    none = jnp.full((owners, capacity), -1, jnp.int32)
    kind_targets = jnp.stack(
        [
            jnp.concatenate([my_target, none, none, none], axis=1),
            jnp.concatenate([none, my_target, none, none], axis=1),
            jnp.concatenate([none, none, pivot_pos], axis=1),
        ]
    )
    kind_targets = kind_targets.reshape(3, owners * kinds).astype(F32)
    rows_mine, message, q = call(
        panel_kernel,
        [
            jax.ShapeDtypeStruct((owned, PW), F32),
            jax.ShapeDtypeStruct((owned + LOW_ROWS, PW), BF),
            jax.ShapeDtypeStruct((owned, PW), BF),
        ],
        flops=8 * owned * owners * kinds * PW,
        in_specs=[smem] + [vmem] * 3,
    )(place, packed.reshape(owners * kinds, PW), kind_targets, parent_front[:, 0, : PW // 2])
    theirs = swapped(message)
    bulk = [exchanged(spread[0])]
    rows, message = call(
        rows_kernel,
        [
            jax.ShapeDtypeStruct((owned, PW), F32),
            jax.ShapeDtypeStruct((half + half // 2 + LOW_ROWS, PW), BF),
        ],
        in_specs=[smem, vmem, vmem],
    )(place, rows_mine, theirs)
    front_cols = lax.all_gather(message, "grid")

    product = call(
        product_kernel,
        [jax.ShapeDtypeStruct((owners, width, lanes), F32)] * CHUNKS,
        flops=4 * owners * width * owned * PW,
    )(panel_all, q)
    rest, product = lax.optimization_barrier((spread[1:], product))
    bulk = bulk + [exchanged(part) for part in rest]

    own_t, other_t = [], []
    for c in range(CHUNKS):
        a, b = call(
            functools.partial(owner_kernel, owners, slots, owned),
            [jax.ShapeDtypeStruct((owners, half, lanes), BF)] * 2,
            [pltpu.VMEM((owners, total, lanes), BF)],
            flops=OWNER_COST * owners * total * width * lanes,
        )(bulk[c], product[c], slot_parts, target_own)
        own_t.append(a)
        other_t.append(b)
    recv_t = [swapped(x) for x in other_t]

    strips = half_cols // 128
    lead_rows = half + half // 2 + LOW_ROWS
    square = pltpu.VMEM((PW, PW), F32)
    panel, g, pivot = call(
        factor_kernel,
        [
            jax.ShapeDtypeStruct((owned, PW // 2), F32),
            jax.ShapeDtypeStruct((2, owned, PW), BF),
            jax.ShapeDtypeStruct((2, PW // 2, PW), BF),
        ],
        [square, square, square],
        flops=60 * PW**3,
        grid=(1,),
        in_specs=[smem, pl.BlockSpec((owned, PW), lambda i: (0, 0)), pl.BlockSpec((2, lead_rows, PW), lambda i: (0, 0, 0))],
        out_specs=[
            pl.BlockSpec((owned, PW // 2), lambda i: (0, 0)),
            pl.BlockSpec((2, owned, PW), lambda i: (0, 0, 0)),
            pl.BlockSpec((2, PW // 2, PW), lambda i: (0, 0, 0)),
        ],
    )(place, rows, front_cols)
    parent_rows = parent_front.reshape(owned * strips, 128)
    steps = 2
    schur = []
    for c in range(CHUNKS):

        def part(i, c=c):
            return c * steps + i

        row_block = pl.BlockSpec((lanes * strips // steps, 128), lambda i: (part(i), 0))
        chunk_block = pl.BlockSpec((owners, half, lanes), lambda i: (0, 0, 0))
        schur = [
            call(
                update_kernel,
                jax.ShapeDtypeStruct((owned * strips, 128), F32),
                flops=16 * lanes * half_cols * PW,
                grid=(steps,),
                in_specs=[
                    pl.BlockSpec((2, lanes // steps, PW), lambda i: (0, part(i), 0)),
                    pl.BlockSpec((2, PW // 2, PW), lambda i: (0, 0, 0)),
                    pl.BlockSpec((owners, half, PW), lambda i: (0, 0, 0)),
                    row_block,
                    chunk_block,
                    chunk_block,
                ]
                + [pl.BlockSpec(memory_space=pl.ANY)] * len(schur),
                out_specs=row_block,
                input_output_aliases={6: 0} if schur else {},
            )(g, pivot, front_cols, parent_rows, own_t[c], recv_t[c], *schur)
        ]
    schur = schur[0]
    return (schur.reshape(owned, 1, half_cols), panel[:, None, :])


def solution(mesh):
    in_specs = (P("grid", "cube", None), P("cube", "grid", None), P("cube", "grid", None), P())
    out_specs = (P("grid", "cube", None), P("grid", "cube", None))
    return jax.shard_map(shards, mesh=mesh, in_specs=in_specs, out_specs=out_specs, check_vma=False)
```

```python
import functools

import jax
import jax.numpy as jnp
from jax import lax
from jax.experimental import pallas as pl
from jax.experimental.pallas import tpu as pltpu
from jax.sharding import PartitionSpec as P

PW = 512
CHUNKS = 2
LOW_ROWS = 16
SOURCE_UNROLL = 4
BF = jnp.bfloat16
F32 = jnp.float32
NN = (((1,), (0,)), ((), ()))
NT = (((1,), (1,)), ((), ()))
VMEM_LIMIT = 60 << 20


def dot(a, b, dims=NN, precision=None):
    return lax.dot_general(a, b, dims, precision=precision, preferred_element_type=F32)


def row_numbers(rows, n):
    return lax.broadcasted_iota(jnp.int32, (rows, n), 0).astype(F32).astype(BF)


def hot(numbers, row_vector):
    one, zero = jnp.ones((), BF), jnp.zeros((), BF)
    return jnp.where(numbers == row_vector.astype(BF), one, zero)


def eye(n, dtype=F32):
    r = lax.broadcasted_iota(jnp.int32, (n, n), 0)
    c = lax.broadcasted_iota(jnp.int32, (n, n), 1)
    return jnp.where(r == c, 1.0, 0.0).astype(dtype)


def call(kernel, out_shape, scratch=(), flops=0, **kw):
    moved = sum(x.size * x.dtype.itemsize for x in jax.tree.leaves(out_shape))
    return pl.pallas_call(
        kernel,
        out_shape=out_shape,
        scratch_shapes=list(scratch),
        cost_estimate=pl.CostEstimate(flops=flops, transcendentals=0, bytes_accessed=2 * moved),
        compiler_params=pltpu.CompilerParams(vmem_limit_bytes=VMEM_LIMIT),
        **kw,
    )


def source_kernel(owners, slots, owned, block_ref, slot_ref, target_ref, *refs):
    outs, y_ref = refs[:CHUNKS], refs[CHUNKS]
    width = block_ref.shape[0]
    part = owners * slots // 2
    numbers = row_numbers(part, width)

    def first(pair, carry):
        cols = block_ref[:, pl.ds(pl.multiple_of(pair * 2 * width, 128), 2 * width)]
        for side in range(2):
            s = pair * 2 + side
            mine = cols[:, side * width : (side + 1) * width]
            for b in range(2):
                pick = hot(numbers, slot_ref[b, pl.ds(s, 1), :])
                y = dot(pick, mine, NT).astype(BF).reshape(owners // 2, slots, width)
                y_ref[pl.ds(b * (owners // 2), owners // 2), pl.ds(pl.multiple_of(s * slots, 16), slots), :] = y
        return carry

    lax.fori_loop(0, owners // 2, first, 0, unroll=SOURCE_UNROLL)
    unit = eye(width, BF)
    spots = row_numbers(owned, owners * slots)
    lanes = owned // CHUNKS

    def second(owner, carry):
        turned = dot(hot(spots, target_ref[pl.ds(owner, 1), :]), y_ref[owner]).astype(BF)
        z = dot(unit, turned, NT).astype(BF)
        for c in range(CHUNKS):
            outs[c][owner] = z[:, c * lanes : (c + 1) * lanes]
        return carry

    lax.fori_loop(0, owners, second, 0, unroll=2 * SOURCE_UNROLL)


def panel_kernel(place_ref, received_ref, target_ref, parent_ref, rows_ref, message_ref, q_ref):
    parity, grid_pos = place_ref[0], place_ref[1]
    owned = q_ref.shape[0]

    def chosen(rows, kind):
        at = lax.broadcasted_iota(jnp.int32, (rows, target_ref.shape[1]), 0).astype(F32)
        pick = jnp.where(at == target_ref[kind : kind + 1, :], 1.0, 0.0).astype(BF)
        return dot(pick, received_ref[...])

    placed = chosen(owned, 0)
    q = chosen(owned, 1).astype(BF)
    pan = chosen(PW, 2).astype(BF)
    q_ref[...] = q
    contrib = (placed - dot(q, pan, NT)).astype(BF).astype(F32)
    rows = jnp.concatenate([contrib[:, :owned] + parent_ref[...], contrib[:, owned:]], axis=1)
    rows_ref[...] = rows
    rounded = rows.astype(BF)
    low = jnp.where(diagonal_at(grid_pos, parity, owned), rows - rounded.astype(F32), 0.0)
    message_ref[:owned] = rounded
    message_ref[owned:] = jnp.broadcast_to(jnp.sum(low, axis=0, keepdims=True), (LOW_ROWS, PW)).astype(BF)


def diagonal_at(grid_pos, parity, owned):
    row = lax.broadcasted_iota(jnp.int32, (owned, PW), 0) + grid_pos * owned
    return natural(lax.broadcasted_iota(jnp.int32, (owned, PW), 1), parity, PW // 2) == row


def rows_kernel(place_ref, mine_ref, theirs_ref, rows_ref, message_ref):
    parity, grid_pos = place_ref[0], place_ref[1]
    owned = mine_ref.shape[0]
    half = owned // 2
    theirs = theirs_ref[...].astype(F32)
    theirs = jnp.concatenate([theirs[:, PW // 2 :], theirs[:, : PW // 2]], axis=1)
    on = diagonal_at(grid_pos, parity, owned)
    rows = mine_ref[...] + theirs[:owned] + jnp.where(on, theirs[owned : owned + 1], 0.0)
    rows_ref[...] = rows
    rounded = rows.astype(BF)
    low = jnp.sum(jnp.where(on, rows - rounded.astype(F32), 0.0), axis=0, keepdims=True)
    at = lax.broadcasted_iota(jnp.int32, (owned, owned), 0)
    pick = natural(at, parity, half) == lax.broadcasted_iota(jnp.int32, (owned, owned), 1)
    ordered = dot(jnp.where(pick, 1.0, 0.0).astype(BF), rounded).astype(BF)
    message_ref[:half] = ordered[:half]
    message_ref[half : half + half // 2] = jnp.concatenate(
        [ordered[half : half + half // 2, PW // 2 :], ordered[half + half // 2 :, PW // 2 :]], axis=1
    )
    message_ref[half + half // 2 :] = jnp.broadcast_to(low, (LOW_ROWS, PW)).astype(BF)


def product_kernel(panel_ref, q_ref, *outs):
    lanes = q_ref.shape[0] // CHUNKS
    q = q_ref[...]
    for s in range(panel_ref.shape[0]):
        product = dot(panel_ref[s], q, NT)
        for c in range(CHUNKS):
            outs[c][s] = product[:, c * lanes : (c + 1) * lanes]


def owner_kernel(owners, slots, owned, recv_ref, product_ref, slot_ref, target_ref, own_ref, other_ref, y_ref):
    group, width, lanes = recv_ref.shape
    part = owners * slots // 2
    half = owned // 2
    phases = owners // group
    at = pl.program_id(0)

    @pl.when(at < phases)
    def _():
        numbers = row_numbers(part, width)
        for i in range(group):
            s = at * group + i
            contrib = (recv_ref[i].astype(F32) - product_ref[i]).astype(BF)
            for b in range(2):
                y = dot(hot(numbers, slot_ref[b, pl.ds(s, 1), :]), contrib).astype(BF)
                y_ref[pl.ds(b * (owners // 2), owners // 2), pl.ds(pl.multiple_of(s * slots, 16), slots), :] = y.reshape(
                    owners // 2, slots, lanes
                )

    @pl.when(at >= phases)
    def _():
        spots = row_numbers(owned, owners * slots)
        for i in range(group):
            owner = (at - phases) * group + i
            z = dot(hot(spots, target_ref[pl.ds(owner, 1), :]), y_ref[owner]).astype(BF)
            own_ref[i] = z[:half]
            other_ref[i] = z[half:]


def split(x):
    hi = x.astype(BF)
    return hi, (x - hi.astype(F32)).astype(BF)


def dot3(a, b, dims=NN):
    return dot(a[0], b[0], dims) + (dot(a[0], b[1], dims) + dot(a[1], b[0], dims))


def natural(position, parity, half):
    return jnp.where(position < half, 2 * position + parity, 2 * (position - half) + 1 - parity)


def inverse_factor(parity, a, w_ref, s_ref, t_ref):
    n = a.shape[0]
    half = n // 2
    row_at = lax.broadcasted_iota(jnp.int32, (n, n), 0)
    col_at = lax.broadcasted_iota(jnp.int32, (n, n), 1)
    row_nat = natural(row_at, parity, half)
    col_nat = natural(col_at, parity, half)
    on = row_at == col_at
    a = jnp.where(row_nat >= col_nat, a, a.T)
    phi = jnp.where(on, 0.5, jnp.where(row_nat > col_nat, 1.0, 0.0))
    unit = jnp.where(on, 1.0, 0.0)
    diagonal = jnp.where(on, a, 0.0)
    scale_row = lax.rsqrt(jnp.sum(diagonal, axis=0, keepdims=True))
    scale_col = lax.rsqrt(jnp.sum(diagonal, axis=1, keepdims=True))
    scaled = a * scale_row * scale_col
    s_ref[...] = scaled
    w_ref[...] = unit - phi * (scaled - unit)
    s_parts = split(scaled)

    w = w_ref[...]
    w_hi = w.astype(BF)
    e = dot(dot(w_hi, s_parts[0]).astype(BF), w_hi, NT) - unit
    w_ref[...] = w - dot((phi * e).astype(BF), w_hi)

    def step(state):
        count, _ = state
        w = w_ref[...]
        w_parts = split(w)
        m_parts = split(dot3(w_parts, s_parts))
        e = dot3(m_parts, w_parts, NT) - unit
        w_ref[...] = w - dot3(split(phi * e), w_parts)
        return count + 1, jnp.sum(e * e)

    def more(state):
        count, size = state
        return jnp.logical_and(count < 16, jnp.logical_not(size < 1e-6))

    _, size = lax.while_loop(more, step, (jnp.int32(0), jnp.float32(1.0)))

    @pl.when(jnp.logical_not(size < 1e-6))
    def _():
        lane = lax.broadcasted_iota(jnp.int32, (1, n), 1)
        lane_nat = natural(lane, parity, half)

        def place(j):
            return jnp.where((j & 1) == parity, j >> 1, half + (j >> 1))

        def column(j, carry):
            p = place(j)
            row = jnp.where(lane_nat >= j, s_ref[pl.ds(p, 1), :], 0.0)
            pivot = jnp.sum(jnp.where(lane == p, row, 0.0))
            row = row * lax.rsqrt(jnp.full((1, n), pivot))
            t_ref[pl.ds(p, 1), :] = row
            col = jnp.sum(jnp.where(on, row, 0.0), axis=1, keepdims=True)
            s_ref[...] = s_ref[...] - col * row
            return carry

        lax.fori_loop(0, n, column, 0)
        w_ref[...] = jnp.zeros_like(w_ref)

        def solve(j, carry):
            p = place(j)
            col = jnp.sum(jnp.where(col_at == p, t_ref[...], 0.0), axis=1, keepdims=True)
            known = jnp.sum(col * w_ref[...], axis=0, keepdims=True)
            pivot = jnp.sum(jnp.where(lane == p, t_ref[pl.ds(p, 1), :], 0.0))
            w_ref[pl.ds(p, 1), :] = (jnp.where(lane == p, 1.0, 0.0) - known) / pivot
            return carry

        lax.fori_loop(0, n, solve, 0)

    return w_ref[...] * scale_row


def factor_kernel(parity_ref, rows_ref, front_hbm, parent_hbm, *refs):
    own_hbm, recv_hbm = refs[:CHUNKS], refs[CHUNKS : 2 * CHUNKS - 1]
    schur_ref, panel_ref, w_ref, s_ref, t_ref, lead_ref, cols_ref, parent_ref = refs[2 * CHUNKS - 1 : 2 * CHUNKS + 7]
    own_ref, recv_ref, sems = refs[2 * CHUNKS + 7 :]
    owned = rows_ref.shape[0]
    half = owned // 2
    strips = parent_ref.shape[0] // owned
    high = lax.Precision.HIGHEST
    copies = [
        pltpu.make_async_copy(front_hbm.at[pl.ds(0, 2)], lead_ref, sems.at[0]),
        pltpu.make_async_copy(front_hbm.at[:, pl.ds(0, half), :], cols_ref, sems.at[1]),
        pltpu.make_async_copy(parent_hbm, parent_ref, sems.at[2]),
    ]
    for c in range(CHUNKS):
        copies.append(pltpu.make_async_copy(own_hbm[c], own_ref.at[c], sems.at[3 + c]))
    for c in range(CHUNKS - 1):
        copies.append(pltpu.make_async_copy(recv_hbm[c], recv_ref.at[c], sems.at[3 + CHUNKS + c]))
    for copy in copies:
        copy.start()
    copies[0].wait()
    top = jnp.concatenate([lead_ref[0, :half], lead_ref[1, :half]], axis=0).astype(F32)
    fold = lead_ref[:, half : half + half // 2].astype(F32)
    corner = jnp.concatenate([fold[b, :, i : i + owned] for b in range(2) for i in (0, owned)], axis=0)
    low = lead_ref[:, half + half // 2 : half + half // 2 + 1].astype(F32)
    bottom = jnp.concatenate([top[:, owned:].T, corner], axis=1)
    pivot = jnp.concatenate([top, bottom], axis=0) + eye(PW) * (low[0] + low[1])
    lead_cols = split(pivot[: PW // 2])
    w = inverse_factor(parity_ref[0], pivot, w_ref, s_ref, t_ref)
    w_ref[...] = w
    factor = dot(rows_ref[...], w, NT, high)
    for b in range(2):
        panel_ref[pl.ds(b, owned, stride=2), :] = factor[:, b * half : (b + 1) * half]
    g_hi, g_lo = split(dot(factor, w_ref[...], NN, high))
    for copy in copies[1:]:
        copy.wait()
    lanes = owned // CHUNKS
    unit = eye(lanes, BF)
    for pair in range(strips // 2):
        cols = cols_ref[pl.ds(2 * pair, 2)].reshape(2 * half, PW)
        if pair == 0:
            update = dot3((g_hi, g_lo), lead_cols, NT)
        else:
            update = dot(g_hi, cols, NT) + dot(g_lo, cols, NT)
        placed = []
        for c in range(CHUNKS):
            z = dot(unit, own_ref[c, pl.ds(2 * pair, 2)].reshape(2 * half, lanes), NT)
            if c < CHUNKS - 1:
                z = z + dot(unit, recv_ref[c, pl.ds(2 * pair, 2)].reshape(2 * half, lanes), NT)
            placed.append(z)
        change = jnp.concatenate(placed, axis=0) - update
        for side in range(2):
            at = pl.ds(2 * pair + side, owned, stride=strips)
            schur_ref[at, :] = parent_ref[at, :] + change[:, side * half : (side + 1) * half]


def last_kernel(schur_ref, recv_ref, out_ref):
    rows = pl.program_id(0)
    lanes = recv_ref.shape[2]
    strips = recv_ref.shape[0]
    part = schur_ref.shape[0] // strips
    r = lax.broadcasted_iota(jnp.int32, (part, lanes), 0) + rows * part
    c = lax.broadcasted_iota(jnp.int32, (part, lanes), 1)
    unit = jnp.where(r == c, 1.0, 0.0).astype(BF)
    for pair in range(strips // 2):
        z = dot(unit, recv_ref[pl.ds(2 * pair, 2)].reshape(-1, lanes), NT)
        for side in range(2):
            at = pl.ds(2 * pair + side, part, stride=strips)
            out_ref[at, :] = schur_ref[at, :] + z[:, side * 128 : (side + 1) * 128]


def swapped(block):
    count = lax.axis_size("cube")
    return lax.ppermute(block, "cube", [(i, i ^ 1) for i in range(count)])


def exchanged(block):
    return lax.all_to_all(block, "grid", 0, 0, tiled=True)


def shards(parent_front, child_block, child_panel, row_map):
    owners = lax.axis_size("grid")
    cube_pos = lax.axis_index("cube")
    grid_pos = lax.axis_index("grid")
    parity = cube_pos % 2
    width = child_block.shape[1]
    owned = parent_front.shape[0]
    half_cols = parent_front.shape[2]
    capacity = 2 * width // owners
    slots = -(-capacity // 16) * 16
    total = owners * slots
    half = owned // 2
    lanes = owned // CHUNKS
    own_panel = child_panel[0]
    panel_all = lax.all_gather(own_panel, "grid")

    row_of = lax.dynamic_index_in_dim(row_map, cube_pos, 0, keepdims=False).reshape(owners, width)
    owner_of = row_of // owned
    local_of = row_of % owned
    earlier = lax.iota(jnp.int32, width)[:, None] < lax.iota(jnp.int32, width)[None, :]
    same = (owner_of[:, :, None] == owner_of[:, None, :]) & earlier[None]
    rank_of = jnp.sum(same.astype(jnp.int32), axis=1)
    slot_of = owner_of * slots + rank_of
    hits = slot_of[:, :, None] == lax.iota(jnp.int32, total)[None, None, :]
    target = jnp.sum(jnp.where(hits, local_of[:, :, None] + 1, 0), axis=1) - 1
    target = target.reshape(owners, owners, slots).transpose(1, 0, 2)
    target_nat = target.reshape(owners, total)
    target_own = jnp.where(
        target_nat >= 0, ((target_nat & 1) ^ parity) * half + (target_nat >> 1), -1
    ).astype(F32)
    slot_parts = slot_of[None] - jnp.array([0, total // 2])[:, None, None]
    slot_parts = jnp.where((slot_parts >= 0) & (slot_parts < total // 2), slot_parts, -1).astype(F32)

    row_flat = row_of.reshape(-1)
    pan_of = jnp.where(row_flat < PW, ((row_flat & 1) ^ parity) * (PW // 2) + (row_flat >> 1), -1)
    block_pan = dot(child_block[0], (pan_of[:, None] == lax.iota(jnp.int32, PW)[None, :]).astype(BF)).astype(BF)

    my_owner = lax.dynamic_index_in_dim(owner_of, grid_pos, 0, keepdims=False)
    my_rank = lax.dynamic_index_in_dim(rank_of, grid_pos, 0, keepdims=False)
    kinds = 4 * capacity
    code = my_owner * kinds + my_rank
    pivot_code = jnp.where(my_owner < 2, (2 + my_owner) * capacity + my_rank, -1)
    never = jnp.full((width,), -1, jnp.int32)
    code = jnp.concatenate([code, code + capacity])
    pivot_code = jnp.concatenate([never, pivot_code])
    at = lax.iota(jnp.int32, owners * kinds)[:, None]
    pack = ((at == code[None, :]) | (at % kinds == pivot_code[None, :])).astype(BF)
    packed = dot(pack, jnp.concatenate([block_pan, own_panel], axis=0)).astype(BF).reshape(owners, kinds, PW)
    packed, slot_parts = lax.optimization_barrier((packed, slot_parts))
    packed = exchanged(packed)
    spread = call(
        functools.partial(source_kernel, owners, slots, owned),
        [jax.ShapeDtypeStruct((owners, width, lanes), BF)] * CHUNKS,
        [pltpu.VMEM((owners, total, width), BF)],
        flops=6 * owners * total * width * width,
    )(child_block[0], slot_parts, target_nat.astype(F32))
    packed, spread = lax.optimization_barrier((packed, spread))

    smem, vmem = pl.BlockSpec(memory_space=pltpu.SMEM), pl.BlockSpec(memory_space=pltpu.VMEM)
    place = jnp.stack([parity, grid_pos]).astype(jnp.int32)
    my_target = lax.dynamic_index_in_dim(target, grid_pos, 0, keepdims=False)[:, :capacity]
    pivot_target = target[:2, :, :capacity]
    pivot_pos = jnp.where(
        pivot_target >= 0,
        ((pivot_target & 1) ^ parity) * (PW // 2)
        + lax.iota(jnp.int32, 2)[:, None, None] * half
        + (pivot_target >> 1),
        -1,
    )
    pivot_pos = pivot_pos.transpose(1, 0, 2).reshape(owners, 2 * capacity)
    none = jnp.full((owners, capacity), -1, jnp.int32)
    kind_targets = jnp.stack(
        [
            jnp.concatenate([my_target, none, none, none], axis=1),
            jnp.concatenate([none, my_target, none, none], axis=1),
            jnp.concatenate([none, none, pivot_pos], axis=1),
        ]
    )
    kind_targets = kind_targets.reshape(3, owners * kinds).astype(F32)
    rows_mine, message, q = call(
        panel_kernel,
        [
            jax.ShapeDtypeStruct((owned, PW), F32),
            jax.ShapeDtypeStruct((owned + LOW_ROWS, PW), BF),
            jax.ShapeDtypeStruct((owned, PW), BF),
        ],
        flops=8 * owned * owners * kinds * PW,
        in_specs=[smem] + [vmem] * 3,
    )(place, packed.reshape(owners * kinds, PW), kind_targets, parent_front[:, 0, : PW // 2])
    theirs = swapped(message)
    bulk = [exchanged(spread[0])]
    rows, message = call(
        rows_kernel,
        [
            jax.ShapeDtypeStruct((owned, PW), F32),
            jax.ShapeDtypeStruct((half + half // 2 + LOW_ROWS, PW), BF),
        ],
        in_specs=[smem, vmem, vmem],
    )(place, rows_mine, theirs)
    front_cols = lax.all_gather(message, "grid")

    phases = 4
    group = owners // phases
    product = call(
        product_kernel,
        [jax.ShapeDtypeStruct((owners, width, lanes), F32)] * CHUNKS,
        flops=4 * owners * width * owned * PW,
        grid=(phases,),
        in_specs=[pl.BlockSpec((group, width, PW), lambda i: (i, 0, 0)), pl.BlockSpec((owned, PW), lambda i: (0, 0))],
        out_specs=[pl.BlockSpec((group, width, lanes), lambda i: (i, 0, 0))] * CHUNKS,
    )(panel_all, q)
    rest, product = lax.optimization_barrier((spread[1:], product))
    bulk = bulk + [exchanged(part) for part in rest]

    own_t, other_t = [], []
    for c in range(CHUNKS):
        a, b = call(
            functools.partial(owner_kernel, owners, slots, owned),
            [jax.ShapeDtypeStruct((owners, half, lanes), BF)] * 2,
            [pltpu.VMEM((owners, total, lanes), BF)],
            flops=8 * owners * total * width * lanes,
            grid=(2 * phases,),
            in_specs=[
                pl.BlockSpec((group, width, lanes), lambda i: (jnp.minimum(i, phases - 1), 0, 0)),
                pl.BlockSpec((group, width, lanes), lambda i: (jnp.minimum(i, phases - 1), 0, 0)),
                pl.BlockSpec((2, owners, width), lambda i: (0, 0, 0)),
                pl.BlockSpec((owners, total), lambda i: (0, 0)),
            ],
            out_specs=[pl.BlockSpec((group, half, lanes), lambda i: (jnp.maximum(i - phases, 0), 0, 0))] * 2,
        )(bulk[c], product[c], slot_parts, target_own)
        own_t.append(a)
        other_t.append(b)
    recv_t = [swapped(x) for x in other_t]

    strips = half_cols // 128
    anywhere = pl.BlockSpec(memory_space=pl.ANY)
    schur, panel = call(
        factor_kernel,
        [
            jax.ShapeDtypeStruct((owned * strips, 128), F32),
            jax.ShapeDtypeStruct((2 * owned, half), F32),
        ],
        [
            pltpu.VMEM((PW, PW), F32),
            pltpu.VMEM((PW, PW), F32),
            pltpu.VMEM((PW, PW), F32),
            pltpu.VMEM((2, half + half // 2 + LOW_ROWS, PW), BF),
            pltpu.VMEM((owners, half, PW), BF),
            pltpu.VMEM((owned * strips, 128), F32),
            pltpu.VMEM((CHUNKS, owners, half, lanes), BF),
            pltpu.VMEM((CHUNKS - 1, owners, half, lanes), BF),
            pltpu.SemaphoreType.DMA((2 + 2 * CHUNKS,)),
        ],
        flops=60 * PW**3,
        in_specs=[smem, vmem] + [anywhere] * (1 + 2 * CHUNKS),
        out_specs=[vmem, vmem],
    )(
        place,
        rows,
        front_cols,
        parent_front.reshape(owned * strips, 128),
        *own_t,
        *recv_t[:-1],
    )
    steps = 2
    last_rows = pl.BlockSpec((lanes * strips // steps, 128), lambda i: ((CHUNKS - 1) * steps + i, 0))
    schur = call(
        last_kernel,
        jax.ShapeDtypeStruct((owned * strips, 128), F32),
        grid=(steps,),
        in_specs=[last_rows, pl.BlockSpec((owners, half, lanes), lambda i: (0, 0, 0))],
        out_specs=last_rows,
        input_output_aliases={0: 0},
    )(schur, recv_t[-1])
    return (schur.reshape(owned, 1, half_cols), panel.reshape(owned, 1, PW // 2))


def solution(mesh):
    in_specs = (P("grid", "cube", None), P("cube", "grid", None), P("cube", "grid", None), P())
    out_specs = (P("grid", "cube", None), P("grid", "cube", None))
    return jax.shard_map(shards, mesh=mesh, in_specs=in_specs, out_specs=out_specs, check_vma=False)
```

```python
import functools

import jax
import jax.numpy as jnp
from jax import lax
from jax.experimental import pallas as pl
from jax.experimental.pallas import tpu as pltpu
from jax.sharding import PartitionSpec as P

PW = 512
CHUNKS = 2
LOW_ROWS = 16
SOURCE_UNROLL = 4
BF = jnp.bfloat16
F32 = jnp.float32
NN = (((1,), (0,)), ((), ()))
NT = (((1,), (1,)), ((), ()))
VMEM_LIMIT = 60 << 20


def dot(a, b, dims=NN, precision=None):
    return lax.dot_general(a, b, dims, precision=precision, preferred_element_type=F32)


def row_numbers(rows, n):
    return lax.broadcasted_iota(jnp.int32, (rows, n), 0).astype(F32).astype(BF)


def hot(numbers, row_vector):
    one, zero = jnp.ones((), BF), jnp.zeros((), BF)
    return jnp.where(numbers == row_vector.astype(BF), one, zero)


def eye(n, dtype=F32):
    r = lax.broadcasted_iota(jnp.int32, (n, n), 0)
    c = lax.broadcasted_iota(jnp.int32, (n, n), 1)
    return jnp.where(r == c, 1.0, 0.0).astype(dtype)


def call(kernel, out_shape, scratch=(), flops=0, **kw):
    moved = sum(x.size * x.dtype.itemsize for x in jax.tree.leaves(out_shape))
    return pl.pallas_call(
        kernel,
        out_shape=out_shape,
        scratch_shapes=list(scratch),
        cost_estimate=pl.CostEstimate(flops=flops, transcendentals=0, bytes_accessed=2 * moved),
        compiler_params=pltpu.CompilerParams(vmem_limit_bytes=VMEM_LIMIT),
        **kw,
    )


def source_kernel(owners, slots, owned, block_ref, slot_ref, target_ref, *refs):
    outs, y_ref = refs[:CHUNKS], refs[CHUNKS]
    width = block_ref.shape[0]
    part = owners * slots // 2
    numbers = row_numbers(part, width)

    def first(pair, carry):
        cols = block_ref[:, pl.ds(pl.multiple_of(pair * 2 * width, 128), 2 * width)]
        for side in range(2):
            s = pair * 2 + side
            mine = cols[:, side * width : (side + 1) * width]
            for b in range(2):
                pick = hot(numbers, slot_ref[b, pl.ds(s, 1), :])
                y = dot(pick, mine, NT).astype(BF).reshape(owners // 2, slots, width)
                y_ref[pl.ds(b * (owners // 2), owners // 2), pl.ds(pl.multiple_of(s * slots, 16), slots), :] = y
        return carry

    lax.fori_loop(0, owners // 2, first, 0, unroll=SOURCE_UNROLL)
    unit = eye(width, BF)
    spots = row_numbers(owned, owners * slots)
    lanes = owned // CHUNKS

    def second(owner, carry):
        turned = dot(hot(spots, target_ref[pl.ds(owner, 1), :]), y_ref[owner]).astype(BF)
        z = dot(unit, turned, NT).astype(BF)
        for c in range(CHUNKS):
            outs[c][owner] = z[:, c * lanes : (c + 1) * lanes]
        return carry

    lax.fori_loop(0, owners, second, 0, unroll=2 * SOURCE_UNROLL)


def panel_kernel(place_ref, received_ref, target_ref, parent_ref, rows_ref, message_ref, q_ref):
    parity, grid_pos = place_ref[0], place_ref[1]
    owned = q_ref.shape[0]

    def chosen(rows, kind):
        at = lax.broadcasted_iota(jnp.int32, (rows, target_ref.shape[1]), 0).astype(F32)
        pick = jnp.where(at == target_ref[kind : kind + 1, :], 1.0, 0.0).astype(BF)
        return dot(pick, received_ref[...])

    placed = chosen(owned, 0)
    q = chosen(owned, 1).astype(BF)
    pan = chosen(PW, 2).astype(BF)
    q_ref[...] = q
    contrib = (placed - dot(q, pan, NT)).astype(BF).astype(F32)
    rows = jnp.concatenate([contrib[:, :owned] + parent_ref[...], contrib[:, owned:]], axis=1)
    rows_ref[...] = rows
    rounded = rows.astype(BF)
    low = jnp.where(diagonal_at(grid_pos, parity, owned), rows - rounded.astype(F32), 0.0)
    message_ref[:owned] = rounded
    message_ref[owned:] = jnp.broadcast_to(jnp.sum(low, axis=0, keepdims=True), (LOW_ROWS, PW)).astype(BF)


def diagonal_at(grid_pos, parity, owned):
    row = lax.broadcasted_iota(jnp.int32, (owned, PW), 0) + grid_pos * owned
    return natural(lax.broadcasted_iota(jnp.int32, (owned, PW), 1), parity, PW // 2) == row


def rows_kernel(place_ref, mine_ref, theirs_ref, rows_ref, message_ref):
    parity, grid_pos = place_ref[0], place_ref[1]
    owned = mine_ref.shape[0]
    half = owned // 2
    theirs = theirs_ref[...].astype(F32)
    theirs = jnp.concatenate([theirs[:, PW // 2 :], theirs[:, : PW // 2]], axis=1)
    on = diagonal_at(grid_pos, parity, owned)
    rows = mine_ref[...] + theirs[:owned] + jnp.where(on, theirs[owned : owned + 1], 0.0)
    rows_ref[...] = rows
    rounded = rows.astype(BF)
    low = jnp.sum(jnp.where(on, rows - rounded.astype(F32), 0.0), axis=0, keepdims=True)
    at = lax.broadcasted_iota(jnp.int32, (owned, owned), 0)
    pick = natural(at, parity, half) == lax.broadcasted_iota(jnp.int32, (owned, owned), 1)
    ordered = dot(jnp.where(pick, 1.0, 0.0).astype(BF), rounded).astype(BF)
    message_ref[:half] = ordered[:half]
    message_ref[half : half + half // 2] = jnp.concatenate(
        [ordered[half : half + half // 2, PW // 2 :], ordered[half + half // 2 :, PW // 2 :]], axis=1
    )
    message_ref[half + half // 2 :] = jnp.broadcast_to(low, (LOW_ROWS, PW)).astype(BF)


def product_kernel(panel_ref, q_ref, *outs):
    lanes = q_ref.shape[0] // CHUNKS
    q = q_ref[...]
    for s in range(panel_ref.shape[0]):
        product = dot(panel_ref[s], q, NT)
        for c in range(CHUNKS):
            outs[c][s] = product[:, c * lanes : (c + 1) * lanes]


def owner_kernel(owners, slots, owned, recv_ref, product_ref, slot_ref, target_ref, own_ref, other_ref, y_ref):
    group, width, lanes = recv_ref.shape
    part = owners * slots // 2
    half = owned // 2
    phases = owners // group
    at = pl.program_id(0)

    @pl.when(at < phases)
    def _():
        numbers = row_numbers(part, width)
        for i in range(group):
            s = at * group + i
            contrib = (recv_ref[i].astype(F32) - product_ref[i]).astype(BF)
            for b in range(2):
                y = dot(hot(numbers, slot_ref[b, pl.ds(s, 1), :]), contrib).astype(BF)
                y_ref[pl.ds(b * (owners // 2), owners // 2), pl.ds(pl.multiple_of(s * slots, 16), slots), :] = y.reshape(
                    owners // 2, slots, lanes
                )

    @pl.when(at >= phases)
    def _():
        spots = row_numbers(owned, owners * slots)
        for i in range(group):
            owner = (at - phases) * group + i
            z = dot(hot(spots, target_ref[pl.ds(owner, 1), :]), y_ref[owner]).astype(BF)
            own_ref[i] = z[:half]
            other_ref[i] = z[half:]


def split(x):
    hi = x.astype(BF)
    return hi, (x - hi.astype(F32)).astype(BF)


def dot3(a, b, dims=NN):
    return dot(a[0], b[0], dims) + (dot(a[0], b[1], dims) + dot(a[1], b[0], dims))


def natural(position, parity, half):
    return jnp.where(position < half, 2 * position + parity, 2 * (position - half) + 1 - parity)


def inverse_factor(parity, a, w_ref, s_ref, t_ref):
    n = a.shape[0]
    half = n // 2
    row_at = lax.broadcasted_iota(jnp.int32, (n, n), 0)
    col_at = lax.broadcasted_iota(jnp.int32, (n, n), 1)
    row_nat = natural(row_at, parity, half)
    col_nat = natural(col_at, parity, half)
    on = row_at == col_at
    a = jnp.where(row_nat >= col_nat, a, a.T)
    phi = jnp.where(on, 0.5, jnp.where(row_nat > col_nat, 1.0, 0.0))
    unit = jnp.where(on, 1.0, 0.0)
    diagonal = jnp.where(on, a, 0.0)
    scale_row = lax.rsqrt(jnp.sum(diagonal, axis=0, keepdims=True))
    scale_col = lax.rsqrt(jnp.sum(diagonal, axis=1, keepdims=True))
    scaled = a * scale_row * scale_col
    s_ref[...] = scaled
    w_ref[...] = unit - phi * (scaled - unit)
    s_parts = split(scaled)

    w = w_ref[...]
    w_hi = w.astype(BF)
    e = dot(dot(w_hi, s_parts[0]).astype(BF), w_hi, NT) - unit
    w_ref[...] = w - dot((phi * e).astype(BF), w_hi)

    def step(state):
        count, _ = state
        w = w_ref[...]
        w_parts = split(w)
        m_parts = split(dot3(w_parts, s_parts))
        e = dot3(m_parts, w_parts, NT) - unit
        w_ref[...] = w - dot((phi * e).astype(BF), w_parts[0])
        return count + 1, jnp.sum(e * e)

    def more(state):
        count, size = state
        return jnp.logical_and(count < 16, jnp.logical_not(size < 1e-6))

    _, size = lax.while_loop(more, step, (jnp.int32(0), jnp.float32(1.0)))

    @pl.when(jnp.logical_not(size < 1e-6))
    def _():
        lane = lax.broadcasted_iota(jnp.int32, (1, n), 1)
        lane_nat = natural(lane, parity, half)

        def place(j):
            return jnp.where((j & 1) == parity, j >> 1, half + (j >> 1))

        def column(j, carry):
            p = place(j)
            row = jnp.where(lane_nat >= j, s_ref[pl.ds(p, 1), :], 0.0)
            pivot = jnp.sum(jnp.where(lane == p, row, 0.0))
            row = row * lax.rsqrt(jnp.full((1, n), pivot))
            t_ref[pl.ds(p, 1), :] = row
            col = jnp.sum(jnp.where(on, row, 0.0), axis=1, keepdims=True)
            s_ref[...] = s_ref[...] - col * row
            return carry

        lax.fori_loop(0, n, column, 0)
        w_ref[...] = jnp.zeros_like(w_ref)

        def solve(j, carry):
            p = place(j)
            col = jnp.sum(jnp.where(col_at == p, t_ref[...], 0.0), axis=1, keepdims=True)
            known = jnp.sum(col * w_ref[...], axis=0, keepdims=True)
            pivot = jnp.sum(jnp.where(lane == p, t_ref[pl.ds(p, 1), :], 0.0))
            w_ref[pl.ds(p, 1), :] = (jnp.where(lane == p, 1.0, 0.0) - known) / pivot
            return carry

        lax.fori_loop(0, n, solve, 0)

    return w_ref[...] * scale_row


def factor_kernel(parity_ref, rows_ref, front_hbm, parent_hbm, *refs):
    own_hbm, recv_hbm = refs[:CHUNKS], refs[CHUNKS : 2 * CHUNKS - 1]
    schur_ref, panel_ref, w_ref, s_ref, t_ref, lead_ref, cols_ref, parent_ref = refs[2 * CHUNKS - 1 : 2 * CHUNKS + 7]
    own_ref, recv_ref, sems = refs[2 * CHUNKS + 7 :]
    owned = rows_ref.shape[0]
    half = owned // 2
    strips = parent_ref.shape[0] // owned
    high = lax.Precision.HIGHEST
    copies = [
        pltpu.make_async_copy(front_hbm.at[pl.ds(0, 2)], lead_ref, sems.at[0]),
        pltpu.make_async_copy(front_hbm.at[:, pl.ds(0, half), :], cols_ref, sems.at[1]),
        pltpu.make_async_copy(parent_hbm, parent_ref, sems.at[2]),
    ]
    for c in range(CHUNKS):
        copies.append(pltpu.make_async_copy(own_hbm[c], own_ref.at[c], sems.at[3 + c]))
    for c in range(CHUNKS - 1):
        copies.append(pltpu.make_async_copy(recv_hbm[c], recv_ref.at[c], sems.at[3 + CHUNKS + c]))
    for copy in copies:
        copy.start()
    copies[0].wait()
    top = jnp.concatenate([lead_ref[0, :half], lead_ref[1, :half]], axis=0).astype(F32)
    fold = lead_ref[:, half : half + half // 2].astype(F32)
    corner = jnp.concatenate([fold[b, :, i : i + owned] for b in range(2) for i in (0, owned)], axis=0)
    low = lead_ref[:, half + half // 2 : half + half // 2 + 1].astype(F32)
    bottom = jnp.concatenate([top[:, owned:].T, corner], axis=1)
    pivot = jnp.concatenate([top, bottom], axis=0) + eye(PW) * (low[0] + low[1])
    lead_cols = split(pivot[: PW // 2])
    w = inverse_factor(parity_ref[0], pivot, w_ref, s_ref, t_ref)
    w_ref[...] = w
    factor = dot(rows_ref[...], w, NT, high)
    for b in range(2):
        panel_ref[pl.ds(b, owned, stride=2), :] = factor[:, b * half : (b + 1) * half]
    g_hi, g_lo = split(dot(factor, w_ref[...], NN, high))
    for copy in copies[1:]:
        copy.wait()
    lanes = owned // CHUNKS
    unit = eye(lanes, BF)
    twice = jnp.concatenate([unit, unit], axis=1)
    both = jnp.concatenate([g_hi, g_lo], axis=0)
    for pair in range(strips // 2):
        if pair == 0:
            update = dot3((g_hi, g_lo), lead_cols, NT)
        else:
            update = dot(both, cols_ref[pl.ds(2 * pair, 2)].reshape(2 * half, PW), NT)
            update = update[:owned] + update[owned:]
        for c in range(CHUNKS):
            own = own_ref[c, pl.ds(2 * pair, 2)].reshape(2 * half, lanes)
            if c < CHUNKS - 1:
                recv = recv_ref[c, pl.ds(2 * pair, 2)].reshape(2 * half, lanes)
                placed = dot(twice, jnp.concatenate([own, recv], axis=1), NT)
            else:
                placed = dot(unit, own, NT)
            change = placed - update[c * lanes : (c + 1) * lanes]
            for side in range(2):
                at = pl.ds(c * lanes * strips + 2 * pair + side, lanes, stride=strips)
                schur_ref[at, :] = parent_ref[at, :] + change[:, side * half : (side + 1) * half]


def last_kernel(schur_ref, recv_ref, out_ref):
    rows = pl.program_id(0)
    lanes = recv_ref.shape[2]
    strips = recv_ref.shape[0]
    part = schur_ref.shape[0] // strips
    r = lax.broadcasted_iota(jnp.int32, (part, lanes), 0) + rows * part
    c = lax.broadcasted_iota(jnp.int32, (part, lanes), 1)
    unit = jnp.where(r == c, 1.0, 0.0).astype(BF)
    for pair in range(strips // 2):
        z = dot(unit, recv_ref[pl.ds(2 * pair, 2)].reshape(-1, lanes), NT)
        for side in range(2):
            at = pl.ds(2 * pair + side, part, stride=strips)
            out_ref[at, :] = schur_ref[at, :] + z[:, side * 128 : (side + 1) * 128]


def swapped(block):
    count = lax.axis_size("cube")
    return lax.ppermute(block, "cube", [(i, i ^ 1) for i in range(count)])


def exchanged(block):
    return lax.all_to_all(block, "grid", 0, 0, tiled=True)


def shards(parent_front, child_block, child_panel, row_map):
    owners = lax.axis_size("grid")
    cube_pos = lax.axis_index("cube")
    grid_pos = lax.axis_index("grid")
    parity = cube_pos % 2
    width = child_block.shape[1]
    owned = parent_front.shape[0]
    half_cols = parent_front.shape[2]
    capacity = 2 * width // owners
    slots = -(-capacity // 16) * 16
    total = owners * slots
    half = owned // 2
    lanes = owned // CHUNKS
    own_panel = child_panel[0]
    panel_all = lax.all_gather(own_panel, "grid")

    row_of = lax.dynamic_index_in_dim(row_map, cube_pos, 0, keepdims=False).reshape(owners, width)
    owner_of = row_of // owned
    local_of = row_of % owned
    earlier = lax.iota(jnp.int32, width)[:, None] < lax.iota(jnp.int32, width)[None, :]
    same = (owner_of[:, :, None] == owner_of[:, None, :]) & earlier[None]
    rank_of = jnp.sum(same.astype(jnp.int32), axis=1)
    slot_of = owner_of * slots + rank_of
    hits = slot_of[:, :, None] == lax.iota(jnp.int32, total)[None, None, :]
    target = jnp.sum(jnp.where(hits, local_of[:, :, None] + 1, 0), axis=1) - 1
    target = target.reshape(owners, owners, slots).transpose(1, 0, 2)
    target_nat = target.reshape(owners, total)
    target_own = jnp.where(
        target_nat >= 0, ((target_nat & 1) ^ parity) * half + (target_nat >> 1), -1
    ).astype(F32)
    slot_parts = slot_of[None] - jnp.array([0, total // 2])[:, None, None]
    slot_parts = jnp.where((slot_parts >= 0) & (slot_parts < total // 2), slot_parts, -1).astype(F32)

    row_flat = row_of.reshape(-1)
    pan_of = jnp.where(row_flat < PW, ((row_flat & 1) ^ parity) * (PW // 2) + (row_flat >> 1), -1)
    block_pan = dot(child_block[0], (pan_of[:, None] == lax.iota(jnp.int32, PW)[None, :]).astype(BF)).astype(BF)

    my_owner = lax.dynamic_index_in_dim(owner_of, grid_pos, 0, keepdims=False)
    my_rank = lax.dynamic_index_in_dim(rank_of, grid_pos, 0, keepdims=False)
    kinds = 4 * capacity
    code = my_owner * kinds + my_rank
    pivot_code = jnp.where(my_owner < 2, (2 + my_owner) * capacity + my_rank, -1)
    never = jnp.full((width,), -1, jnp.int32)
    code = jnp.concatenate([code, code + capacity])
    pivot_code = jnp.concatenate([never, pivot_code])
    at = lax.iota(jnp.int32, owners * kinds)[:, None]
    pack = ((at == code[None, :]) | (at % kinds == pivot_code[None, :])).astype(BF)
    packed = dot(pack, jnp.concatenate([block_pan, own_panel], axis=0)).astype(BF).reshape(owners, kinds, PW)
    packed, slot_parts = lax.optimization_barrier((packed, slot_parts))
    packed = exchanged(packed)
    spread = call(
        functools.partial(source_kernel, owners, slots, owned),
        [jax.ShapeDtypeStruct((owners, width, lanes), BF)] * CHUNKS,
        [pltpu.VMEM((owners, total, width), BF)],
        flops=6 * owners * total * width * width,
    )(child_block[0], slot_parts, target_nat.astype(F32))
    packed, spread = lax.optimization_barrier((packed, spread))

    smem, vmem = pl.BlockSpec(memory_space=pltpu.SMEM), pl.BlockSpec(memory_space=pltpu.VMEM)
    place = jnp.stack([parity, grid_pos]).astype(jnp.int32)
    my_target = lax.dynamic_index_in_dim(target, grid_pos, 0, keepdims=False)[:, :capacity]
    pivot_target = target[:2, :, :capacity]
    pivot_pos = jnp.where(
        pivot_target >= 0,
        ((pivot_target & 1) ^ parity) * (PW // 2)
        + lax.iota(jnp.int32, 2)[:, None, None] * half
        + (pivot_target >> 1),
        -1,
    )
    pivot_pos = pivot_pos.transpose(1, 0, 2).reshape(owners, 2 * capacity)
    none = jnp.full((owners, capacity), -1, jnp.int32)
    kind_targets = jnp.stack(
        [
            jnp.concatenate([my_target, none, none, none], axis=1),
            jnp.concatenate([none, my_target, none, none], axis=1),
            jnp.concatenate([none, none, pivot_pos], axis=1),
        ]
    )
    kind_targets = kind_targets.reshape(3, owners * kinds).astype(F32)
    rows_mine, message, q = call(
        panel_kernel,
        [
            jax.ShapeDtypeStruct((owned, PW), F32),
            jax.ShapeDtypeStruct((owned + LOW_ROWS, PW), BF),
            jax.ShapeDtypeStruct((owned, PW), BF),
        ],
        flops=8 * owned * owners * kinds * PW,
        in_specs=[smem] + [vmem] * 3,
    )(place, packed.reshape(owners * kinds, PW), kind_targets, parent_front[:, 0, : PW // 2])
    theirs = swapped(message)
    bulk = [exchanged(spread[0])]
    rows, message = call(
        rows_kernel,
        [
            jax.ShapeDtypeStruct((owned, PW), F32),
            jax.ShapeDtypeStruct((half + half // 2 + LOW_ROWS, PW), BF),
        ],
        in_specs=[smem, vmem, vmem],
    )(place, rows_mine, theirs)
    front_cols = lax.all_gather(message, "grid")

    phases = 4
    group = owners // phases
    product = call(
        product_kernel,
        [jax.ShapeDtypeStruct((owners, width, lanes), F32)] * CHUNKS,
        flops=4 * owners * width * owned * PW,
        grid=(phases,),
        in_specs=[pl.BlockSpec((group, width, PW), lambda i: (i, 0, 0)), pl.BlockSpec((owned, PW), lambda i: (0, 0))],
        out_specs=[pl.BlockSpec((group, width, lanes), lambda i: (i, 0, 0))] * CHUNKS,
    )(panel_all, q)
    rest, product = lax.optimization_barrier((spread[1:], product))
    bulk = bulk + [exchanged(part) for part in rest]

    own_t, other_t = [], []
    for c in range(CHUNKS):
        a, b = call(
            functools.partial(owner_kernel, owners, slots, owned),
            [jax.ShapeDtypeStruct((owners, half, lanes), BF)] * 2,
            [pltpu.VMEM((owners, total, lanes), BF)],
            flops=8 * owners * total * width * lanes,
            grid=(2 * phases,),
            in_specs=[
                pl.BlockSpec((group, width, lanes), lambda i: (jnp.minimum(i, phases - 1), 0, 0)),
                pl.BlockSpec((group, width, lanes), lambda i: (jnp.minimum(i, phases - 1), 0, 0)),
                pl.BlockSpec((2, owners, width), lambda i: (0, 0, 0)),
                pl.BlockSpec((owners, total), lambda i: (0, 0)),
            ],
            out_specs=[pl.BlockSpec((group, half, lanes), lambda i: (jnp.maximum(i - phases, 0), 0, 0))] * 2,
        )(bulk[c], product[c], slot_parts, target_own)
        own_t.append(a)
        other_t.append(b)
    recv_t = [swapped(x) for x in other_t]

    strips = half_cols // 128
    anywhere = pl.BlockSpec(memory_space=pl.ANY)
    schur, panel = call(
        factor_kernel,
        [
            jax.ShapeDtypeStruct((owned * strips, 128), F32),
            jax.ShapeDtypeStruct((2 * owned, half), F32),
        ],
        [
            pltpu.VMEM((PW, PW), F32),
            pltpu.VMEM((PW, PW), F32),
            pltpu.VMEM((PW, PW), F32),
            pltpu.VMEM((2, half + half // 2 + LOW_ROWS, PW), BF),
            pltpu.VMEM((owners, half, PW), BF),
            pltpu.VMEM((owned * strips, 128), F32),
            pltpu.VMEM((CHUNKS, owners, half, lanes), BF),
            pltpu.VMEM((CHUNKS - 1, owners, half, lanes), BF),
            pltpu.SemaphoreType.DMA((2 + 2 * CHUNKS,)),
        ],
        flops=60 * PW**3,
        in_specs=[smem, vmem] + [anywhere] * (1 + 2 * CHUNKS),
        out_specs=[vmem, vmem],
    )(
        place,
        rows,
        front_cols,
        parent_front.reshape(owned * strips, 128),
        *own_t,
        *recv_t[:-1],
    )
    steps = 2
    last_rows = pl.BlockSpec((lanes * strips // steps, 128), lambda i: ((CHUNKS - 1) * steps + i, 0))
    schur = call(
        last_kernel,
        jax.ShapeDtypeStruct((owned * strips, 128), F32),
        grid=(steps,),
        in_specs=[last_rows, pl.BlockSpec((owners, half, lanes), lambda i: (0, 0, 0))],
        out_specs=last_rows,
        input_output_aliases={0: 0},
    )(schur, recv_t[-1])
    return (schur.reshape(owned, 1, half_cols), panel.reshape(owned, 1, PW // 2))


def solution(mesh):
    in_specs = (P("grid", "cube", None), P("cube", "grid", None), P("cube", "grid", None), P())
    out_specs = (P("grid", "cube", None), P("grid", "cube", None))
    return jax.shard_map(shards, mesh=mesh, in_specs=in_specs, out_specs=out_specs, check_vma=False)
```

```python
import functools

import jax
import jax.numpy as jnp
from jax import lax
from jax.experimental import pallas as pl
from jax.experimental.pallas import tpu as pltpu
from jax.sharding import PartitionSpec as P

PW = 512
CHUNKS = 2
LOW_ROWS = 16
SOURCE_UNROLL = 4
BF = jnp.bfloat16
F32 = jnp.float32
NN = (((1,), (0,)), ((), ()))
NT = (((1,), (1,)), ((), ()))
VMEM_LIMIT = 60 << 20


def dot(a, b, dims=NN, precision=None):
    return lax.dot_general(a, b, dims, precision=precision, preferred_element_type=F32)


def row_numbers(rows, n):
    return lax.broadcasted_iota(jnp.int32, (rows, n), 0).astype(F32).astype(BF)


def hot(numbers, row_vector):
    one, zero = jnp.ones((), BF), jnp.zeros((), BF)
    return jnp.where(numbers == row_vector.astype(BF), one, zero)


def eye(n, dtype=F32):
    r = lax.broadcasted_iota(jnp.int32, (n, n), 0)
    c = lax.broadcasted_iota(jnp.int32, (n, n), 1)
    return jnp.where(r == c, 1.0, 0.0).astype(dtype)


def call(kernel, out_shape, scratch=(), flops=0, **kw):
    moved = sum(x.size * x.dtype.itemsize for x in jax.tree.leaves(out_shape))
    return pl.pallas_call(
        kernel,
        out_shape=out_shape,
        scratch_shapes=list(scratch),
        cost_estimate=pl.CostEstimate(flops=flops, transcendentals=0, bytes_accessed=2 * moved),
        compiler_params=pltpu.CompilerParams(vmem_limit_bytes=VMEM_LIMIT),
        **kw,
    )


def source_kernel(owners, slots, owned, block_ref, slot_ref, target_ref, *refs):
    outs, y_ref = refs[:CHUNKS], refs[CHUNKS]
    width = block_ref.shape[0]
    part = owners * slots // 2
    numbers = row_numbers(part, width)

    def first(pair, carry):
        cols = block_ref[:, pl.ds(pl.multiple_of(pair * 2 * width, 128), 2 * width)]
        for side in range(2):
            s = pair * 2 + side
            mine = cols[:, side * width : (side + 1) * width]
            for b in range(2):
                pick = hot(numbers, slot_ref[b, pl.ds(s, 1), :])
                y = dot(pick, mine, NT).astype(BF).reshape(owners // 2, slots, width)
                y_ref[pl.ds(b * (owners // 2), owners // 2), pl.ds(pl.multiple_of(s * slots, 16), slots), :] = y
        return carry

    lax.fori_loop(0, owners // 2, first, 0, unroll=SOURCE_UNROLL)
    unit = eye(width, BF)
    spots = row_numbers(owned, owners * slots)
    lanes = owned // CHUNKS

    def second(owner, carry):
        turned = dot(hot(spots, target_ref[pl.ds(owner, 1), :]), y_ref[owner]).astype(BF)
        z = dot(unit, turned, NT).astype(BF)
        for c in range(CHUNKS):
            outs[c][owner] = z[:, c * lanes : (c + 1) * lanes]
        return carry

    lax.fori_loop(0, owners, second, 0, unroll=2 * SOURCE_UNROLL)


def panel_kernel(place_ref, received_ref, target_ref, parent_ref, rows_ref, message_ref, q_ref):
    parity, grid_pos = place_ref[0], place_ref[1]
    owned = q_ref.shape[0]

    def chosen(rows, kind):
        at = lax.broadcasted_iota(jnp.int32, (rows, target_ref.shape[1]), 0).astype(F32)
        pick = jnp.where(at == target_ref[kind : kind + 1, :], 1.0, 0.0).astype(BF)
        return dot(pick, received_ref[...])

    placed = chosen(owned, 0)
    q = chosen(owned, 1).astype(BF)
    pan = chosen(PW, 2).astype(BF)
    q_ref[...] = q
    contrib = (placed - dot(q, pan, NT)).astype(BF).astype(F32)
    rows = jnp.concatenate([contrib[:, :owned] + parent_ref[...], contrib[:, owned:]], axis=1)
    rows_ref[...] = rows
    rounded = rows.astype(BF)
    low = jnp.where(diagonal_at(grid_pos, parity, owned), rows - rounded.astype(F32), 0.0)
    message_ref[:owned] = rounded
    message_ref[owned:] = jnp.broadcast_to(jnp.sum(low, axis=0, keepdims=True), (LOW_ROWS, PW)).astype(BF)


def diagonal_at(grid_pos, parity, owned):
    row = lax.broadcasted_iota(jnp.int32, (owned, PW), 0) + grid_pos * owned
    return natural(lax.broadcasted_iota(jnp.int32, (owned, PW), 1), parity, PW // 2) == row


def rows_kernel(place_ref, mine_ref, theirs_ref, rows_ref, message_ref):
    parity, grid_pos = place_ref[0], place_ref[1]
    owned = mine_ref.shape[0]
    half = owned // 2
    theirs = theirs_ref[...].astype(F32)
    theirs = jnp.concatenate([theirs[:, PW // 2 :], theirs[:, : PW // 2]], axis=1)
    on = diagonal_at(grid_pos, parity, owned)
    rows = mine_ref[...] + theirs[:owned] + jnp.where(on, theirs[owned : owned + 1], 0.0)
    rows_ref[...] = rows
    rounded = rows.astype(BF)
    low = jnp.sum(jnp.where(on, rows - rounded.astype(F32), 0.0), axis=0, keepdims=True)
    at = lax.broadcasted_iota(jnp.int32, (owned, owned), 0)
    pick = natural(at, parity, half) == lax.broadcasted_iota(jnp.int32, (owned, owned), 1)
    ordered = dot(jnp.where(pick, 1.0, 0.0).astype(BF), rounded).astype(BF)
    message_ref[:half] = ordered[:half]
    message_ref[half : half + half // 2] = jnp.concatenate(
        [ordered[half : half + half // 2, PW // 2 :], ordered[half + half // 2 :, PW // 2 :]], axis=1
    )
    message_ref[half + half // 2 :] = jnp.broadcast_to(low, (LOW_ROWS, PW)).astype(BF)


def product_kernel(panel_ref, q_ref, *outs):
    lanes = q_ref.shape[0] // CHUNKS
    q = q_ref[...]
    for s in range(panel_ref.shape[0]):
        product = dot(panel_ref[s], q, NT)
        for c in range(CHUNKS):
            outs[c][s] = product[:, c * lanes : (c + 1) * lanes]


def owner_kernel(owners, slots, owned, recv_ref, product_ref, slot_ref, target_ref, own_ref, other_ref, y_ref):
    group, width, lanes = recv_ref.shape
    part = owners * slots // 2
    half = owned // 2
    phases = owners // group
    at = pl.program_id(0)

    @pl.when(at < phases)
    def _():
        numbers = row_numbers(part, width)
        for i in range(group):
            s = at * group + i
            contrib = (recv_ref[i].astype(F32) - product_ref[i]).astype(BF)
            for b in range(2):
                y = dot(hot(numbers, slot_ref[b, pl.ds(s, 1), :]), contrib).astype(BF)
                y_ref[pl.ds(b * (owners // 2), owners // 2), pl.ds(pl.multiple_of(s * slots, 16), slots), :] = y.reshape(
                    owners // 2, slots, lanes
                )

    @pl.when(at >= phases)
    def _():
        spots = row_numbers(owned, owners * slots)
        for i in range(group):
            owner = (at - phases) * group + i
            z = dot(hot(spots, target_ref[pl.ds(owner, 1), :]), y_ref[owner]).astype(BF)
            own_ref[i] = z[:half]
            other_ref[i] = z[half:]


def split(x):
    hi = x.astype(BF)
    return hi, (x - hi.astype(F32)).astype(BF)


def dot3(a, b, dims=NN):
    return dot(a[0], b[0], dims) + (dot(a[0], b[1], dims) + dot(a[1], b[0], dims))


def natural(position, parity, half):
    return jnp.where(position < half, 2 * position + parity, 2 * (position - half) + 1 - parity)


def inverse_factor(parity, a, w_ref, s_ref, t_ref):
    n = a.shape[0]
    half = n // 2
    row_at = lax.broadcasted_iota(jnp.int32, (n, n), 0)
    col_at = lax.broadcasted_iota(jnp.int32, (n, n), 1)
    row_nat = natural(row_at, parity, half)
    col_nat = natural(col_at, parity, half)
    on = row_at == col_at
    a = jnp.where(row_nat >= col_nat, a, a.T)
    phi = jnp.where(on, 0.5, jnp.where(row_nat > col_nat, 1.0, 0.0))
    unit = jnp.where(on, 1.0, 0.0)
    diagonal = jnp.where(on, a, 0.0)
    scale_row = lax.rsqrt(jnp.sum(diagonal, axis=0, keepdims=True))
    scale_col = lax.rsqrt(jnp.sum(diagonal, axis=1, keepdims=True))
    scaled = a * scale_row * scale_col
    s_ref[...] = scaled
    w_ref[...] = unit - phi * (scaled - unit)
    s_parts = split(scaled)

    w = w_ref[...]
    w_hi = w.astype(BF)
    e = dot(dot(w_hi, s_parts[0]).astype(BF), w_hi, NT) - unit
    w_ref[...] = w - dot((phi * e).astype(BF), w_hi)

    def step(state):
        count, _ = state
        w = w_ref[...]
        w_parts = split(w)
        m_parts = split(dot3(w_parts, s_parts))
        e = dot3(m_parts, w_parts, NT) - unit
        w_ref[...] = w - dot((phi * e).astype(BF), w_parts[0])
        return count + 1, jnp.sum(e * e)

    def more(state):
        count, size = state
        return jnp.logical_and(count < 16, jnp.logical_not(size < 1e-6))

    _, size = lax.while_loop(more, step, (jnp.int32(0), jnp.float32(1.0)))

    @pl.when(jnp.logical_not(size < 1e-6))
    def _():
        lane = lax.broadcasted_iota(jnp.int32, (1, n), 1)
        lane_nat = natural(lane, parity, half)

        def place(j):
            return jnp.where((j & 1) == parity, j >> 1, half + (j >> 1))

        def column(j, carry):
            p = place(j)
            row = jnp.where(lane_nat >= j, s_ref[pl.ds(p, 1), :], 0.0)
            pivot = jnp.sum(jnp.where(lane == p, row, 0.0))
            row = row * lax.rsqrt(jnp.full((1, n), pivot))
            t_ref[pl.ds(p, 1), :] = row
            col = jnp.sum(jnp.where(on, row, 0.0), axis=1, keepdims=True)
            s_ref[...] = s_ref[...] - col * row
            return carry

        lax.fori_loop(0, n, column, 0)
        w_ref[...] = jnp.zeros_like(w_ref)

        def solve(j, carry):
            p = place(j)
            col = jnp.sum(jnp.where(col_at == p, t_ref[...], 0.0), axis=1, keepdims=True)
            known = jnp.sum(col * w_ref[...], axis=0, keepdims=True)
            pivot = jnp.sum(jnp.where(lane == p, t_ref[pl.ds(p, 1), :], 0.0))
            w_ref[pl.ds(p, 1), :] = (jnp.where(lane == p, 1.0, 0.0) - known) / pivot
            return carry

        lax.fori_loop(0, n, solve, 0)

    return w_ref[...] * scale_row


def factor_kernel(parity_ref, rows_ref, front_hbm, parent_hbm, *refs):
    own_hbm, recv_hbm = refs[:CHUNKS], refs[CHUNKS : 2 * CHUNKS - 1]
    schur_ref, panel_ref, w_ref, s_ref, t_ref, lead_ref, cols_ref, parent_ref = refs[2 * CHUNKS - 1 : 2 * CHUNKS + 7]
    own_ref, recv_ref, sems = refs[2 * CHUNKS + 7 :]
    owned = rows_ref.shape[0]
    half = owned // 2
    strips = parent_ref.shape[0] // owned
    high = lax.Precision.HIGHEST
    copies = [
        pltpu.make_async_copy(front_hbm.at[pl.ds(0, 2)], lead_ref, sems.at[0]),
        pltpu.make_async_copy(front_hbm.at[:, pl.ds(0, half), :], cols_ref, sems.at[1]),
        pltpu.make_async_copy(parent_hbm, parent_ref, sems.at[2]),
    ]
    for c in range(CHUNKS):
        copies.append(pltpu.make_async_copy(own_hbm[c], own_ref.at[c], sems.at[3 + c]))
    for c in range(CHUNKS - 1):
        copies.append(pltpu.make_async_copy(recv_hbm[c], recv_ref.at[c], sems.at[3 + CHUNKS + c]))
    for copy in copies:
        copy.start()
    copies[0].wait()
    top = jnp.concatenate([lead_ref[0, :half], lead_ref[1, :half]], axis=0).astype(F32)
    fold = lead_ref[:, half : half + half // 2].astype(F32)
    corner = jnp.concatenate([fold[b, :, i : i + owned] for b in range(2) for i in (0, owned)], axis=0)
    low = lead_ref[:, half + half // 2 : half + half // 2 + 1].astype(F32)
    bottom = jnp.concatenate([top[:, owned:].T, corner], axis=1)
    pivot = jnp.concatenate([top, bottom], axis=0) + eye(PW) * (low[0] + low[1])
    lead_cols = split(pivot[: PW // 2])
    w = inverse_factor(parity_ref[0], pivot, w_ref, s_ref, t_ref)
    w_ref[...] = w
    factor = dot(rows_ref[...], w, NT, high)
    for b in range(2):
        panel_ref[pl.ds(b, owned, stride=2), :] = factor[:, b * half : (b + 1) * half]
    g_hi, g_lo = split(dot(factor, w_ref[...], NN, high))
    for copy in copies[1:]:
        copy.wait()
    lanes = owned // CHUNKS
    unit = eye(lanes, BF)
    twice = jnp.concatenate([unit, unit], axis=1)
    both = jnp.concatenate([g_hi, g_lo], axis=0)
    for pair in range(strips // 2):
        if pair == 0:
            update = dot3((g_hi, g_lo), lead_cols, NT)
        else:
            update = dot(both, cols_ref[pl.ds(2 * pair, 2)].reshape(2 * half, PW), NT)
            update = update[:owned] + update[owned:]
        for c in range(CHUNKS):
            own = own_ref[c, pl.ds(2 * pair, 2)].reshape(2 * half, lanes)
            if c < CHUNKS - 1:
                recv = recv_ref[c, pl.ds(2 * pair, 2)].reshape(2 * half, lanes)
                placed = dot(twice, jnp.concatenate([own, recv], axis=1), NT)
            else:
                placed = dot(unit, own, NT)
            change = placed - update[c * lanes : (c + 1) * lanes]
            for side in range(2):
                at = pl.ds(c * lanes * strips + 2 * pair + side, lanes, stride=strips)
                schur_ref[at, :] = parent_ref[at, :] + change[:, side * half : (side + 1) * half]


def last_kernel(schur_ref, recv_ref, out_ref):
    rows = pl.program_id(0)
    lanes = recv_ref.shape[2]
    strips = recv_ref.shape[0]
    part = schur_ref.shape[0] // strips
    r = lax.broadcasted_iota(jnp.int32, (part, lanes), 0) + rows * part
    c = lax.broadcasted_iota(jnp.int32, (part, lanes), 1)
    unit = jnp.where(r == c, 1.0, 0.0).astype(BF)
    for pair in range(strips // 2):
        z = dot(unit, recv_ref[pl.ds(2 * pair, 2)].reshape(-1, lanes), NT)
        for side in range(2):
            at = pl.ds(2 * pair + side, part, stride=strips)
            out_ref[at, :] = schur_ref[at, :] + z[:, side * 128 : (side + 1) * 128]


def swapped(block):
    count = lax.axis_size("cube")
    return lax.ppermute(block, "cube", [(i, i ^ 1) for i in range(count)])


def exchanged(block):
    return lax.all_to_all(block, "grid", 0, 0, tiled=True)


def shards(parent_front, child_block, child_panel, row_map):
    owners = lax.axis_size("grid")
    cube_pos = lax.axis_index("cube")
    grid_pos = lax.axis_index("grid")
    parity = cube_pos % 2
    width = child_block.shape[1]
    owned = parent_front.shape[0]
    half_cols = parent_front.shape[2]
    capacity = 2 * width // owners
    slots = -(-capacity // 16) * 16
    total = owners * slots
    half = owned // 2
    lanes = owned // CHUNKS
    own_panel = child_panel[0]
    panel_all = lax.all_gather(own_panel, "grid")

    row_of = lax.dynamic_index_in_dim(row_map, cube_pos, 0, keepdims=False).reshape(owners, width)
    owner_of = row_of // owned
    local_of = row_of % owned
    earlier = lax.iota(jnp.int32, width)[:, None] < lax.iota(jnp.int32, width)[None, :]
    same = (owner_of[:, :, None] == owner_of[:, None, :]) & earlier[None]
    rank_of = jnp.sum(same.astype(jnp.int32), axis=1)
    slot_of = owner_of * slots + rank_of
    hits = slot_of[:, :, None] == lax.iota(jnp.int32, total)[None, None, :]
    target = jnp.sum(jnp.where(hits, local_of[:, :, None] + 1, 0), axis=1) - 1
    target = target.reshape(owners, owners, slots).transpose(1, 0, 2)
    target_nat = target.reshape(owners, total)
    target_own = jnp.where(
        target_nat >= 0, ((target_nat & 1) ^ parity) * half + (target_nat >> 1), -1
    ).astype(F32)
    slot_parts = slot_of[None] - jnp.array([0, total // 2])[:, None, None]
    slot_parts = jnp.where((slot_parts >= 0) & (slot_parts < total // 2), slot_parts, -1).astype(F32)

    row_flat = row_of.reshape(-1)
    pan_of = jnp.where(row_flat < PW, ((row_flat & 1) ^ parity) * (PW // 2) + (row_flat >> 1), -1)
    block_pan = dot(child_block[0], (pan_of[:, None] == lax.iota(jnp.int32, PW)[None, :]).astype(BF)).astype(BF)

    my_owner = lax.dynamic_index_in_dim(owner_of, grid_pos, 0, keepdims=False)
    my_rank = lax.dynamic_index_in_dim(rank_of, grid_pos, 0, keepdims=False)
    kinds = 4 * capacity
    code = my_owner * kinds + my_rank
    pivot_code = jnp.where(my_owner < 2, (2 + my_owner) * capacity + my_rank, -1)
    never = jnp.full((width,), -1, jnp.int32)
    code = jnp.concatenate([code, code + capacity])
    pivot_code = jnp.concatenate([never, pivot_code])
    at = lax.iota(jnp.int32, owners * kinds)[:, None]
    pack = ((at == code[None, :]) | (at % kinds == pivot_code[None, :])).astype(BF)
    packed = dot(pack, jnp.concatenate([block_pan, own_panel], axis=0)).astype(BF).reshape(owners, kinds, PW)
    packed, slot_parts = lax.optimization_barrier((packed, slot_parts))
    packed = exchanged(packed)
    spread = call(
        functools.partial(source_kernel, owners, slots, owned),
        [jax.ShapeDtypeStruct((owners, width, lanes), BF)] * CHUNKS,
        [pltpu.VMEM((owners, total, width), BF)],
        flops=6 * owners * total * width * width,
    )(child_block[0], slot_parts, target_nat.astype(F32))
    packed, spread = lax.optimization_barrier((packed, spread))

    smem, vmem = pl.BlockSpec(memory_space=pltpu.SMEM), pl.BlockSpec(memory_space=pltpu.VMEM)
    place = jnp.stack([parity, grid_pos]).astype(jnp.int32)
    my_target = lax.dynamic_index_in_dim(target, grid_pos, 0, keepdims=False)[:, :capacity]
    pivot_target = target[:2, :, :capacity]
    pivot_pos = jnp.where(
        pivot_target >= 0,
        ((pivot_target & 1) ^ parity) * (PW // 2)
        + lax.iota(jnp.int32, 2)[:, None, None] * half
        + (pivot_target >> 1),
        -1,
    )
    pivot_pos = pivot_pos.transpose(1, 0, 2).reshape(owners, 2 * capacity)
    none = jnp.full((owners, capacity), -1, jnp.int32)
    kind_targets = jnp.stack(
        [
            jnp.concatenate([my_target, none, none, none], axis=1),
            jnp.concatenate([none, my_target, none, none], axis=1),
            jnp.concatenate([none, none, pivot_pos], axis=1),
        ]
    )
    kind_targets = kind_targets.reshape(3, owners * kinds).astype(F32)
    rows_mine, message, q = call(
        panel_kernel,
        [
            jax.ShapeDtypeStruct((owned, PW), F32),
            jax.ShapeDtypeStruct((owned + LOW_ROWS, PW), BF),
            jax.ShapeDtypeStruct((owned, PW), BF),
        ],
        flops=8 * owned * owners * kinds * PW,
        in_specs=[smem] + [vmem] * 3,
    )(place, packed.reshape(owners * kinds, PW), kind_targets, parent_front[:, 0, : PW // 2])
    message, ready = lax.optimization_barrier((message, spread[0]))
    theirs = swapped(message)
    bulk = [exchanged(ready)]
    rows, message = call(
        rows_kernel,
        [
            jax.ShapeDtypeStruct((owned, PW), F32),
            jax.ShapeDtypeStruct((half + half // 2 + LOW_ROWS, PW), BF),
        ],
        in_specs=[smem, vmem, vmem],
    )(place, rows_mine, theirs)
    front_cols = lax.all_gather(message, "grid")

    phases = 4
    group = owners // phases
    product = call(
        product_kernel,
        [jax.ShapeDtypeStruct((owners, width, lanes), F32)] * CHUNKS,
        flops=4 * owners * width * owned * PW,
        grid=(phases,),
        in_specs=[pl.BlockSpec((group, width, PW), lambda i: (i, 0, 0)), pl.BlockSpec((owned, PW), lambda i: (0, 0))],
        out_specs=[pl.BlockSpec((group, width, lanes), lambda i: (i, 0, 0))] * CHUNKS,
    )(panel_all, q)
    rest, product = lax.optimization_barrier((spread[1:], product))
    bulk = bulk + [exchanged(part) for part in rest]

    own_t, other_t = [], []
    for c in range(CHUNKS):
        a, b = call(
            functools.partial(owner_kernel, owners, slots, owned),
            [jax.ShapeDtypeStruct((owners, half, lanes), BF)] * 2,
            [pltpu.VMEM((owners, total, lanes), BF)],
            flops=250 * owners * total * width * lanes,
            grid=(2 * phases,),
            in_specs=[
                pl.BlockSpec((group, width, lanes), lambda i: (jnp.minimum(i, phases - 1), 0, 0)),
                pl.BlockSpec((group, width, lanes), lambda i: (jnp.minimum(i, phases - 1), 0, 0)),
                pl.BlockSpec((2, owners, width), lambda i: (0, 0, 0)),
                pl.BlockSpec((owners, total), lambda i: (0, 0)),
            ],
            out_specs=[pl.BlockSpec((group, half, lanes), lambda i: (jnp.maximum(i - phases, 0), 0, 0))] * 2,
        )(bulk[c], product[c], slot_parts, target_own)
        own_t.append(a)
        other_t.append(b)
    recv_t = [swapped(x) for x in other_t]

    strips = half_cols // 128
    anywhere = pl.BlockSpec(memory_space=pl.ANY)
    schur, panel = call(
        factor_kernel,
        [
            jax.ShapeDtypeStruct((owned * strips, 128), F32),
            jax.ShapeDtypeStruct((2 * owned, half), F32),
        ],
        [
            pltpu.VMEM((PW, PW), F32),
            pltpu.VMEM((PW, PW), F32),
            pltpu.VMEM((PW, PW), F32),
            pltpu.VMEM((2, half + half // 2 + LOW_ROWS, PW), BF),
            pltpu.VMEM((owners, half, PW), BF),
            pltpu.VMEM((owned * strips, 128), F32),
            pltpu.VMEM((CHUNKS, owners, half, lanes), BF),
            pltpu.VMEM((CHUNKS - 1, owners, half, lanes), BF),
            pltpu.SemaphoreType.DMA((2 + 2 * CHUNKS,)),
        ],
        flops=60 * PW**3,
        in_specs=[smem, vmem] + [anywhere] * (1 + 2 * CHUNKS),
        out_specs=[vmem, vmem],
    )(
        place,
        rows,
        front_cols,
        parent_front.reshape(owned * strips, 128),
        *own_t,
        *recv_t[:-1],
    )
    steps = 1
    last_rows = pl.BlockSpec((lanes * strips // steps, 128), lambda i: ((CHUNKS - 1) * steps + i, 0))
    schur = call(
        last_kernel,
        jax.ShapeDtypeStruct((owned * strips, 128), F32),
        grid=(steps,),
        in_specs=[last_rows, pl.BlockSpec((owners, half, lanes), lambda i: (0, 0, 0))],
        out_specs=last_rows,
        input_output_aliases={0: 0},
    )(schur, recv_t[-1])
    return (schur.reshape(owned, 1, half_cols), panel.reshape(owned, 1, PW // 2))


def solution(mesh):
    in_specs = (P("grid", "cube", None), P("cube", "grid", None), P("cube", "grid", None), P())
    out_specs = (P("grid", "cube", None), P("grid", "cube", None))
    return jax.shard_map(shards, mesh=mesh, in_specs=in_specs, out_specs=out_specs, check_vma=False)
```

```python
import functools

import jax
import jax.numpy as jnp
from jax import lax
from jax.experimental import pallas as pl
from jax.experimental.pallas import tpu as pltpu
from jax.sharding import PartitionSpec as P

PW = 512
CHUNKS = 2
LOW_ROWS = 8
SOURCE_UNROLL = 4
BF = jnp.bfloat16
F32 = jnp.float32
NN = (((1,), (0,)), ((), ()))
NT = (((1,), (1,)), ((), ()))
VMEM_LIMIT = 60 << 20


def dot(a, b, dims=NN, precision=None):
    return lax.dot_general(a, b, dims, precision=precision, preferred_element_type=F32)


def row_numbers(rows, n):
    return lax.broadcasted_iota(jnp.int32, (rows, n), 0).astype(F32).astype(BF)


def hot(numbers, row_vector):
    one, zero = jnp.ones((), BF), jnp.zeros((), BF)
    return jnp.where(numbers == row_vector.astype(BF), one, zero)


def eye(n, dtype=F32):
    r = lax.broadcasted_iota(jnp.int32, (n, n), 0)
    c = lax.broadcasted_iota(jnp.int32, (n, n), 1)
    return jnp.where(r == c, 1.0, 0.0).astype(dtype)


def call(kernel, out_shape, scratch=(), flops=0, **kw):
    moved = sum(x.size * x.dtype.itemsize for x in jax.tree.leaves(out_shape))
    return pl.pallas_call(
        kernel,
        out_shape=out_shape,
        scratch_shapes=list(scratch),
        cost_estimate=pl.CostEstimate(flops=flops, transcendentals=0, bytes_accessed=2 * moved),
        compiler_params=pltpu.CompilerParams(vmem_limit_bytes=VMEM_LIMIT),
        **kw,
    )


def source_kernel(owners, slots, owned, block_ref, slot_ref, target_ref, *refs):
    outs, y_ref = refs[:CHUNKS], refs[CHUNKS]
    width = block_ref.shape[0]
    part = owners * slots // 2
    numbers = row_numbers(part, width)

    def first(pair, carry):
        cols = block_ref[:, pl.ds(pl.multiple_of(pair * 2 * width, 128), 2 * width)]
        for side in range(2):
            s = pair * 2 + side
            mine = cols[:, side * width : (side + 1) * width]
            for b in range(2):
                pick = hot(numbers, slot_ref[b, pl.ds(s, 1), :])
                y = dot(pick, mine, NT).astype(BF).reshape(owners // 2, slots, width)
                y_ref[pl.ds(b * (owners // 2), owners // 2), pl.ds(pl.multiple_of(s * slots, 16), slots), :] = y
        return carry

    lax.fori_loop(0, owners // 2, first, 0, unroll=SOURCE_UNROLL)
    unit = eye(width, BF)
    spots = row_numbers(owned, owners * slots)
    lanes = owned // CHUNKS

    def second(owner, carry):
        turned = dot(hot(spots, target_ref[pl.ds(owner, 1), :]), y_ref[owner]).astype(BF)
        z = dot(unit, turned, NT).astype(BF)
        for c in range(CHUNKS):
            outs[c][owner] = z[:, c * lanes : (c + 1) * lanes]
        return carry

    lax.fori_loop(0, owners, second, 0, unroll=2 * SOURCE_UNROLL)


def panel_kernel(place_ref, received_ref, target_ref, parent_ref, rows_ref, message_ref, q_ref):
    parity, grid_pos = place_ref[0], place_ref[1]
    owned = q_ref.shape[0]

    def chosen(rows, kind):
        at = lax.broadcasted_iota(jnp.int32, (rows, target_ref.shape[1]), 0).astype(F32)
        pick = jnp.where(at == target_ref[kind : kind + 1, :], 1.0, 0.0).astype(BF)
        return dot(pick, received_ref[...])

    placed = chosen(owned, 0)
    q = chosen(owned, 1).astype(BF)
    pan = chosen(PW, 2).astype(BF)
    q_ref[...] = q
    contrib = (placed - dot(q, pan, NT)).astype(BF).astype(F32)
    rows = jnp.concatenate([contrib[:, :owned] + parent_ref[...], contrib[:, owned:]], axis=1)
    rows_ref[...] = rows
    rounded = rows.astype(BF)
    low = jnp.where(diagonal_at(grid_pos, parity, owned), rows - rounded.astype(F32), 0.0)
    message_ref[:owned] = rounded
    message_ref[owned:] = jnp.broadcast_to(jnp.sum(low, axis=0, keepdims=True), (LOW_ROWS, PW)).astype(BF)


def diagonal_at(grid_pos, parity, owned):
    row = lax.broadcasted_iota(jnp.int32, (owned, PW), 0) + grid_pos * owned
    return natural(lax.broadcasted_iota(jnp.int32, (owned, PW), 1), parity, PW // 2) == row


def rows_kernel(place_ref, mine_ref, theirs_ref, rows_ref, message_ref):
    parity, grid_pos = place_ref[0], place_ref[1]
    owned = mine_ref.shape[0]
    half = owned // 2
    theirs = theirs_ref[...].astype(F32)
    theirs = jnp.concatenate([theirs[:, PW // 2 :], theirs[:, : PW // 2]], axis=1)
    on = diagonal_at(grid_pos, parity, owned)
    rows = mine_ref[...] + theirs[:owned] + jnp.where(on, theirs[owned : owned + 1], 0.0)
    rows_ref[...] = rows
    rounded = rows.astype(BF)
    low = jnp.sum(jnp.where(on, rows - rounded.astype(F32), 0.0), axis=0, keepdims=True)
    at = lax.broadcasted_iota(jnp.int32, (owned, owned), 0)
    pick = natural(at, parity, half) == lax.broadcasted_iota(jnp.int32, (owned, owned), 1)
    ordered = dot(jnp.where(pick, 1.0, 0.0).astype(BF), rounded).astype(BF)
    message_ref[:half] = ordered[:half]
    message_ref[half : half + half // 2] = jnp.concatenate(
        [ordered[half : half + half // 2, PW // 2 :], ordered[half + half // 2 :, PW // 2 :]], axis=1
    )
    message_ref[half + half // 2 :] = jnp.broadcast_to(low, (LOW_ROWS, PW)).astype(BF)


def product_kernel(panel_ref, q_ref, *outs):
    lanes = q_ref.shape[0] // CHUNKS
    q = q_ref[...]
    for s in range(panel_ref.shape[0]):
        product = dot(panel_ref[s], q, NT)
        for c in range(CHUNKS):
            outs[c][s] = product[:, c * lanes : (c + 1) * lanes]


def owner_kernel(owners, slots, owned, recv_ref, product_ref, slot_ref, target_ref, own_ref, other_ref, y_ref):
    group, width, lanes = recv_ref.shape
    part = owners * slots // 2
    half = owned // 2
    phases = owners // group
    at = pl.program_id(0)

    @pl.when(at < phases)
    def _():
        numbers = row_numbers(part, width)
        for i in range(group):
            s = at * group + i
            contrib = (recv_ref[i].astype(F32) - product_ref[i]).astype(BF)
            for b in range(2):
                y = dot(hot(numbers, slot_ref[b, pl.ds(s, 1), :]), contrib).astype(BF)
                y_ref[pl.ds(b * (owners // 2), owners // 2), pl.ds(pl.multiple_of(s * slots, 16), slots), :] = y.reshape(
                    owners // 2, slots, lanes
                )

    @pl.when(at >= phases)
    def _():
        spots = row_numbers(owned, owners * slots)
        for i in range(group):
            owner = (at - phases) * group + i
            z = dot(hot(spots, target_ref[pl.ds(owner, 1), :]), y_ref[owner]).astype(BF)
            own_ref[i] = z[:half]
            other_ref[i] = z[half:]


def split(x):
    hi = x.astype(BF)
    return hi, (x - hi.astype(F32)).astype(BF)


def dot3(a, b, dims=NN):
    return dot(a[0], b[0], dims) + (dot(a[0], b[1], dims) + dot(a[1], b[0], dims))


def natural(position, parity, half):
    return jnp.where(position < half, 2 * position + parity, 2 * (position - half) + 1 - parity)


def inverse_factor(parity, a, w_ref, s_ref, t_ref):
    n = a.shape[0]
    half = n // 2
    row_at = lax.broadcasted_iota(jnp.int32, (n, n), 0)
    col_at = lax.broadcasted_iota(jnp.int32, (n, n), 1)
    row_nat = natural(row_at, parity, half)
    col_nat = natural(col_at, parity, half)
    on = row_at == col_at
    a = jnp.where(row_nat >= col_nat, a, a.T)
    phi = jnp.where(on, 0.5, jnp.where(row_nat > col_nat, 1.0, 0.0))
    unit = jnp.where(on, 1.0, 0.0)
    diagonal = jnp.where(on, a, 0.0)
    scale_row = lax.rsqrt(jnp.sum(diagonal, axis=0, keepdims=True))
    scale_col = lax.rsqrt(jnp.sum(diagonal, axis=1, keepdims=True))
    scaled = a * scale_row * scale_col
    s_ref[...] = scaled
    w_ref[...] = unit - phi * (scaled - unit)
    s_parts = split(scaled)

    w = w_ref[...]
    w_hi = w.astype(BF)
    e = dot(dot(w_hi, s_parts[0]).astype(BF), w_hi, NT) - unit
    w_ref[...] = w - dot((phi * e).astype(BF), w_hi)

    def step(state):
        count, _ = state
        w = w_ref[...]
        w_parts = split(w)
        m_parts = split(dot3(w_parts, s_parts))
        e = dot3(m_parts, w_parts, NT) - unit
        w_ref[...] = w - dot((phi * e).astype(BF), w_parts[0])
        return count + 1, jnp.sum(e * e)

    def more(state):
        count, size = state
        return jnp.logical_and(count < 16, jnp.logical_not(size < 1e-6))

    _, size = lax.while_loop(more, step, (jnp.int32(0), jnp.float32(1.0)))

    @pl.when(jnp.logical_not(size < 1e-6))
    def _():
        lane = lax.broadcasted_iota(jnp.int32, (1, n), 1)
        lane_nat = natural(lane, parity, half)

        def place(j):
            return jnp.where((j & 1) == parity, j >> 1, half + (j >> 1))

        def column(j, carry):
            p = place(j)
            row = jnp.where(lane_nat >= j, s_ref[pl.ds(p, 1), :], 0.0)
            pivot = jnp.sum(jnp.where(lane == p, row, 0.0))
            row = row * lax.rsqrt(jnp.full((1, n), pivot))
            t_ref[pl.ds(p, 1), :] = row
            col = jnp.sum(jnp.where(on, row, 0.0), axis=1, keepdims=True)
            s_ref[...] = s_ref[...] - col * row
            return carry

        lax.fori_loop(0, n, column, 0)
        w_ref[...] = jnp.zeros_like(w_ref)

        def solve(j, carry):
            p = place(j)
            col = jnp.sum(jnp.where(col_at == p, t_ref[...], 0.0), axis=1, keepdims=True)
            known = jnp.sum(col * w_ref[...], axis=0, keepdims=True)
            pivot = jnp.sum(jnp.where(lane == p, t_ref[pl.ds(p, 1), :], 0.0))
            w_ref[pl.ds(p, 1), :] = (jnp.where(lane == p, 1.0, 0.0) - known) / pivot
            return carry

        lax.fori_loop(0, n, solve, 0)

    return w_ref[...] * scale_row


def factor_kernel(parity_ref, rows_ref, front_hbm, parent_hbm, *refs):
    own_hbm, recv_hbm = refs[:CHUNKS], refs[CHUNKS : 2 * CHUNKS - 1]
    schur_ref, panel_ref, w_ref, s_ref, t_ref, lead_ref, cols_ref, parent_ref = refs[2 * CHUNKS - 1 : 2 * CHUNKS + 7]
    own_ref, recv_ref, sems = refs[2 * CHUNKS + 7 :]
    owned = rows_ref.shape[0]
    half = owned // 2
    strips = parent_ref.shape[0] // owned
    high = lax.Precision.HIGHEST
    copies = [
        pltpu.make_async_copy(front_hbm.at[pl.ds(0, 2)], lead_ref, sems.at[0]),
        pltpu.make_async_copy(front_hbm.at[:, pl.ds(0, half), :], cols_ref, sems.at[1]),
        pltpu.make_async_copy(parent_hbm, parent_ref, sems.at[2]),
    ]
    for c in range(CHUNKS):
        copies.append(pltpu.make_async_copy(own_hbm[c], own_ref.at[c], sems.at[3 + c]))
    for c in range(CHUNKS - 1):
        copies.append(pltpu.make_async_copy(recv_hbm[c], recv_ref.at[c], sems.at[3 + CHUNKS + c]))
    for copy in copies:
        copy.start()
    copies[0].wait()
    top = jnp.concatenate([lead_ref[0, :half], lead_ref[1, :half]], axis=0).astype(F32)
    fold = lead_ref[:, half : half + half // 2].astype(F32)
    corner = jnp.concatenate([fold[b, :, i : i + owned] for b in range(2) for i in (0, owned)], axis=0)
    low = lead_ref[:, half + half // 2 : half + half // 2 + 1].astype(F32)
    bottom = jnp.concatenate([top[:, owned:].T, corner], axis=1)
    pivot = jnp.concatenate([top, bottom], axis=0) + eye(PW) * (low[0] + low[1])
    lead_cols = split(pivot[: PW // 2])
    w = inverse_factor(parity_ref[0], pivot, w_ref, s_ref, t_ref)
    w_ref[...] = w
    factor = dot(rows_ref[...], w, NT, high)
    for b in range(2):
        panel_ref[pl.ds(b, owned, stride=2), :] = factor[:, b * half : (b + 1) * half]
    g_hi, g_lo = split(dot(factor, w_ref[...], NN, high))
    for copy in copies[1:]:
        copy.wait()
    lanes = owned // CHUNKS
    unit = eye(lanes, BF)
    twice = jnp.concatenate([unit, unit], axis=1)
    both = jnp.concatenate([g_hi, g_lo], axis=0)
    for pair in range(strips // 2):
        if pair == 0:
            update = dot3((g_hi, g_lo), lead_cols, NT)
        else:
            update = dot(both, cols_ref[pl.ds(2 * pair, 2)].reshape(2 * half, PW), NT)
            update = update[:owned] + update[owned:]
        for c in range(CHUNKS):
            own = own_ref[c, pl.ds(2 * pair, 2)].reshape(2 * half, lanes)
            if c < CHUNKS - 1:
                recv = recv_ref[c, pl.ds(2 * pair, 2)].reshape(2 * half, lanes)
                placed = dot(twice, jnp.concatenate([own, recv], axis=1), NT)
            else:
                placed = dot(unit, own, NT)
            change = placed - update[c * lanes : (c + 1) * lanes]
            for side in range(2):
                at = pl.ds(c * lanes * strips + 2 * pair + side, lanes, stride=strips)
                schur_ref[at, :] = parent_ref[at, :] + change[:, side * half : (side + 1) * half]


def last_kernel(schur_ref, recv_ref, out_ref):
    rows = pl.program_id(0)
    lanes = recv_ref.shape[2]
    strips = recv_ref.shape[0]
    part = schur_ref.shape[0] // strips
    r = lax.broadcasted_iota(jnp.int32, (part, lanes), 0) + rows * part
    c = lax.broadcasted_iota(jnp.int32, (part, lanes), 1)
    unit = jnp.where(r == c, 1.0, 0.0).astype(BF)
    for pair in range(strips // 2):
        z = dot(unit, recv_ref[pl.ds(2 * pair, 2)].reshape(-1, lanes), NT)
        for side in range(2):
            at = pl.ds(2 * pair + side, part, stride=strips)
            out_ref[at, :] = schur_ref[at, :] + z[:, side * 128 : (side + 1) * 128]


def swapped(block):
    count = lax.axis_size("cube")
    return lax.ppermute(block, "cube", [(i, i ^ 1) for i in range(count)])


def exchanged(block):
    return lax.all_to_all(block, "grid", 0, 0, tiled=True)


def shards(parent_front, child_block, child_panel, row_map):
    owners = lax.axis_size("grid")
    cube_pos = lax.axis_index("cube")
    grid_pos = lax.axis_index("grid")
    parity = cube_pos % 2
    width = child_block.shape[1]
    owned = parent_front.shape[0]
    half_cols = parent_front.shape[2]
    capacity = 2 * width // owners
    slots = -(-capacity // 16) * 16
    total = owners * slots
    half = owned // 2
    lanes = owned // CHUNKS
    own_panel = child_panel[0]
    panel_all = lax.all_gather(own_panel, "grid")

    row_of = lax.dynamic_index_in_dim(row_map, cube_pos, 0, keepdims=False).reshape(owners, width)
    owner_of = row_of // owned
    local_of = row_of % owned
    earlier = lax.iota(jnp.int32, width)[:, None] < lax.iota(jnp.int32, width)[None, :]
    same = (owner_of[:, :, None] == owner_of[:, None, :]) & earlier[None]
    rank_of = jnp.sum(same.astype(jnp.int32), axis=1)
    slot_of = owner_of * slots + rank_of
    hits = slot_of[:, :, None] == lax.iota(jnp.int32, total)[None, None, :]
    target = jnp.sum(jnp.where(hits, local_of[:, :, None] + 1, 0), axis=1) - 1
    target = target.reshape(owners, owners, slots).transpose(1, 0, 2)
    target_nat = target.reshape(owners, total)
    target_own = jnp.where(
        target_nat >= 0, ((target_nat & 1) ^ parity) * half + (target_nat >> 1), -1
    ).astype(F32)
    slot_parts = slot_of[None] - jnp.array([0, total // 2])[:, None, None]
    slot_parts = jnp.where((slot_parts >= 0) & (slot_parts < total // 2), slot_parts, -1).astype(F32)

    row_flat = row_of.reshape(-1)
    pan_of = jnp.where(row_flat < PW, ((row_flat & 1) ^ parity) * (PW // 2) + (row_flat >> 1), -1)
    block_pan = dot(child_block[0], (pan_of[:, None] == lax.iota(jnp.int32, PW)[None, :]).astype(BF)).astype(BF)

    my_owner = lax.dynamic_index_in_dim(owner_of, grid_pos, 0, keepdims=False)
    my_rank = lax.dynamic_index_in_dim(rank_of, grid_pos, 0, keepdims=False)
    kinds = 4 * capacity
    code = my_owner * kinds + my_rank
    pivot_code = jnp.where(my_owner < 2, (2 + my_owner) * capacity + my_rank, -1)
    never = jnp.full((width,), -1, jnp.int32)
    code = jnp.concatenate([code, code + capacity])
    pivot_code = jnp.concatenate([never, pivot_code])
    at = lax.iota(jnp.int32, owners * kinds)[:, None]
    pack = ((at == code[None, :]) | (at % kinds == pivot_code[None, :])).astype(BF)
    packed = dot(pack, jnp.concatenate([block_pan, own_panel], axis=0)).astype(BF).reshape(owners, kinds, PW)
    packed, slot_parts = lax.optimization_barrier((packed, slot_parts))
    packed = exchanged(packed)
    spread = call(
        functools.partial(source_kernel, owners, slots, owned),
        [jax.ShapeDtypeStruct((owners, width, lanes), BF)] * CHUNKS,
        [pltpu.VMEM((owners, total, width), BF)],
        flops=6 * owners * total * width * width,
    )(child_block[0], slot_parts, target_nat.astype(F32))
    packed, spread = lax.optimization_barrier((packed, spread))

    smem, vmem = pl.BlockSpec(memory_space=pltpu.SMEM), pl.BlockSpec(memory_space=pltpu.VMEM)
    place = jnp.stack([parity, grid_pos]).astype(jnp.int32)
    my_target = lax.dynamic_index_in_dim(target, grid_pos, 0, keepdims=False)[:, :capacity]
    pivot_target = target[:2, :, :capacity]
    pivot_pos = jnp.where(
        pivot_target >= 0,
        ((pivot_target & 1) ^ parity) * (PW // 2)
        + lax.iota(jnp.int32, 2)[:, None, None] * half
        + (pivot_target >> 1),
        -1,
    )
    pivot_pos = pivot_pos.transpose(1, 0, 2).reshape(owners, 2 * capacity)
    none = jnp.full((owners, capacity), -1, jnp.int32)
    kind_targets = jnp.stack(
        [
            jnp.concatenate([my_target, none, none, none], axis=1),
            jnp.concatenate([none, my_target, none, none], axis=1),
            jnp.concatenate([none, none, pivot_pos], axis=1),
        ]
    )
    kind_targets = kind_targets.reshape(3, owners * kinds).astype(F32)
    rows_mine, message, q = call(
        panel_kernel,
        [
            jax.ShapeDtypeStruct((owned, PW), F32),
            jax.ShapeDtypeStruct((owned + LOW_ROWS, PW), BF),
            jax.ShapeDtypeStruct((owned, PW), BF),
        ],
        flops=8 * owned * owners * kinds * PW,
        in_specs=[smem] + [vmem] * 3,
    )(place, packed.reshape(owners * kinds, PW), kind_targets, parent_front[:, 0, : PW // 2])
    theirs = swapped(message)
    bulk = [exchanged(spread[0])]
    rows, message = call(
        rows_kernel,
        [
            jax.ShapeDtypeStruct((owned, PW), F32),
            jax.ShapeDtypeStruct((half + half // 2 + LOW_ROWS, PW), BF),
        ],
        in_specs=[smem, vmem, vmem],
    )(place, rows_mine, theirs)
    front_cols = lax.all_gather(message, "grid")

    phases = 4
    group = owners // phases
    product = call(
        product_kernel,
        [jax.ShapeDtypeStruct((owners, width, lanes), F32)] * CHUNKS,
        flops=4 * owners * width * owned * PW,
        grid=(phases,),
        in_specs=[pl.BlockSpec((group, width, PW), lambda i: (i, 0, 0)), pl.BlockSpec((owned, PW), lambda i: (0, 0))],
        out_specs=[pl.BlockSpec((group, width, lanes), lambda i: (i, 0, 0))] * CHUNKS,
    )(panel_all, q)
    rest, product = lax.optimization_barrier((spread[1:], product))
    bulk = bulk + [exchanged(part) for part in rest]

    own_t, other_t = [], []
    for c in range(CHUNKS):
        a, b = call(
            functools.partial(owner_kernel, owners, slots, owned),
            [jax.ShapeDtypeStruct((owners, half, lanes), BF)] * 2,
            [pltpu.VMEM((owners, total, lanes), BF)],
            flops=8 * owners * total * width * lanes,
            grid=(2 * phases,),
            in_specs=[
                pl.BlockSpec((group, width, lanes), lambda i: (jnp.minimum(i, phases - 1), 0, 0)),
                pl.BlockSpec((group, width, lanes), lambda i: (jnp.minimum(i, phases - 1), 0, 0)),
                pl.BlockSpec((2, owners, width), lambda i: (0, 0, 0)),
                pl.BlockSpec((owners, total), lambda i: (0, 0)),
            ],
            out_specs=[pl.BlockSpec((group, half, lanes), lambda i: (jnp.maximum(i - phases, 0), 0, 0))] * 2,
        )(bulk[c], product[c], slot_parts, target_own)
        own_t.append(a)
        other_t.append(b)
    recv_t = [swapped(x) for x in other_t]

    strips = half_cols // 128
    anywhere = pl.BlockSpec(memory_space=pl.ANY)
    schur, panel = call(
        factor_kernel,
        [
            jax.ShapeDtypeStruct((owned * strips, 128), F32),
            jax.ShapeDtypeStruct((2 * owned, half), F32),
        ],
        [
            pltpu.VMEM((PW, PW), F32),
            pltpu.VMEM((PW, PW), F32),
            pltpu.VMEM((PW, PW), F32),
            pltpu.VMEM((2, half + half // 2 + LOW_ROWS, PW), BF),
            pltpu.VMEM((owners, half, PW), BF),
            pltpu.VMEM((owned * strips, 128), F32),
            pltpu.VMEM((CHUNKS, owners, half, lanes), BF),
            pltpu.VMEM((CHUNKS - 1, owners, half, lanes), BF),
            pltpu.SemaphoreType.DMA((2 + 2 * CHUNKS,)),
        ],
        flops=60 * PW**3,
        in_specs=[smem, vmem] + [anywhere] * (1 + 2 * CHUNKS),
        out_specs=[vmem, vmem],
    )(
        place,
        rows,
        front_cols,
        parent_front.reshape(owned * strips, 128),
        *own_t,
        *recv_t[:-1],
    )
    steps = 2
    last_rows = pl.BlockSpec((lanes * strips // steps, 128), lambda i: ((CHUNKS - 1) * steps + i, 0))
    schur = call(
        last_kernel,
        jax.ShapeDtypeStruct((owned * strips, 128), F32),
        grid=(steps,),
        in_specs=[last_rows, pl.BlockSpec((owners, half, lanes), lambda i: (0, 0, 0))],
        out_specs=last_rows,
        input_output_aliases={0: 0},
    )(schur, recv_t[-1])
    return (schur.reshape(owned, 1, half_cols), panel.reshape(owned, 1, PW // 2))


def solution(mesh):
    in_specs = (P("grid", "cube", None), P("cube", "grid", None), P("cube", "grid", None), P())
    out_specs = (P("grid", "cube", None), P("grid", "cube", None))
    return jax.shard_map(shards, mesh=mesh, in_specs=in_specs, out_specs=out_specs, check_vma=False)
```
